256 devices in a mesh: dp: 16 (over z_lo, x, core), section: 16 (over y, z_hi).
Axes of the slice: x: 4, y: 4, z: 8 (z_hi: 4, z_lo: 2; z = z_hi * 2 + z_lo), core: 2. Of those that a mesh axis runs over, the one named last changes fastest.
Arguments:
- frames: bfloat16 [16, 64, 40, 1024], P('section', 'dp'), may hold values from -240 to 240
- frame_lens: int32 [16, 16, 4], P('section', 'dp'), may hold values from 1 to 40, 128 in all within a row
- tgt_lens: int32 [16, 64], P(None, 'dp'), may hold values from 1 to 8
- enc_gain_in: float32 [1024], replicated, may hold values from 0.25 to 1.75
- w_in: bfloat16 [1024, 2048], P('dp'), may hold values from -0.1875 to 0.1875
- depthwise: bfloat16 [31, 1024], replicated, may hold values from -1 to 1
- enc_gain_mid: float32 [1024], replicated, may hold values from 0.25 to 1.75
- w_out: bfloat16 [1024, 1024], P('dp'), may hold values from -0.1875 to 0.1875
- dec_gain: float32 [16, 1024], P('section'), may hold values from 0.25 to 1.75
- w_query: bfloat16 [16, 1024, 1024], P('section'), may hold values from -1 to 1
- w_key: bfloat16 [16, 1024, 1024], P('section'), may hold values from -1 to 1
- w_value: bfloat16 [16, 1024, 1024], P('section'), may hold values from -0.1875 to 0.1875
- w_output: bfloat16 [16, 1024, 1024], P('section'), may hold values from -0.1875 to 0.1875
- hidden: bfloat16 [16, 16, 64, 8, 1024], P('section', None, 'dp'), may hold values from -6 to 6
Outputs:
- decoded: bfloat16 [16, 16, 64, 8, 1024], P('section', None, 'dp')
The draws below stay inside these ranges and needn't reach their ends.
Inputs may be any that keep to these rules, and one draw needn't show every extreme that they name: `frame_lens`: the 4 utterances at [m, g] have 128 frames together, and the longest of them exactly 40.
All inputs are finite; a program needn't handle non-finite values.
Results may differ from the reference program's by a relative error of at most 0.019.
Values may be sent and summed in bfloat16 or wider, within the bound.
No kernel may reach another device: no remote copies, remote signals or barrier semaphores. Data moves between devices by JAX's collectives and lax.ppermute only.
A program may use at most 128 MiB of HBM per device.

```python
import math
import jax
import jax.numpy as jnp
import numpy as np
from jax import lax

D = 1024
HEADS = 16
HEAD = 64
KERNEL = 31
UTT_DEV = 4
FR = 40
TGT = 8
TOT = 128
SECTIONS = 16
MICRO = 16
SHARDS = 16
UTTS = 64


def clipped_normal(key, shape):
    return jnp.clip(jax.random.normal(key, shape, jnp.float32), -6.0, 6.0)


def query_base(key):
    return clipped_normal(jax.random.fold_in(key, 7002), (SECTIONS, D, D)) * D ** (-0.5)


def draw_frames(key, part):
    values = clipped_normal(jax.random.fold_in(key, 11), (MICRO, UTTS, FR, D))
    return values.astype(jnp.bfloat16)


def draw_hidden(key, part):
    values = clipped_normal(jax.random.fold_in(key, 13), (SECTIONS, MICRO, UTTS, TGT, D))
    return values.astype(jnp.bfloat16)


def draw_w_query(key, part):
    return query_base(key).astype(jnp.bfloat16)


def draw_w_key(key, part):
    values = clipped_normal(jax.random.fold_in(key, 17), (SECTIONS, D, D)) * D ** (-0.5)
    return values.astype(jnp.bfloat16)


def touch_ends(entries, rng, low, top_value):
    longest = entries.shape.index(max(entries.shape))
    spots = []
    for shift in (0, 1):
        where = [jax.random.randint(jax.random.fold_in(rng, axis), (), 0, length) for axis, length in enumerate(entries.shape)]
        where[longest] = (where[longest] + shift) % entries.shape[longest]
        spots.append(tuple(where))
    return entries.at[spots[0]].set(low).at[spots[1]].set(top_value)


def level_of(own_key, shape, cuts, smallest, largest):
    level = 1.0
    for axis_at, blocks in cuts:
        heights = jax.random.uniform(jax.random.fold_in(jax.random.fold_in(own_key, 6), axis_at), (blocks,), jnp.float32, smallest / len(cuts), largest / len(cuts))
        level = level * jnp.repeat(jnp.exp(heights), shape[axis_at] // blocks).reshape((-1,) + (1,) * (len(shape) - 1 - axis_at))
    return level


def length_profile(number_of, total, bound, slope):
    weights = [(1 << 20) // math.isqrt(rank ** slope) + 1 for rank in range(2, number_of + 1)]
    spare, counts = total - bound - (number_of - 1), [1] * (number_of - 1)
    while spare > 0:
        movable = [i for i in range(number_of - 1) if counts[i] < bound]
        mass, left = sum([weights[i] for i in movable]), spare
        for i in movable:
            more = min(bound - counts[i], max(1, left * weights[i] // mass), spare)
            counts[i] = counts[i] + more
            spare = spare - more
    return np.array([bound] + counts)


def uneven_parts(rng, number_of, total, most, slope):
    if number_of == 2:
        one = jax.random.randint(rng, (), max(1, total - most), min(most, total - 1) + 1)
        return jnp.stack([one, total - one])
    sizes = jnp.asarray(length_profile(number_of, total, most, slope), jnp.int32)
    couples = (number_of - 1) // 2
    giver, receiver = sizes[1:1 + 2 * couples:2], sizes[2:2 + 2 * couples:2]
    margin = jnp.minimum(giver - 1, most - receiver)
    shifted = jax.random.randint(jax.random.fold_in(rng, 1), (couples,), 0, 1 << 20) % (margin + 1)
    sizes = sizes.at[1:1 + 2 * couples:2].set(giver - shifted).at[2:2 + 2 * couples:2].set(receiver + shifted)
    return sizes[jax.random.permutation(jax.random.fold_in(rng, 2), number_of)]


def scatter_about(stream_key, extent, scale, most, pieces=(), held_as=jnp.bfloat16):
    level = level_of(stream_key, extent, pieces, -0.22, 0.18) if pieces else 1.0
    array = jax.random.normal(stream_key, extent, jnp.float32) * scale * level
    return jnp.minimum(jnp.maximum(array, -most), most).astype(held_as)


def setup_inputs(seed: int = 0) -> dict:
    arg_keys = jax.random.split(jax.random.key(seed), 15)
    return {
        "frames": draw_frames(jax.random.fold_in(arg_keys[14], 71), 0),
        "frame_lens": jax.vmap(lambda own: uneven_parts(own, UTT_DEV, TOT, FR, 1))(jax.random.split(arg_keys[1], MICRO * SHARDS)).reshape((MICRO, SHARDS, UTT_DEV)).astype(jnp.int32),
        "tgt_lens": touch_ends(jax.random.randint(arg_keys[2], (MICRO, UTTS), 1, TGT + 1), jax.random.fold_in(arg_keys[2], 1), 1, TGT).astype(jnp.int32),
        "enc_gain_in": jnp.clip(1.0 + 0.15 * jax.random.normal(arg_keys[3], (D,), jnp.float32), 0.25, 1.75),
        "w_in": scatter_about(arg_keys[4], (D, 2 * D), D ** -0.5, 0.1875, ((0, 16),)),
        "depthwise": scatter_about(arg_keys[5], (KERNEL, D), KERNEL ** -0.5, 1.0),
        "enc_gain_mid": jnp.clip(1.0 + 0.15 * jax.random.normal(arg_keys[6], (D,), jnp.float32), 0.25, 1.75),
        "w_out": scatter_about(arg_keys[7], (D, D), D ** -0.5, 0.1875, ((0, 16),)),
        "dec_gain": jnp.clip(1.0 + 0.15 * jax.random.normal(arg_keys[8], (SECTIONS, D), jnp.float32), 0.25, 1.75),
        "w_query": draw_w_query(jax.random.fold_in(arg_keys[14], 71), 0),
        "w_key": draw_w_key(jax.random.fold_in(arg_keys[14], 71), 0),
        "w_value": scatter_about(arg_keys[11], (SECTIONS, D, D), D ** -0.5, 0.1875, ((0, 16),)),
        "w_output": scatter_about(arg_keys[12], (SECTIONS, D, D), D ** -0.5, 0.1875, ((0, 16),)),
        "hidden": draw_hidden(jax.random.fold_in(arg_keys[14], 71), 0),
    }


def layer_norm(values, gain):
    average = lax.optimization_barrier(jnp.mean(values, -1, keepdims=True))
    centered = values - average
    spread = lax.optimization_barrier(jnp.mean(centered * centered, -1, keepdims=True))
    return centered * lax.rsqrt(spread + 1e-05) * gain.astype(jnp.float32)

def encode_micro(frames_m, lengths_m, enc_gain_in, w_in, depthwise, enc_gain_mid, w_out):
    utter, count, width = frames_m.shape
    in_range = (jnp.arange(count)[None, :] < lengths_m[:, None]).astype(jnp.float32)[..., None]
    source = frames_m.astype(jnp.float32)
    normed = layer_norm(source, enc_gain_in).astype(jnp.bfloat16)
    lifted = jnp.dot(normed.reshape(-1, width), w_in, preferred_element_type=jnp.float32).reshape(utter, count, 2 * width)
    gated = (in_range * lifted[..., :width] * jax.nn.sigmoid(lifted[..., width:])).astype(jnp.bfloat16)
    half_width = (KERNEL - 1) // 2
    padded = jnp.pad(gated.astype(jnp.float32), ((0, 0), (half_width, half_width), (0, 0)))
    convolved = jnp.zeros((utter, count, width), jnp.float32)
    for offset in range(KERNEL):
        convolved = convolved + padded[:, offset:offset + count, :] * depthwise[offset].astype(jnp.float32)
    activated = jax.nn.silu(layer_norm(convolved, enc_gain_mid)).astype(jnp.bfloat16)
    lowered = jnp.dot(activated.reshape(-1, width), w_out, preferred_element_type=jnp.float32).reshape(utter, count, width)
    return (in_range * (source + lowered)).astype(jnp.bfloat16)

def reference(frames, frame_lens, tgt_lens, enc_gain_in, w_in, depthwise, enc_gain_mid, w_out, dec_gain, w_query, w_key, w_value, w_output, hidden):
    lengths = frame_lens.reshape(MICRO, UTTS)
    memory = lax.map(lambda pair: encode_micro(pair[0], pair[1], enc_gain_in, w_in, depthwise, enc_gain_mid, w_out), (frames, lengths))
    tmask = (jnp.arange(TGT)[None, None, :] < tgt_lens[..., None]).astype(jnp.float32)[..., None]
    frame_mask = (jnp.arange(FR)[None, None, :] < lengths[..., None])[:, :, None, None, :]
    scale = HEAD ** (-0.5)

    def one_section(items):
        hidden_s, gain_s, query_w, key_w, value_w, output_w = items
        source = hidden_s.astype(jnp.float32)
        normed = layer_norm(source, gain_s).astype(jnp.bfloat16)
        query = jnp.dot(normed.reshape(-1, D), query_w, preferred_element_type=jnp.float32).astype(jnp.bfloat16)
        query = query.reshape(MICRO, UTTS, TGT, HEADS, HEAD)
        flat_memory = memory.reshape(-1, D)
        key_rows = jnp.dot(flat_memory, key_w, preferred_element_type=jnp.float32).astype(jnp.bfloat16).reshape(MICRO, UTTS, FR, HEADS, HEAD)
        value_rows = jnp.dot(flat_memory, value_w, preferred_element_type=jnp.float32).astype(jnp.bfloat16).reshape(MICRO, UTTS, FR, HEADS, HEAD)
        scores = jnp.einsum('mutha,mufha->muhtf', query.astype(jnp.float32), key_rows.astype(jnp.float32)) * scale
        scores = jnp.where(frame_mask, scores, -1e+30)
        top = lax.optimization_barrier(jnp.max(scores, -1, keepdims=True))
        expo = jnp.exp(scores - top)
        prob = (expo / lax.optimization_barrier(jnp.sum(expo, -1, keepdims=True))).astype(jnp.bfloat16)
        context = jnp.einsum('muhtf,mufha->mutha', prob.astype(jnp.float32), value_rows.astype(jnp.float32)).astype(jnp.bfloat16)
        projected = jnp.dot(context.reshape(-1, D), output_w, preferred_element_type=jnp.float32).reshape(MICRO, UTTS, TGT, D)
        return (tmask * (source + projected)).astype(jnp.bfloat16)
    return lax.map(one_section, (hidden, dec_gain, w_query, w_key, w_value, w_output))
```

```python
import functools

import jax
import jax.numpy as jnp
from jax import lax
from jax.experimental import pallas as pl
from jax.experimental.pallas import tpu as pltpu
from jax.sharding import PartitionSpec as P

HEADS = 16
D = 1024
HEAD = 64
FR = 40
TGT = 8
UTT = 4
TOT = 128
TAPS = 31
HALF = 15
GROUP = 4
BF = jnp.bfloat16
F32 = jnp.float32
ANY = pl.BlockSpec(memory_space=pl.ANY)
VM = pl.BlockSpec(memory_space=pltpu.VMEM)
SM = pl.BlockSpec(memory_space=pltpu.SMEM)


def norm_rows(values, gain):
    average = jnp.mean(values, -1, keepdims=True)
    centered = values - average
    spread = jnp.mean(centered * centered, -1, keepdims=True)
    return centered * lax.rsqrt(spread + 1e-05) * gain


def params(limit=56):
    return pltpu.CompilerParams(vmem_limit_bytes=limit << 20)


def one_hot(flags):
    return jnp.where(flags, 1.0, 0.0).astype(BF)


def pack_kernel(src_ref, frames_ref, top_ref, low_ref):
    rows = lax.broadcasted_iota(jnp.int32, (TOT, UTT * FR), 0)
    pick = one_hot(src_ref[...] == rows)
    packed = jnp.dot(pick, frames_ref[...], preferred_element_type=F32).astype(BF)
    top_ref[...] = packed[: TOT // 2]
    low_ref[...] = packed[TOT // 2 :]


def pack_frames(src, frames):
    half = jax.ShapeDtypeStruct((TOT // 2, D), BF)
    return pl.pallas_call(
        pack_kernel,
        out_shape=(half, half),
        in_specs=[VM, VM],
        out_specs=(VM, VM),
        compiler_params=params(16),
        cost_estimate=pl.CostEstimate(flops=50_000_000, bytes_accessed=600_000, transcendentals=0),
        name="pack_frames",
    )(src, frames)


def query_kernel(hidden_ref, gain_ref, w_ref, out_ref, normed):
    step = 32

    @pl.loop(0, hidden_ref.shape[0] // step)
    def _(i):
        rows = pl.ds(pl.multiple_of(i * step, step), step)
        normed[rows, :] = norm_rows(hidden_ref[rows, :].astype(F32), gain_ref[...]).astype(BF)

    for j in range(D // 256):
        cols = pl.ds(j * 256, 256)
        q = jnp.dot(normed[...], w_ref[:, cols], preferred_element_type=F32)
        out_ref[:, cols] = (q * (HEAD**-0.5)).astype(BF)


def project_query(hidden, gain, w):
    rows = hidden.shape[0]
    return pl.pallas_call(
        query_kernel,
        out_shape=jax.ShapeDtypeStruct((rows, D), BF),
        in_specs=[VM, VM, VM],
        out_specs=VM,
        scratch_shapes=[pltpu.VMEM((rows, D), BF)],
        compiler_params=params(32),
        cost_estimate=pl.CostEstimate(
            flops=2 * rows * D * D, bytes_accessed=4 << 20, transcendentals=0
        ),
        name="project_query",
    )(hidden, gain, w)


def encode_kernel(shards, n_x, offs_ref, *refs):
    x_refs = refs[:n_x]
    gain_in_ref, dw_ref, gain_mid_ref, src_col_ref, src_row_ref = refs[n_x : n_x + 5]
    w_refs = refs[n_x + 5 : n_x + 5 + shards]
    out_ref, w_full, normed, gated, spread, conv, taps, act, sems = refs[n_x + 5 + shards :]
    depth = w_refs[0].shape[0]
    copies = []
    for i, w in enumerate(w_refs):
        at = pl.multiple_of(offs_ref[i], depth)
        copy = pltpu.make_async_copy(w, w_full.at[pl.ds(at, depth), :], sems.at[i])
        copy.start()
        copies.append(copy)
    part = x_refs[0].shape[0]
    step = 32
    for i, x in enumerate(x_refs):
        for r in range(0, part, step):
            normed[i * part + r : i * part + r + step, :] = norm_rows(
                x[r : r + step, :].astype(F32), gain_in_ref[...]
            ).astype(BF)
    taps[...] = dw_ref[...].astype(F32)
    rows = normed.shape[0]
    frame_rows = conv.shape[0]
    lane = lax.broadcasted_iota(jnp.int32, (frame_rows, rows), 1)
    expand = one_hot(src_col_ref[...] == lane)
    for copy in copies:
        copy.wait()
    for j in range(D // 256):
        cols = pl.ds(j * 256, 256)
        gate_cols = pl.ds(D + j * 256, 256)
        value = jnp.dot(normed[...], w_full[:, cols], preferred_element_type=F32)
        gate = jnp.dot(normed[...], w_full[:, gate_cols], preferred_element_type=F32)
        gated[:, cols] = (value * jax.nn.sigmoid(gate)).astype(BF)
        spread[:, cols] = jnp.dot(expand, gated[:, cols], preferred_element_type=F32)
    lanes = frame_rows // FR
    block = 8

    @pl.loop(0, D // 128)
    def _(c):
        cols = pl.ds(pl.multiple_of(c * 128, 128), 128)
        weights = [jnp.broadcast_to(taps[k : k + 1, cols], (lanes, 128)) for k in range(TAPS)]
        for first in range(0, FR, block):
            sums = [None] * block
            for f in range(max(0, first - HALF), min(FR, first + block + HALF)):
                here = spread[f * lanes : (f + 1) * lanes, cols]
                for b in range(block):
                    k = f - (first + b) + HALF
                    if 0 <= k < TAPS:
                        term = here * weights[k]
                        sums[b] = term if sums[b] is None else sums[b] + term
            for b in range(block):
                at = (first + b) * lanes
                conv[at : at + lanes, cols] = sums[b]

    @pl.loop(0, frame_rows // step)
    def _(i):
        at = pl.ds(pl.multiple_of(i * step, step), step)
        v = norm_rows(conv[at, :], gain_mid_ref[...])
        act[at, :] = (v * jax.nn.sigmoid(v)).astype(BF)

    down = lax.broadcasted_iota(jnp.int32, (rows, frame_rows), 0)
    shrink = one_hot(src_row_ref[...] == down)
    out_ref[...] = jnp.dot(shrink, act[...], preferred_element_type=F32).astype(BF)


def encode(offs, xs, gain_in, dw, gain_mid, src, shards):
    rows = sum(x.shape[0] for x in xs)
    frame_rows = src.shape[0]
    return pl.pallas_call(
        functools.partial(encode_kernel, len(shards), len(xs)),
        out_shape=jax.ShapeDtypeStruct((rows, D), BF),
        in_specs=[SM] + [VM] * (len(xs) + 5) + [ANY] * len(shards),
        out_specs=VM,
        scratch_shapes=[
            pltpu.VMEM((D, 2 * D), BF),
            pltpu.VMEM((rows, D), BF),
            pltpu.VMEM((rows, D), BF),
            pltpu.VMEM((frame_rows, D), F32),
            pltpu.VMEM((frame_rows, D), F32),
            pltpu.VMEM((TAPS, D), F32),
            pltpu.VMEM((frame_rows, D), BF),
            pltpu.SemaphoreType.DMA((len(shards),)),
        ],
        compiler_params=params(32),
        cost_estimate=pl.CostEstimate(
            flops=8_000_000_000, bytes_accessed=6 << 20, transcendentals=0
        ),
        name="encode",
    )(
        offs,
        *xs,
        gain_in,
        dw,
        gain_mid,
        src.reshape(frame_rows, 1),
        src.reshape(1, frame_rows),
        *shards,
    )


def lower_kernel(shards, n_x, offs_ref, act_ref, *refs):
    x_refs = refs[:n_x]
    w_refs = refs[n_x : n_x + shards]
    out_ref, w_full, sems = refs[n_x + shards :]
    depth = w_refs[0].shape[0]
    copies = []
    for i, w in enumerate(w_refs):
        at = pl.multiple_of(offs_ref[i], depth)
        copy = pltpu.make_async_copy(w, w_full.at[pl.ds(at, depth), :], sems.at[i])
        copy.start()
        copies.append(copy)
    for copy in copies:
        copy.wait()
    part = x_refs[0].shape[0]
    for j in range(D // 256):
        cols = pl.ds(j * 256, 256)
        low = jnp.dot(act_ref[...], w_full[:, cols], preferred_element_type=F32)
        for i, x in enumerate(x_refs):
            at = slice(i * part, (i + 1) * part)
            out_ref[at, cols] = (x[:, cols].astype(F32) + low[at]).astype(BF)


def lower(offs, act, xs, shards):
    rows = act.shape[0]
    return pl.pallas_call(
        functools.partial(lower_kernel, len(shards), len(xs)),
        out_shape=jax.ShapeDtypeStruct((rows, D), BF),
        in_specs=[SM, VM] + [VM] * len(xs) + [ANY] * len(shards),
        out_specs=VM,
        scratch_shapes=[pltpu.VMEM((D, D), BF), pltpu.SemaphoreType.DMA((len(shards),))],
        compiler_params=params(24),
        cost_estimate=pl.CostEstimate(
            flops=2 * rows * D * D, bytes_accessed=4 << 20, transcendentals=0
        ),
        name="lower",
    )(offs, act, *xs, *shards)


def decode_kernel(n_mem, aliased, micro_ref, tgt_ref, seg_ref, *refs):
    mem_refs = refs[:n_mem]
    q_hbm, hidden_hbm, wk_hbm, wv_hbm, wo_hbm = refs[n_mem : n_mem + 5]
    rest = refs[n_mem + 5 + (1 if aliased else 0) :]
    out_hbm, wk, wv, wo, keys, values, qs, hs, ctx, res, sems, row_sems, out_sems = rest
    slots = UTT * TGT
    per = mem_refs[0].shape[0]
    micros = n_mem * per // TOT
    loads = [
        pltpu.make_async_copy(a, b, sems.at[i])
        for i, (a, b) in enumerate([(wk_hbm, wk), (wv_hbm, wv), (wo_hbm, wo)])
    ]
    loads[0].start()
    small = []
    for i in range(micros):
        at = pl.ds(pl.multiple_of(micro_ref[i] * slots, slots), slots)
        here = pl.ds(i * slots, slots)
        small.append(pltpu.make_async_copy(q_hbm.at[at, :], qs.at[here, :], row_sems.at[i]))
        small.append(
            pltpu.make_async_copy(hidden_hbm.at[at, :], hs.at[here, :], row_sems.at[micros + i])
        )
    for copy in small:
        copy.start()
    loads[1].start()
    loads[2].start()
    for load, w, out in ((loads[0], wk, keys), (loads[1], wv, values)):
        load.wait()
        for p, mem in enumerate(mem_refs):
            for j in range(D // 256):
                cols = pl.ds(j * 256, 256)
                out[p * per : (p + 1) * per, cols] = jnp.dot(
                    mem[...], w[:, cols], preferred_element_type=F32
                ).astype(BF)
    for copy in small:
        copy.wait()
    width = GROUP * HEAD
    tall = GROUP * slots
    row = lax.broadcasted_iota(jnp.int32, (tall, width), 0)
    lane = lax.broadcasted_iota(jnp.int32, (tall, width), 1)
    own = (row // slots) == (lane // HEAD)
    utt_of_row = (lax.broadcasted_iota(jnp.int32, (tall, TOT), 0) // TGT) % UTT
    for i in range(micros):
        allowed = utt_of_row == seg_ref[i : i + 1, :]
        at = slice(i * TOT, (i + 1) * TOT)
        mine = slice(i * slots, (i + 1) * slots)
        for j in range(HEADS // GROUP):
            cols = slice(j * width, (j + 1) * width)
            q = qs[mine, cols].astype(F32)
            q = jnp.where(own, jnp.concatenate([q] * GROUP, axis=0), 0.0).astype(BF)
            scores = lax.dot_general(
                q, keys[at, cols], (((1,), (1,)), ((), ())), preferred_element_type=F32
            )
            scores = jnp.where(allowed, scores, -1e30)
            expo = jnp.exp(scores - jnp.max(scores, -1, keepdims=True))
            prob = (expo / jnp.sum(expo, -1, keepdims=True)).astype(BF)
            mixed = jnp.dot(prob, values[at, cols], preferred_element_type=F32)
            mixed = jnp.where(own, mixed, 0.0)
            total = mixed[:slots]
            for g in range(1, GROUP):
                total = total + mixed[g * slots : (g + 1) * slots]
            ctx[mine, cols] = total.astype(BF)
    loads[2].wait()
    for j in range(D // 256):
        cols = pl.ds(j * 256, 256)
        proj = jnp.dot(ctx[...], wo[:, cols], preferred_element_type=F32)
        pos = lax.broadcasted_iota(jnp.int32, (slots, 256), 0)
        for i in range(micros):
            mine = slice(i * slots, (i + 1) * slots)
            base = micro_ref[i] * UTT
            limit = jnp.full((slots, 256), tgt_ref[base], jnp.int32)
            for u in range(1, UTT):
                limit = jnp.where(pos // TGT == u, tgt_ref[base + u], limit)
            both = hs[mine, cols].astype(F32) + proj[mine]
            res[mine, cols] = jnp.where(pos % TGT < limit, both, 0.0).astype(BF)
    outs = []
    for i in range(micros):
        at = pl.ds(pl.multiple_of(micro_ref[i] * slots, slots), slots)
        here = pl.ds(i * slots, slots)
        copy = pltpu.make_async_copy(res.at[here, :], out_hbm.at[at, :], out_sems.at[i])
        copy.start()
        outs.append(copy)
    for copy in outs:
        copy.wait()


def decode(micro, tgt, seg, mems, q, hidden, wk, wv, wo, prev):
    rows = hidden.shape[0]
    total = sum(m.shape[0] for m in mems)
    micros = total // TOT
    slots = UTT * TGT
    aliased = prev is not None
    args = [micro, tgt, seg, *mems, q, hidden, wk, wv, wo] + ([prev] if aliased else [])
    return pl.pallas_call(
        functools.partial(decode_kernel, len(mems), aliased),
        out_shape=jax.ShapeDtypeStruct((rows, D), BF),
        in_specs=[SM, SM, VM] + [VM] * len(mems) + [ANY] * (5 + aliased),
        out_specs=ANY,
        scratch_shapes=[
            pltpu.VMEM((D, D), BF),
            pltpu.VMEM((D, D), BF),
            pltpu.VMEM((D, D), BF),
            pltpu.VMEM((total, D), BF),
            pltpu.VMEM((total, D), BF),
            pltpu.VMEM((micros * slots, D), BF),
            pltpu.VMEM((micros * slots, D), BF),
            pltpu.VMEM((micros * slots, D), BF),
            pltpu.VMEM((micros * slots, D), BF),
            pltpu.SemaphoreType.DMA((3,)),
            pltpu.SemaphoreType.DMA((2 * micros,)),
            pltpu.SemaphoreType.DMA((micros,)),
        ],
        input_output_aliases={len(args) - 1: 0} if aliased else {},
        compiler_params=params(32),
        cost_estimate=pl.CostEstimate(
            flops=5 * total * D * D, bytes_accessed=8 << 20, transcendentals=0
        ),
        name="decode",
    )(*args)


def dp_perm(move):
    pairs = []
    for z in range(2):
        for x in range(4):
            for c in range(2):
                nz, nx, nc = move(z, x, c)
                pairs.append(((z * 4 + x) * 2 + c, (nz * 4 + nx % 4) * 2 + nc))
    return pairs


def section_perm(dy, dz):
    return [(y * 4 + z, (y + dy) % 4 * 4 + (z + dz) % 4) for y in range(4) for z in range(4)]


TO_PAIR = dp_perm(lambda z, x, c: (1 - z, x, c))
TO_RIGHT = dp_perm(lambda z, x, c: (z, x + 1, c))
TO_LEFT = dp_perm(lambda z, x, c: (z, x + 3, c))
TO_CORE = dp_perm(lambda z, x, c: (z, x, 1 - c))


def gather_shards(own):
    send = lambda v, perm: lax.ppermute(v, "dp", perm)
    pair = send(own, TO_PAIR)
    own_l, own_r = send(own, TO_RIGHT), send(own, TO_LEFT)
    pair_l, pair_r = send(pair, TO_RIGHT), send(pair, TO_LEFT)
    own_2, pair_2 = send(own_l, TO_RIGHT), send(pair_r, TO_LEFT)
    mine = [own, pair, own_l, own_r, pair_l, pair_r, own_2, pair_2]
    return mine + [send(v, TO_CORE) for v in mine]


def shard_order():
    index = lax.axis_index("dp")
    z, x, c = index // 8, index // 2 % 4, index % 2
    places = [(0, 0), (1, 0), (0, 3), (0, 1), (1, 3), (1, 1), (0, 2), (1, 2)]
    return jnp.stack(
        [
            (((z + a) % 2) * 4 + (x + b) % 4) * 2 + (c + s) % 2
            for s in (0, 1)
            for a, b in places
        ]
    ).astype(jnp.int32)


def exclusive(lengths):
    start = [jnp.zeros_like(lengths[..., 0])]
    for u in range(UTT - 1):
        start.append(start[-1] + lengths[..., u])
    return jnp.stack(start, -1)


def body(
    frames,
    frame_lens,
    tgt_lens,
    enc_gain_in,
    w_in,
    depthwise,
    enc_gain_mid,
    w_out,
    dec_gain,
    w_query,
    w_key,
    w_value,
    w_output,
    hidden,
):
    along = lambda v, dy, dz: lax.ppermute(v, "section", section_perm(dy, dz))
    section = lax.axis_index("section")
    my_y, my_z = section // 4, section % 4
    lengths = frame_lens.reshape(UTT)
    frame = jnp.arange(FR, dtype=jnp.int32)

    start = exclusive(lengths)
    spot = jnp.where(frame[None, :] < lengths[:, None], start[:, None] + frame[None, :], -1)
    top, low = pack_frames(spot.reshape(1, UTT * FR), frames.reshape(UTT * FR, D))

    order = shard_order()
    in_shards = gather_shards(w_in)

    top_b, low_b = along(top, 0, 1), along(low, 0, 1)
    top_a, low_a = along(top, 0, -1), along(low, 0, -1)
    top_2, low_2 = along(top_b, 0, 1), along(low_a, 0, -1)
    out_shards = gather_shards(w_out)

    line = lengths.reshape(1, UTT)
    line = jnp.concatenate([line, along(line, 0, 1), along(line, 0, -1), along(line, 0, 2)])
    line = line[None]
    counts = jnp.concatenate([line, along(line, 1, 0), along(line, -1, 0), along(line, 2, 0)])
    rel = (0, -1, 1, 2)
    micro_of = jnp.stack(
        [jnp.stack([(my_y + dy) % 4 * 4 + (my_z + dz) % 4 for dz in rel]) for dy in rel]
    ).astype(jnp.int32)
    slot = jnp.arange(TOT, dtype=jnp.int32)
    ends = exclusive(counts) + counts
    segment = jnp.sum((slot >= ends[..., :3, None]).astype(jnp.int32), axis=2)

    source = hidden.reshape(-1, D)
    query = project_query(source, dec_gain, w_query[0])

    def encode_pair(first, pieces):
        lens = counts[0, first : first + 2]
        begin = exclusive(lens) + jnp.array([[0], [TOT]], jnp.int32)
        src = jnp.where(frame[:, None, None] < lens, begin + frame[:, None, None], -1)
        act = encode(
            order * (D // 16),
            pieces,
            enc_gain_in.reshape(1, D),
            depthwise,
            enc_gain_mid.reshape(1, D),
            src.reshape(FR * 2 * UTT),
            in_shards,
        )
        return lower(order * (D // 16), act, pieces, out_shards)

    mem_a = encode_pair(0, [top, low, top_b, low_b])
    mem_b = encode_pair(2, [top_a, low_a, top_2, low_2])

    a_from_l, a_from_r = along(mem_a, 1, 0), along(mem_a, -1, 0)
    b_from_l, b_from_r = along(mem_b, 1, 0), along(mem_b, -1, 0)
    a_far, b_far = along(a_from_l, 1, 0), along(b_from_r, -1, 0)

    tgt = tgt_lens.reshape(-1)

    def attend(parts, mems, prev):
        micro = jnp.concatenate([micro_of[y, z : z + 2] for y, z in parts])
        seg = jnp.concatenate([segment[y, z : z + 2] for y, z in parts])
        return decode(
            micro, tgt, seg, mems, query, source, w_key[0], w_value[0], w_output[0], prev
        )

    out = attend([(0, 0), (0, 2)], [mem_a, mem_b], None)
    out = attend([(1, 0), (2, 0)], [a_from_l, a_from_r], out)
    out = attend([(1, 2), (2, 2)], [b_from_l, b_from_r], out)
    out = attend([(3, 0), (3, 2)], [a_far, b_far], out)
    return out.reshape(hidden.shape)


def solution(mesh):
    return jax.shard_map(
        body,
        mesh=mesh,
        in_specs=(
            P("section", "dp", None, None),
            P("section", "dp", None),
            P(None, "dp"),
            P(),
            P("dp", None),
            P(),
            P(),
            P("dp", None),
            P("section", None),
            P("section", None, None),
            P("section", None, None),
            P("section", None, None),
            P("section", None, None),
            P("section", None, "dp", None, None),
        ),
        out_specs=P("section", None, "dp", None, None),
        check_vma=False,
    )
```

```python
import functools

import jax
import jax.numpy as jnp
from jax import lax
from jax.experimental import pallas as pl
from jax.experimental.pallas import tpu as pltpu
from jax.sharding import PartitionSpec as P

HEADS = 16
D = 1024
HEAD = 64
FR = 40
TGT = 8
UTT = 4
TOT = 128
TAPS = 31
HALF = 15
GROUP = 4
EXTRA = 16
BF = jnp.bfloat16
F32 = jnp.float32
HBM = pl.BlockSpec(memory_space=pltpu.HBM)
VM = pl.BlockSpec(memory_space=pltpu.VMEM)
SM = pl.BlockSpec(memory_space=pltpu.SMEM)


def norm_rows(values, gain):
    average = jnp.mean(values, -1, keepdims=True)
    centered = values - average
    spread = jnp.mean(centered * centered, -1, keepdims=True)
    return centered * lax.rsqrt(spread + 1e-05) * gain


def params(limit):
    return pltpu.CompilerParams(vmem_limit_bytes=limit << 20)


def cost(flops, moved):
    return pl.CostEstimate(flops=flops, bytes_accessed=moved, transcendentals=0)


def one_hot(flags):
    return jnp.where(flags, 1.0, 0.0).astype(BF)


def slot_place(slot, lens_ref):
    utt = jnp.zeros_like(slot)
    start = jnp.zeros_like(slot)
    end = jnp.int32(0)
    for u in range(UTT - 1):
        end = end + lens_ref[u]
        later = slot >= end
        utt = jnp.where(later, u + 1, utt)
        start = jnp.where(later, end, start)
    return utt, slot - start


def pack_kernel(lens_ref, frames_ref, out_ref):
    slot = lax.broadcasted_iota(jnp.int32, (TOT, UTT * FR), 0)
    lane = lax.broadcasted_iota(jnp.int32, (TOT, UTT * FR), 1)
    utt, frame = slot_place(slot, lens_ref)
    pick = one_hot(utt * FR + frame == lane)
    for j in range(D // 256):
        cols = slice(j * 256, (j + 1) * 256)
        out_ref[:TOT, cols] = jnp.dot(
            pick, frames_ref[:, cols], preferred_element_type=F32
        ).astype(BF)
    utt, frame = slot_place(lax.broadcasted_iota(jnp.int32, (EXTRA, TOT), 1), lens_ref)
    kind = lax.broadcasted_iota(jnp.int32, (EXTRA, TOT), 0)
    places = jnp.where(kind == 0, frame, utt).astype(F32).astype(BF)
    out_ref[TOT:, :TOT] = places
    out_ref[TOT:, TOT:] = jnp.zeros((EXTRA, D - TOT), BF)


def pack_frames(lens, frames):
    return pl.pallas_call(
        pack_kernel,
        out_shape=jax.ShapeDtypeStruct((TOT + EXTRA, D), BF),
        in_specs=[SM, VM],
        out_specs=VM,
        compiler_params=params(16),
        cost_estimate=cost(50_000_000, 600_000),
        name="pack_frames",
    )(lens, frames)


def query_kernel(hidden_ref, gain_ref, w_ref, out_ref, normed):
    step = 32

    @pl.loop(0, hidden_ref.shape[0] // step)
    def _(i):
        rows = pl.ds(pl.multiple_of(i * step, step), step)
        normed[rows, :] = norm_rows(hidden_ref[rows, :].astype(F32), gain_ref[...]).astype(BF)

    for j in range(D // 256):
        cols = pl.ds(j * 256, 256)
        q = jnp.dot(normed[...], w_ref[:, cols], preferred_element_type=F32)
        out_ref[:, cols] = (q * (HEAD**-0.5)).astype(BF)


def project_query(hidden, gain, w):
    rows = hidden.shape[0]
    return pl.pallas_call(
        query_kernel,
        out_shape=jax.ShapeDtypeStruct((rows, D), BF),
        in_specs=[VM, VM, VM],
        out_specs=VM,
        scratch_shapes=[pltpu.VMEM((rows, D), BF)],
        compiler_params=params(32),
        cost_estimate=cost(2 * rows * D * D, 4 << 20),
        name="project_query",
    )(hidden, gain, w)


def encode_kernel(shards, where_ref, *refs):
    x_refs = refs[:2]
    gain_in_ref, dw_ref, gain_mid_ref = refs[2:5]
    w_refs = refs[5 : 5 + shards]
    out_ref, w_lift, w_low, normed, spread, conv, taps, act, sems = refs[5 + shards :]
    depth = w_refs[0].shape[0]
    lifts, lows = [], []
    for i, w in enumerate(w_refs):
        at = pl.ds(pl.multiple_of(where_ref[i] * depth, depth), depth)
        copy = pltpu.make_async_copy(w.at[:, pl.ds(0, 2 * D)], w_lift.at[at, :], sems.at[0, i])
        copy.start()
        lifts.append(copy)
    for i, w in enumerate(w_refs):
        at = pl.ds(pl.multiple_of(where_ref[i] * depth, depth), depth)
        copy = pltpu.make_async_copy(w.at[:, pl.ds(2 * D, D)], w_low.at[at, :], sems.at[1, i])
        copy.start()
        lows.append(copy)
    step = 32
    for i, x in enumerate(x_refs):
        for r in range(0, TOT, step):
            normed[i * TOT + r : i * TOT + r + step, :] = norm_rows(
                x[r : r + step, :].astype(F32), gain_in_ref[...]
            ).astype(BF)
    taps[...] = dw_ref[...].astype(F32)
    rows = normed.shape[0]
    frame_rows = conv.shape[0]
    lanes = 2 * UTT
    target = []
    for i, x in enumerate(x_refs):
        places = x[TOT : TOT + EXTRA, :TOT].astype(F32)
        target.append(places[0:1] * lanes + places[1:2] + i * UTT)
    target = jnp.concatenate(target, axis=1).astype(jnp.int32)
    spot = lax.broadcasted_iota(jnp.int32, (frame_rows, rows), 0)
    expand = jnp.where(target == spot, 1.0, 0.0)
    shrink = expand.T.astype(BF)
    expand = expand.astype(BF)
    for copy in lifts:
        copy.wait()
    for j in range(D // 256):
        cols = pl.ds(j * 256, 256)
        gate_cols = pl.ds(D + j * 256, 256)
        value = jnp.dot(normed[...], w_lift[:, cols], preferred_element_type=F32)
        gate = jnp.dot(normed[...], w_lift[:, gate_cols], preferred_element_type=F32)
        gated = (value * jax.nn.sigmoid(gate)).astype(BF)
        spread[:, cols] = jnp.dot(expand, gated, preferred_element_type=F32)
    block = 8

    @pl.loop(0, D // 128)
    def _(c):
        cols = pl.ds(pl.multiple_of(c * 128, 128), 128)
        weights = [jnp.broadcast_to(taps[k : k + 1, cols], (lanes, 128)) for k in range(TAPS)]
        for first in range(0, FR, block):
            sums = [None] * block
            for f in range(max(0, first - HALF), min(FR, first + block + HALF)):
                here = spread[f * lanes : (f + 1) * lanes, cols]
                for b in range(block):
                    k = f - (first + b) + HALF
                    if 0 <= k < TAPS:
                        term = here * weights[k]
                        sums[b] = term if sums[b] is None else sums[b] + term
            for b in range(block):
                at = (first + b) * lanes
                conv[at : at + lanes, cols] = sums[b]

    @pl.loop(0, frame_rows // step)
    def _(i):
        at = pl.ds(pl.multiple_of(i * step, step), step)
        v = norm_rows(conv[at, :], gain_mid_ref[...])
        act[at, :] = (v * jax.nn.sigmoid(v)).astype(BF)

    packed = jnp.dot(shrink, act[...], preferred_element_type=F32).astype(BF)
    for copy in lows:
        copy.wait()
    for j in range(D // 256):
        cols = pl.ds(j * 256, 256)
        low = jnp.dot(packed, w_low[:, cols], preferred_element_type=F32)
        for i, x in enumerate(x_refs):
            at = slice(i * TOT, (i + 1) * TOT)
            out_ref[at, cols] = (x[:TOT, cols].astype(F32) + low[at]).astype(BF)
    for i, x in enumerate(x_refs):
        at = slice(rows + i * EXTRA, rows + (i + 1) * EXTRA)
        out_ref[at, :] = x[TOT:, :]


def encode(where, xs, gain_in, dw, gain_mid, shards):
    rows = 2 * TOT
    frame_rows = 2 * UTT * FR
    return pl.pallas_call(
        functools.partial(encode_kernel, len(shards)),
        out_shape=jax.ShapeDtypeStruct((rows + 2 * EXTRA, D), BF),
        in_specs=[SM] + [VM] * 5 + [HBM] * len(shards),
        out_specs=VM,
        scratch_shapes=[
            pltpu.VMEM((D, 2 * D), BF),
            pltpu.VMEM((D, D), BF),
            pltpu.VMEM((rows, D), BF),
            pltpu.VMEM((frame_rows, D), F32),
            pltpu.VMEM((frame_rows, D), F32),
            pltpu.VMEM((TAPS, D), F32),
            pltpu.VMEM((frame_rows, D), BF),
            pltpu.SemaphoreType.DMA((2, len(shards))),
        ],
        compiler_params=params(40),
        cost_estimate=cost(8_000_000_000, 8 << 20),
        name="encode",
    )(where, *xs, gain_in, dw, gain_mid, *shards)


def decode_kernel(n_mem, aliased, micro_ref, tgt_ref, *refs):
    mem_refs = refs[:n_mem]
    q_hbm, hidden_hbm, wk_hbm, wv_hbm, wo_hbm = refs[n_mem : n_mem + 5]
    rest = refs[n_mem + 5 + (1 if aliased else 0) :]
    out_hbm, wk, wv, wo, keys, values, qs, hs, ctx, res, seg, sems, row_sems, out_sems = rest
    slots = UTT * TGT
    micros = 2 * n_mem
    loads = [
        pltpu.make_async_copy(a, b, sems.at[i])
        for i, (a, b) in enumerate([(wk_hbm, wk), (wv_hbm, wv), (wo_hbm, wo)])
    ]
    loads[0].start()
    small = []
    for i in range(micros):
        at = pl.ds(pl.multiple_of(micro_ref[i] * slots, slots), slots)
        here = pl.ds(i * slots, slots)
        small.append(pltpu.make_async_copy(q_hbm.at[at, :], qs.at[here, :], row_sems.at[i]))
        small.append(
            pltpu.make_async_copy(hidden_hbm.at[at, :], hs.at[here, :], row_sems.at[micros + i])
        )
    for copy in small:
        copy.start()
    loads[1].start()
    loads[2].start()
    for p, mem in enumerate(mem_refs):
        for i in range(2):
            first = 2 * TOT + i * EXTRA
            places = mem[first : first + EXTRA, :TOT].astype(F32)
            at = (2 * p + i) * 8
            seg[at : at + 8, :] = jnp.broadcast_to(places[1:2], (8, TOT)).astype(jnp.int32)
    for load, w, out in ((loads[0], wk, keys), (loads[1], wv, values)):
        load.wait()
        for p, mem in enumerate(mem_refs):
            for j in range(D // 256):
                cols = pl.ds(j * 256, 256)
                out[p * 2 * TOT : (p + 1) * 2 * TOT, cols] = jnp.dot(
                    mem[: 2 * TOT, :], w[:, cols], preferred_element_type=F32
                ).astype(BF)
    for copy in small:
        copy.wait()
    width = GROUP * HEAD
    tall = GROUP * slots
    row = lax.broadcasted_iota(jnp.int32, (tall, width), 0)
    lane = lax.broadcasted_iota(jnp.int32, (tall, width), 1)
    own = (row // slots) == (lane // HEAD)
    utt_of_row = (lax.broadcasted_iota(jnp.int32, (tall, TOT), 0) // TGT) % UTT

    @pl.loop(0, micros)
    def _(i):
        line = seg[pl.ds(pl.multiple_of(i * 8, 8), 8), :]
        allowed = utt_of_row == line[0:1]
        at = pl.ds(pl.multiple_of(i * TOT, TOT), TOT)
        mine = pl.ds(pl.multiple_of(i * slots, slots), slots)
        for j in range(HEADS // GROUP):
            cols = slice(j * width, (j + 1) * width)
            q = qs[mine, cols].astype(F32)
            q = jnp.where(own, jnp.concatenate([q] * GROUP, axis=0), 0.0).astype(BF)
            scores = lax.dot_general(
                q, keys[at, cols], (((1,), (1,)), ((), ())), preferred_element_type=F32
            )
            scores = jnp.where(allowed, scores, -1e30)
            expo = jnp.exp(scores - jnp.max(scores, -1, keepdims=True))
            prob = (expo / jnp.sum(expo, -1, keepdims=True)).astype(BF)
            mixed = jnp.dot(prob, values[at, cols], preferred_element_type=F32)
            mixed = jnp.where(own, mixed, 0.0)
            total = mixed[:slots]
            for g in range(1, GROUP):
                total = total + mixed[g * slots : (g + 1) * slots]
            ctx[mine, cols] = total.astype(BF)

    loads[2].wait()
    pos = lax.broadcasted_iota(jnp.int32, (slots, 256), 0)
    for j in range(D // 256):
        cols = pl.ds(j * 256, 256)
        proj = jnp.dot(ctx[...], wo[:, cols], preferred_element_type=F32)
        for i in range(micros):
            mine = slice(i * slots, (i + 1) * slots)
            base = micro_ref[i] * UTT
            limit = jnp.full((slots, 256), tgt_ref[base], jnp.int32)
            for u in range(1, UTT):
                limit = jnp.where(pos // TGT == u, tgt_ref[base + u], limit)
            both = hs[mine, cols].astype(F32) + proj[mine]
            res[mine, cols] = jnp.where(pos % TGT < limit, both, 0.0).astype(BF)
    outs = []
    for i in range(micros):
        at = pl.ds(pl.multiple_of(micro_ref[i] * slots, slots), slots)
        here = pl.ds(i * slots, slots)
        copy = pltpu.make_async_copy(res.at[here, :], out_hbm.at[at, :], out_sems.at[i])
        copy.start()
        outs.append(copy)
    for copy in outs:
        copy.wait()


def decode(micro, tgt, mems, q, hidden, wk, wv, wo, prev):
    rows = hidden.shape[0]
    micros = 2 * len(mems)
    total = micros * TOT
    slots = UTT * TGT
    aliased = prev is not None
    args = [micro, tgt, *mems, q, hidden, wk, wv, wo] + ([prev] if aliased else [])
    return pl.pallas_call(
        functools.partial(decode_kernel, len(mems), aliased),
        out_shape=jax.ShapeDtypeStruct((rows, D), BF),
        in_specs=[SM, SM] + [VM] * len(mems) + [HBM] * (5 + aliased),
        out_specs=HBM,
        scratch_shapes=[
            pltpu.VMEM((D, D), BF),
            pltpu.VMEM((D, D), BF),
            pltpu.VMEM((D, D), BF),
            pltpu.VMEM((total, D), BF),
            pltpu.VMEM((total, D), BF),
            pltpu.VMEM((micros * slots, D), BF),
            pltpu.VMEM((micros * slots, D), BF),
            pltpu.VMEM((micros * slots, D), BF),
            pltpu.VMEM((micros * slots, D), BF),
            pltpu.VMEM((micros * 8, TOT), jnp.int32),
            pltpu.SemaphoreType.DMA((3,)),
            pltpu.SemaphoreType.DMA((2 * micros,)),
            pltpu.SemaphoreType.DMA((micros,)),
        ],
        input_output_aliases={len(args) - 1: 0} if aliased else {},
        compiler_params=params(32),
        cost_estimate=cost(16 * total * D * D, 8 << 20),
        name="decode",
    )(*args)


def dp_perm(move):
    pairs = []
    for z in range(2):
        for x in range(4):
            for c in range(2):
                nz, nx, nc = move(z, x, c)
                pairs.append(((z * 4 + x) * 2 + c, (nz * 4 + nx % 4) * 2 + nc))
    return pairs


def section_perm(dy, dz):
    return [(y * 4 + z, (y + dy) % 4 * 4 + (z + dz) % 4) for y in range(4) for z in range(4)]


TO_PAIR = dp_perm(lambda z, x, c: (1 - z, x, c))
TO_RIGHT = dp_perm(lambda z, x, c: (z, x + 1, c))
TO_LEFT = dp_perm(lambda z, x, c: (z, x + 3, c))
TO_CORE = dp_perm(lambda z, x, c: (z, x, 1 - c))


def after(value, *others):
    return lax.optimization_barrier((value, *others))[0]


def shard_table():
    places = [(0, 0), (1, 0), (0, 3), (0, 1), (1, 3), (1, 1), (0, 2), (1, 2)]
    table = []
    for index in range(16):
        z, x, c = index // 8, index // 2 % 4, index % 2
        table.append(
            [
                ((z + a) % 2 * 4 + (x + b) % 4) * 2 + (c + s) % 2
                for s in (0, 1)
                for a, b in places
            ]
        )
    return table


REL = (0, -1, 1, 2)


def micro_table():
    return [
        [(y + dy) % 4 * 4 + (z + dz) % 4 for dy in REL for dz in REL]
        for y in range(4)
        for z in range(4)
    ]


def body(
    frames,
    frame_lens,
    tgt_lens,
    enc_gain_in,
    w_in,
    depthwise,
    enc_gain_mid,
    w_out,
    dec_gain,
    w_query,
    w_key,
    w_value,
    w_output,
    hidden,
):
    across = lambda v, perm: lax.ppermute(v, "dp", perm)
    along = lambda v, dy, dz: lax.ppermute(v, "section", section_perm(dy, dz))
    where = jnp.array(shard_table(), jnp.int32)[lax.axis_index("dp")]
    micros = jnp.array(micro_table(), jnp.int32)[lax.axis_index("section")].reshape(4, 4)

    own = jnp.concatenate([w_in, w_out], axis=1)
    pair = across(own, TO_PAIR)
    own_l, own_r = across(own, TO_RIGHT), across(own, TO_LEFT)
    packed = pack_frames(frame_lens.reshape(UTT), frames.reshape(UTT * FR, D))
    pair_l, pair_r = across(pair, TO_RIGHT), across(pair, TO_LEFT)
    own_2, pair_2 = across(own_l, TO_RIGHT), across(pair_r, TO_LEFT)
    shards = [own, pair, own_l, own_r, pair_l, pair_r, own_2, pair_2]
    shards = shards + [across(v, TO_CORE) for v in shards]

    ready = after(packed, pair)
    from_b, from_a = along(ready, 0, 1), along(ready, 0, -1)
    from_2 = along(ready, 0, 2)

    source = hidden.reshape(-1, D)
    query = project_query(source, dec_gain, w_query[0])

    def encode_pair(first, second):
        return encode(
            where,
            [first, second],
            enc_gain_in.reshape(1, D),
            depthwise,
            enc_gain_mid.reshape(1, D),
            shards,
        )

    mem_a = encode_pair(packed, from_b)
    mem_b = encode_pair(from_a, from_2)

    a_from_l, a_from_r = along(mem_a, 1, 0), along(mem_a, -1, 0)
    b_from_l, b_from_r = along(mem_b, 1, 0), along(mem_b, -1, 0)

    tgt = tgt_lens.reshape(-1)

    def attend(parts, mems, prev):
        micro = jnp.concatenate([micros[y, z : z + 2] for y, z in parts])
        return decode(micro, tgt, mems, query, source, w_key[0], w_value[0], w_output[0], prev)

    out = attend([(0, 0), (0, 2)], [mem_a, mem_b], None)
    a_far = along(a_from_l, 1, 0)
    b_far = along(after(b_from_r, out), -1, 0)
    out = attend([(1, 0), (2, 0)], [a_from_l, a_from_r], out)
    out = attend([(1, 2), (2, 2)], [b_from_l, b_from_r], out)
    out = attend([(3, 0), (3, 2)], [a_far, b_far], out)
    return out.reshape(hidden.shape)


def solution(mesh):
    return jax.shard_map(
        body,
        mesh=mesh,
        in_specs=(
            P("section", "dp", None, None),
            P("section", "dp", None),
            P(None, "dp"),
            P(),
            P("dp", None),
            P(),
            P(),
            P("dp", None),
            P("section", None),
            P("section", None, None),
            P("section", None, None),
            P("section", None, None),
            P("section", None, None),
            P("section", None, "dp", None, None),
        ),
        out_specs=P("section", None, "dp", None, None),
        check_vma=False,
    )
```

```python
import functools

import jax
import jax.numpy as jnp
from jax import lax
from jax.experimental import pallas as pl
from jax.experimental.pallas import tpu as pltpu
from jax.sharding import PartitionSpec as P

HEADS = 16
D = 1024
HEAD = 64
FR = 40
TGT = 8
UTT = 4
TOT = 128
TAPS = 31
HALF = 15
GROUP = 4
EXTRA = 16
BF = jnp.bfloat16
F32 = jnp.float32
HBM = pl.BlockSpec(memory_space=pltpu.HBM)
VM = pl.BlockSpec(memory_space=pltpu.VMEM)
SM = pl.BlockSpec(memory_space=pltpu.SMEM)


def norm_rows(values, gain):
    average = jnp.mean(values, -1, keepdims=True)
    centered = values - average
    spread = jnp.mean(centered * centered, -1, keepdims=True)
    return centered * lax.rsqrt(spread + 1e-05) * gain


def params(limit):
    return pltpu.CompilerParams(vmem_limit_bytes=limit << 20)


def cost(flops, moved):
    return pl.CostEstimate(flops=flops, bytes_accessed=moved, transcendentals=0)


def one_hot(flags):
    return jnp.where(flags, 1.0, 0.0).astype(BF)


def slot_place(slot, lens_ref):
    utt = jnp.zeros_like(slot)
    start = jnp.zeros_like(slot)
    end = jnp.int32(0)
    for u in range(UTT - 1):
        end = end + lens_ref[u]
        later = slot >= end
        utt = jnp.where(later, u + 1, utt)
        start = jnp.where(later, end, start)
    return utt, slot - start


def prepare_kernel(lens_ref, frames_hbm, w_in_hbm, w_out_hbm, own_ref, out_ref, frames_ref, sems):
    loads = [
        pltpu.make_async_copy(w_in_hbm, own_ref.at[:, pl.ds(0, 2 * D)], sems.at[0]),
        pltpu.make_async_copy(w_out_hbm, own_ref.at[:, pl.ds(2 * D, D)], sems.at[1]),
        pltpu.make_async_copy(frames_hbm, frames_ref, sems.at[2]),
    ]
    for load in loads:
        load.start()
    slot = lax.broadcasted_iota(jnp.int32, (TOT, UTT * FR), 0)
    lane = lax.broadcasted_iota(jnp.int32, (TOT, UTT * FR), 1)
    utt, frame = slot_place(slot, lens_ref)
    pick = one_hot(utt * FR + frame == lane)
    utt, frame = slot_place(lax.broadcasted_iota(jnp.int32, (EXTRA, TOT), 1), lens_ref)
    kind = lax.broadcasted_iota(jnp.int32, (EXTRA, TOT), 0)
    out_ref[TOT:, :TOT] = jnp.where(kind == 0, frame, utt).astype(F32).astype(BF)
    out_ref[TOT:, TOT:] = jnp.zeros((EXTRA, D - TOT), BF)
    loads[2].wait()
    for j in range(D // 256):
        cols = slice(j * 256, (j + 1) * 256)
        out_ref[:TOT, cols] = jnp.dot(
            pick, frames_ref[:, cols], preferred_element_type=F32
        ).astype(BF)
    loads[0].wait()
    loads[1].wait()


def prepare(lens, frames, w_in, w_out):
    depth = w_in.shape[0]
    return pl.pallas_call(
        prepare_kernel,
        out_shape=(
            jax.ShapeDtypeStruct((depth, 3 * D), BF),
            jax.ShapeDtypeStruct((TOT + EXTRA, D), BF),
        ),
        in_specs=[SM, HBM, HBM, HBM],
        out_specs=(VM, VM),
        scratch_shapes=[pltpu.VMEM((UTT * FR, D), BF), pltpu.SemaphoreType.DMA((3,))],
        compiler_params=params(8),
        cost_estimate=cost(50_000_000, 1_400_000),
        name="prepare",
    )(lens, frames, w_in, w_out)


def query_kernel(hidden_ref, gain_ref, w_ref, out_ref, normed):
    for r in range(0, hidden_ref.shape[0], 16):
        rows = slice(r, r + 16)
        normed[rows, :] = norm_rows(hidden_ref[rows, :].astype(F32), gain_ref[...]).astype(BF)
    for j in range(D // 256):
        cols = slice(j * 256, (j + 1) * 256)
        q = jnp.dot(normed[...], w_ref[:, cols], preferred_element_type=F32)
        out_ref[:, cols] = (q * (HEAD**-0.5)).astype(BF)


def project_query(hidden, gain, w):
    rows = hidden.shape[0]
    return pl.pallas_call(
        query_kernel,
        out_shape=jax.ShapeDtypeStruct((rows, D), BF),
        in_specs=[VM, VM, VM],
        out_specs=VM,
        scratch_shapes=[pltpu.VMEM((rows, D), BF)],
        compiler_params=params(8),
        cost_estimate=cost(2 * rows * D * D, 4 << 20),
        name="project_query",
    )(hidden, gain, w)


def order_columns(dst, src, where_ref):
    odd = jnp.broadcast_to(where_ref[0] % 2 == 1, (src.shape[0], 128))
    for i in range(D // 128):
        at = pl.multiple_of(where_ref[i] // 2 * 128, 128)
        block = src[:, pl.ds(at, 128)].astype(F32)
        block = jnp.where(odd, pltpu.roll(block, HEAD, 1), block)
        dst[:, i * 128 : (i + 1) * 128] = block.astype(BF)


def shard_rows(w_refs, k, cols):
    own, other = w_refs
    picks = [own[2 * k], other[2 * k], own[2 * k + 1], other[2 * k + 1]]
    return jnp.concatenate([ref[row : row + 64, cols] for ref, row in picks], axis=0)


def dot_shards(lhs, w_refs, cols):
    total = None
    for k in range(D // 256):
        term = jnp.dot(
            lhs[:, k * 256 : (k + 1) * 256],
            shard_rows(w_refs, k, cols),
            preferred_element_type=F32,
        )
        total = term if total is None else total + term
    return total


def encode_kernel(n_w, where_ref, *refs):
    x_refs = refs[:2]
    gain_in_ref, dw_ref, gain_mid_ref = refs[2:5]
    blocks = []
    for ref in refs[5 : 5 + n_w]:
        blocks += [(ref, row) for row in range(0, ref.shape[0], 64)]
    w_refs = blocks[: len(blocks) // 2], blocks[len(blocks) // 2 :]
    out_ref, plain, normed, spread, conv, taps, act = refs[5 + n_w :]
    step = 16
    for i, x in enumerate(x_refs):
        for r in range(0, TOT, step):
            plain[i * TOT + r : i * TOT + r + step, :] = norm_rows(
                x[r : r + step, :].astype(F32), gain_in_ref[...]
            ).astype(BF)
    order_columns(normed, plain, where_ref)
    taps[...] = dw_ref[...].astype(F32)
    rows = normed.shape[0]
    frame_rows = conv.shape[0]
    lanes = 2 * UTT
    target = []
    for i, x in enumerate(x_refs):
        places = x[TOT : TOT + EXTRA, :TOT].astype(F32)
        target.append(places[0:1] * lanes + places[1:2] + i * UTT)
    target = jnp.concatenate(target, axis=1)
    spot = lax.broadcasted_iota(jnp.int32, (frame_rows, rows), 0)
    expand = one_hot(target.astype(jnp.int32) == spot)
    column = jnp.broadcast_to(target, (8, rows)).T[:, 0:1].astype(jnp.int32)
    shrink = one_hot(column == lax.broadcasted_iota(jnp.int32, (rows, frame_rows), 1))
    for j in range(D // 256):
        value = dot_shards(normed, w_refs, slice(j * 256, (j + 1) * 256))
        gate = dot_shards(normed, w_refs, slice(D + j * 256, D + (j + 1) * 256))
        gated = (value * jax.nn.sigmoid(gate)).astype(BF)
        spread[:, j * 256 : (j + 1) * 256] = jnp.dot(expand, gated, preferred_element_type=F32)
    block = 8

    @pl.loop(0, D // 128)
    def _(c):
        cols = pl.ds(pl.multiple_of(c * 128, 128), 128)
        weights = [jnp.broadcast_to(taps[k : k + 1, cols], (lanes, 128)) for k in range(TAPS)]
        for first in range(0, FR, block):
            sums = [None] * block
            for f in range(max(0, first - HALF), min(FR, first + block + HALF)):
                here = spread[f * lanes : (f + 1) * lanes, cols]
                for b in range(block):
                    k = f - (first + b) + HALF
                    if 0 <= k < TAPS:
                        term = here * weights[k]
                        sums[b] = term if sums[b] is None else sums[b] + term
            for b in range(block):
                at = (first + b) * lanes
                conv[at : at + lanes, cols] = sums[b]

    for r in range(0, frame_rows, step):
        v = norm_rows(conv[r : r + step, :], gain_mid_ref[...])
        act[r : r + step, :] = (v * jax.nn.sigmoid(v)).astype(BF)
    for j in range(D // 256):
        cols = slice(j * 256, (j + 1) * 256)
        plain[:, cols] = jnp.dot(shrink, act[:, cols], preferred_element_type=F32).astype(BF)
    order_columns(normed, plain, where_ref)
    for j in range(D // 256):
        cols = slice(j * 256, (j + 1) * 256)
        low = dot_shards(normed, w_refs, slice(2 * D + j * 256, 2 * D + (j + 1) * 256))
        for i, x in enumerate(x_refs):
            at = slice(i * TOT, (i + 1) * TOT)
            out_ref[at, cols] = (x[:TOT, cols].astype(F32) + low[at]).astype(BF)
    utts = [x[TOT : TOT + EXTRA, :TOT].astype(F32)[1:2] for x in x_refs]
    kind = lax.broadcasted_iota(jnp.int32, (EXTRA, TOT), 0)
    out_ref[rows:, :TOT] = jnp.where(kind == 0, utts[0], utts[1]).astype(BF)
    out_ref[rows:, TOT:] = jnp.zeros((EXTRA, D - TOT), BF)


def encode(where, xs, gain_in, dw, gain_mid, shards):
    rows = 2 * TOT
    frame_rows = 2 * UTT * FR
    return pl.pallas_call(
        functools.partial(encode_kernel, len(shards)),
        out_shape=jax.ShapeDtypeStruct((rows + EXTRA, D), BF),
        in_specs=[SM] + [VM] * (5 + len(shards)),
        out_specs=VM,
        scratch_shapes=[
            pltpu.VMEM((rows, D), BF),
            pltpu.VMEM((rows, D), BF),
            pltpu.VMEM((frame_rows, D), F32),
            pltpu.VMEM((frame_rows, D), F32),
            pltpu.VMEM((TAPS, D), F32),
            pltpu.VMEM((frame_rows, D), BF),
        ],
        compiler_params=params(9),
        cost_estimate=cost(8_000_000_000, 8 << 20),
        name="encode",
    )(where, *xs, gain_in, dw, gain_mid, *shards)


def decode_kernel(n_mem, aliased, micro_ref, tgt_ref, *refs):
    mem_refs = refs[:n_mem]
    q_ref, hidden_ref, wk, wv, wo = refs[n_mem : n_mem + 5]
    rest = refs[n_mem + 5 + (1 if aliased else 0) :]
    out_hbm, keys, values, ctx, res, out_sems = rest
    slots = UTT * TGT
    micros = 2 * n_mem
    for w, out in ((wk, keys), (wv, values)):
        for p, mem in enumerate(mem_refs):
            for j in range(D // 256):
                cols = slice(j * 256, (j + 1) * 256)
                out[p * 2 * TOT : (p + 1) * 2 * TOT, cols] = jnp.dot(
                    mem[: 2 * TOT, :], w[:, cols], preferred_element_type=F32
                ).astype(BF)
    width = GROUP * HEAD
    tall = GROUP * slots
    row = lax.broadcasted_iota(jnp.int32, (tall, width), 0)
    lane = lax.broadcasted_iota(jnp.int32, (tall, width), 1)
    own = (row // slots) == (lane // HEAD)
    own_bf = one_hot(own)
    utt_of_row = (lax.broadcasted_iota(jnp.int32, (tall, TOT), 0) // TGT) % UTT
    groups = HEADS // GROUP
    for i in range(micros):
        utts = mem_refs[i // 2][2 * TOT : 2 * TOT + EXTRA, :TOT].astype(F32)
        allowed = utt_of_row == utts[i % 2 : i % 2 + 1].astype(jnp.int32)
        at = slice(i * TOT, (i + 1) * TOT)
        mine = slice(i * slots, (i + 1) * slots)
        from_rows = pl.ds(pl.multiple_of(micro_ref[i] * slots, slots), slots)
        cuts = [slice(j * width, (j + 1) * width) for j in range(groups)]
        scores = []
        for cols in cuts:
            q = q_ref[from_rows, cols]
            q = jnp.concatenate([q] * GROUP, axis=0) * own_bf
            scores.append(
                lax.dot_general(
                    q, keys[at, cols], (((1,), (1,)), ((), ())), preferred_element_type=F32
                )
            )
        probs = []
        for s in scores:
            s = jnp.where(allowed, s, -1e30)
            expo = jnp.exp(s - jnp.max(s, -1, keepdims=True))
            probs.append((expo * (1.0 / jnp.sum(expo, -1, keepdims=True))).astype(BF))
        for prob, cols in zip(probs, cuts):
            mixed = jnp.dot(prob, values[at, cols], preferred_element_type=F32)
            mixed = jnp.where(own, mixed, 0.0)
            total = mixed[:slots]
            for g in range(1, GROUP):
                total = total + mixed[g * slots : (g + 1) * slots]
            ctx[mine, cols] = total.astype(BF)
    pos = lax.broadcasted_iota(jnp.int32, (slots, 256), 0)
    for j in range(D // 256):
        cols = slice(j * 256, (j + 1) * 256)
        proj = jnp.dot(ctx[...], wo[:, cols], preferred_element_type=F32)
        for i in range(micros):
            mine = slice(i * slots, (i + 1) * slots)
            from_rows = pl.ds(pl.multiple_of(micro_ref[i] * slots, slots), slots)
            base = micro_ref[i] * UTT
            limit = jnp.full((slots, 256), tgt_ref[base], jnp.int32)
            for u in range(1, UTT):
                limit = jnp.where(pos // TGT == u, tgt_ref[base + u], limit)
            both = hidden_ref[from_rows, cols].astype(F32) + proj[mine]
            res[mine, cols] = jnp.where(pos % TGT < limit, both, 0.0).astype(BF)
    outs = []
    for i in range(micros):
        at = pl.ds(pl.multiple_of(micro_ref[i] * slots, slots), slots)
        here = pl.ds(i * slots, slots)
        copy = pltpu.make_async_copy(res.at[here, :], out_hbm.at[at, :], out_sems.at[i])
        copy.start()
        outs.append(copy)
    for copy in outs:
        copy.wait()


def decode(micro, tgt, mems, q, hidden, wk, wv, wo, prev):
    rows = hidden.shape[0]
    micros = 2 * len(mems)
    total = micros * TOT
    slots = UTT * TGT
    aliased = prev is not None
    args = [micro, tgt, *mems, q, hidden, wk, wv, wo] + ([prev] if aliased else [])
    return pl.pallas_call(
        functools.partial(decode_kernel, len(mems), aliased),
        out_shape=jax.ShapeDtypeStruct((rows, D), BF),
        in_specs=[SM, SM] + [VM] * (len(mems) + 5) + [HBM] * aliased,
        out_specs=HBM,
        scratch_shapes=[
            pltpu.VMEM((total, D), BF),
            pltpu.VMEM((total, D), BF),
            pltpu.VMEM((micros * slots, D), BF),
            pltpu.VMEM((micros * slots, D), BF),
            pltpu.SemaphoreType.DMA((micros,)),
        ],
        input_output_aliases={len(args) - 1: 0} if aliased else {},
        compiler_params=params(7),
        cost_estimate=cost(16 * total * D * D, 8 << 20),
        name="decode",
    )(*args)


def dp_perm(move):
    pairs = []
    for z in range(2):
        for x in range(4):
            for c in range(2):
                nz, nx, nc = move(z, x, c)
                pairs.append(((z * 4 + x) * 2 + c, (nz * 4 + nx % 4) * 2 + nc))
    return pairs


def section_perm(dy, dz):
    return [(y * 4 + z, (y + dy) % 4 * 4 + (z + dz) % 4) for y in range(4) for z in range(4)]


TO_PAIR = dp_perm(lambda z, x, c: (1 - z, x, c))
TO_RIGHT = dp_perm(lambda z, x, c: (z, x + 1, c))
TO_LEFT = dp_perm(lambda z, x, c: (z, x + 3, c))
TO_CORE = dp_perm(lambda z, x, c: (z, x, 1 - c))


def after(value, *others):
    return lax.optimization_barrier((value, *others))[0]


def stage(*values):
    return lax.optimization_barrier(values)


def shard_table():
    places = [(0, 0), (1, 0), (0, 3), (0, 1), (1, 3), (1, 1), (0, 2), (1, 2)]
    table = []
    for index in range(16):
        z, x, c = index // 8, index // 2 % 4, index % 2
        table.append(
            [
                ((z + a) % 2 * 4 + (x + b) % 4) * 2 + (c + s) % 2
                for s in (0, 1)
                for a, b in places
            ]
        )
    return table


REL = (0, -1, 1, 2)


def micro_table():
    return [
        [(y + dy) % 4 * 4 + (z + dz) % 4 for dy in REL for dz in REL]
        for y in range(4)
        for z in range(4)
    ]


def body(
    frames,
    frame_lens,
    tgt_lens,
    enc_gain_in,
    w_in,
    depthwise,
    enc_gain_mid,
    w_out,
    dec_gain,
    w_query,
    w_key,
    w_value,
    w_output,
    hidden,
):
    across = lambda v, perm: lax.ppermute(v, "dp", perm)
    along = lambda v, dy, dz: lax.ppermute(v, "section", section_perm(dy, dz))
    where = jnp.array(shard_table(), jnp.int32)[lax.axis_index("dp")]
    micros = jnp.array(micro_table(), jnp.int32)[lax.axis_index("section")].reshape(4, 4)

    own, packed = prepare(
        frame_lens.reshape(UTT), frames.reshape(UTT * FR, D), w_in, w_out
    )
    pair = across(own, TO_PAIR)
    own_l, own_r = across(own, TO_RIGHT), across(own, TO_LEFT)
    source = hidden.reshape(-1, D)
    query = project_query(source, dec_gain, w_query[0])
    swap = lambda *parts: across(jnp.concatenate(parts, axis=0), TO_CORE)
    go, packed_go = stage(pair, packed, own_l, own_r, query)[:2]

    pair_l, pair_r = across(go, TO_RIGHT), across(go, TO_LEFT)
    from_b = along(packed_go, 0, 1)
    near = swap(own, pair, own_l, own_r)
    go_l, go_r, packed_go = stage(own_l, pair_r, packed, pair_l, from_b)[:3]

    own_2, pair_2 = across(go_l, TO_RIGHT), across(go_r, TO_LEFT)
    middle = swap(pair_l, pair_r)
    from_a = along(packed_go, 0, -1)
    packed_2 = after(packed, from_a)

    far = swap(own_2, pair_2)
    from_2 = along(packed_2, 0, 2)
    shards = [own, pair, own_l, own_r, pair_l, pair_r, own_2, pair_2, near, middle, far]

    def encode_pair(first, second):
        return encode(
            where,
            [first, second],
            enc_gain_in.reshape(1, D),
            depthwise,
            enc_gain_mid.reshape(1, D),
            shards,
        )

    mem_a = encode_pair(packed, from_b)
    mem_b = encode_pair(from_a, from_2)

    a_from_l, a_from_r = along(mem_a, 1, 0), along(mem_a, -1, 0)
    b_from_l, b_from_r = along(mem_b, 1, 0), along(mem_b, -1, 0)

    tgt = tgt_lens.reshape(-1)

    def attend(parts, mems, prev):
        micro = jnp.concatenate([micros[y, z : z + 2] for y, z in parts])
        return decode(micro, tgt, mems, query, source, w_key[0], w_value[0], w_output[0], prev)

    a_far = along(a_from_l, 1, 0)
    out = attend([(0, 0), (0, 2)], [mem_a, after(mem_b, a_from_l)], None)
    out = attend([(1, 0), (2, 0)], [a_from_l, a_from_r], out)
    b_far = along(after(b_from_r, out), -1, 0)
    out = attend([(1, 2), (2, 2)], [b_from_l, b_from_r], out)
    out = attend([(3, 0), (3, 2)], [a_far, b_far], out)
    return out.reshape(hidden.shape)


def solution(mesh):
    return jax.shard_map(
        body,
        mesh=mesh,
        in_specs=(
            P("section", "dp", None, None),
            P("section", "dp", None),
            P(None, "dp"),
            P(),
            P("dp", None),
            P(),
            P(),
            P("dp", None),
            P("section", None),
            P("section", None, None),
            P("section", None, None),
            P("section", None, None),
            P("section", None, None),
            P("section", None, "dp", None, None),
        ),
        out_specs=P("section", None, "dp", None, None),
        check_vma=False,
    )
```

```python
import functools

import jax
import jax.numpy as jnp
from jax import lax
from jax.experimental import pallas as pl
from jax.experimental.pallas import tpu as pltpu
from jax.sharding import PartitionSpec as P

HEADS = 16
D = 1024
HEAD = 64
FR = 40
TGT = 8
UTT = 4
TOT = 128
TAPS = 31
HALF = 15
GROUP = 4
EXTRA = 16
BF = jnp.bfloat16
F32 = jnp.float32
HBM = pl.BlockSpec(memory_space=pltpu.HBM)
VM = pl.BlockSpec(memory_space=pltpu.VMEM)
SM = pl.BlockSpec(memory_space=pltpu.SMEM)


def norm_rows(values, gain):
    average = jnp.mean(values, -1, keepdims=True)
    centered = values - average
    spread = jnp.mean(centered * centered, -1, keepdims=True)
    return centered * lax.rsqrt(spread + 1e-05) * gain


def params(limit):
    return pltpu.CompilerParams(vmem_limit_bytes=limit << 20)


def cost(flops, moved):
    return pl.CostEstimate(flops=flops, bytes_accessed=moved, transcendentals=0)


def one_hot(flags):
    return jnp.where(flags, 1.0, 0.0).astype(BF)


def slot_place(slot, lens_ref):
    utt = jnp.zeros_like(slot)
    start = jnp.zeros_like(slot)
    end = jnp.int32(0)
    for u in range(UTT - 1):
        end = end + lens_ref[u]
        later = slot >= end
        utt = jnp.where(later, u + 1, utt)
        start = jnp.where(later, end, start)
    return utt, slot - start


def prepare_kernel(lens_ref, frames_hbm, w_in_hbm, w_out_hbm, own_ref, out_ref, frames_ref, sems):
    loads = [
        pltpu.make_async_copy(w_in_hbm, own_ref.at[:, pl.ds(0, 2 * D)], sems.at[0]),
        pltpu.make_async_copy(w_out_hbm, own_ref.at[:, pl.ds(2 * D, D)], sems.at[1]),
        pltpu.make_async_copy(frames_hbm, frames_ref, sems.at[2]),
    ]
    for load in loads:
        load.start()
    slot = lax.broadcasted_iota(jnp.int32, (TOT, UTT * FR), 0)
    lane = lax.broadcasted_iota(jnp.int32, (TOT, UTT * FR), 1)
    utt, frame = slot_place(slot, lens_ref)
    pick = one_hot(utt * FR + frame == lane)
    utt, frame = slot_place(lax.broadcasted_iota(jnp.int32, (EXTRA, TOT), 1), lens_ref)
    kind = lax.broadcasted_iota(jnp.int32, (EXTRA, TOT), 0)
    out_ref[TOT:, :TOT] = jnp.where(kind == 0, frame, utt).astype(F32).astype(BF)
    out_ref[TOT:, TOT:] = jnp.zeros((EXTRA, D - TOT), BF)
    loads[2].wait()
    for j in range(D // 256):
        cols = slice(j * 256, (j + 1) * 256)
        out_ref[:TOT, cols] = jnp.dot(
            pick, frames_ref[:, cols], preferred_element_type=F32
        ).astype(BF)
    loads[0].wait()
    loads[1].wait()


def prepare(lens, frames, w_in, w_out):
    depth = w_in.shape[0]
    return pl.pallas_call(
        prepare_kernel,
        out_shape=(
            jax.ShapeDtypeStruct((depth, 3 * D), BF),
            jax.ShapeDtypeStruct((TOT + EXTRA, D), BF),
        ),
        in_specs=[SM, HBM, HBM, HBM],
        out_specs=(VM, VM),
        scratch_shapes=[pltpu.VMEM((UTT * FR, D), BF), pltpu.SemaphoreType.DMA((3,))],
        compiler_params=params(60),
        cost_estimate=cost(50_000_000, 1_400_000),
        name="prepare",
    )(lens, frames, w_in, w_out)


def query_kernel(hidden_ref, gain_ref, w_ref, out_ref, normed):
    @pl.loop(0, hidden_ref.shape[0] // 64)
    def _(i):
        for r in range(0, 64, 16):
            rows = pl.ds(pl.multiple_of(i * 64 + r, 16), 16)
            normed[rows, :] = norm_rows(hidden_ref[rows, :].astype(F32), gain_ref[...]).astype(BF)

    for j in range(D // 256):
        cols = slice(j * 256, (j + 1) * 256)
        q = jnp.dot(normed[...], w_ref[:, cols], preferred_element_type=F32)
        out_ref[:, cols] = (q * (HEAD**-0.5)).astype(BF)


def project_query(hidden, gain, w):
    rows = hidden.shape[0]
    return pl.pallas_call(
        query_kernel,
        out_shape=jax.ShapeDtypeStruct((rows, D), BF),
        in_specs=[VM, VM, VM],
        out_specs=VM,
        scratch_shapes=[pltpu.VMEM((rows, D), BF)],
        compiler_params=params(8),
        cost_estimate=cost(2 * rows * D * D, 4 << 20),
        name="project_query",
    )(hidden, gain, w)


def order_columns(dst, src, where_ref):
    odd = jnp.broadcast_to(where_ref[0] % 2 == 1, (src.shape[0], 128))
    for i in range(D // 128):
        at = pl.multiple_of(where_ref[i] // 2 * 128, 128)
        block = src[:, pl.ds(at, 128)].astype(F32)
        block = jnp.where(odd, pltpu.roll(block, HEAD, 1), block)
        dst[:, i * 128 : (i + 1) * 128] = block.astype(BF)


def shard_rows(w_refs, k, cols):
    own, other = w_refs
    picks = [own[2 * k], other[2 * k], own[2 * k + 1], other[2 * k + 1]]
    return jnp.concatenate([ref[row : row + 64, cols] for ref, row in picks], axis=0)


def dot_shards(lhs, w_refs, cols):
    total = None
    for k in range(D // 256):
        term = jnp.dot(
            lhs[:, k * 256 : (k + 1) * 256],
            shard_rows(w_refs, k, cols),
            preferred_element_type=F32,
        )
        total = term if total is None else total + term
    return total


def encode_kernel(n_w, where_ref, *refs):
    x_refs = refs[:2]
    gain_in_ref, dw_ref, gain_mid_ref = refs[2:5]
    blocks = []
    for ref in refs[5 : 5 + n_w]:
        blocks += [(ref, row) for row in range(0, ref.shape[0], 64)]
    w_refs = blocks[: len(blocks) // 2], blocks[len(blocks) // 2 :]
    out_ref, plain, normed, spread, conv, taps, act = refs[5 + n_w :]
    step = 16
    for i, x in enumerate(x_refs):
        for r in range(0, TOT, step):
            plain[i * TOT + r : i * TOT + r + step, :] = norm_rows(
                x[r : r + step, :].astype(F32), gain_in_ref[...]
            ).astype(BF)
    order_columns(normed, plain, where_ref)
    taps[...] = dw_ref[...].astype(F32)
    rows = normed.shape[0]
    frame_rows = conv.shape[0]
    lanes = 2 * UTT
    target = []
    for i, x in enumerate(x_refs):
        places = x[TOT : TOT + EXTRA, :TOT].astype(F32)
        target.append(places[0:1] * lanes + places[1:2] + i * UTT)
    target = jnp.concatenate(target, axis=1)
    spot = lax.broadcasted_iota(jnp.int32, (frame_rows, rows), 0)
    expand = one_hot(target.astype(jnp.int32) == spot)
    column = jnp.broadcast_to(target, (8, rows)).T[:, 0:1].astype(jnp.int32)
    shrink = one_hot(column == lax.broadcasted_iota(jnp.int32, (rows, frame_rows), 1))
    for j in range(D // 256):
        value = dot_shards(normed, w_refs, slice(j * 256, (j + 1) * 256))
        gate = dot_shards(normed, w_refs, slice(D + j * 256, D + (j + 1) * 256))
        gated = (value * jax.nn.sigmoid(gate)).astype(BF)
        spread[:, j * 256 : (j + 1) * 256] = jnp.dot(expand, gated, preferred_element_type=F32)
    block = 8

    @pl.loop(0, D // 128)
    def _(c):
        cols = pl.ds(pl.multiple_of(c * 128, 128), 128)
        weights = [jnp.broadcast_to(taps[k : k + 1, cols], (lanes, 128)) for k in range(TAPS)]
        for first in range(0, FR, block):
            sums = [None] * block
            for f in range(max(0, first - HALF), min(FR, first + block + HALF)):
                here = spread[f * lanes : (f + 1) * lanes, cols]
                for b in range(block):
                    k = f - (first + b) + HALF
                    if 0 <= k < TAPS:
                        term = here * weights[k]
                        sums[b] = term if sums[b] is None else sums[b] + term
            for b in range(block):
                at = (first + b) * lanes
                conv[at : at + lanes, cols] = sums[b]

    for r in range(0, frame_rows, step):
        v = norm_rows(conv[r : r + step, :], gain_mid_ref[...])
        act[r : r + step, :] = (v * jax.nn.sigmoid(v)).astype(BF)
    for j in range(D // 256):
        cols = slice(j * 256, (j + 1) * 256)
        plain[:, cols] = jnp.dot(shrink, act[:, cols], preferred_element_type=F32).astype(BF)
    order_columns(normed, plain, where_ref)
    for j in range(D // 256):
        cols = slice(j * 256, (j + 1) * 256)
        low = dot_shards(normed, w_refs, slice(2 * D + j * 256, 2 * D + (j + 1) * 256))
        for i, x in enumerate(x_refs):
            at = slice(i * TOT, (i + 1) * TOT)
            out_ref[at, cols] = (x[:TOT, cols].astype(F32) + low[at]).astype(BF)
    utts = [x[TOT : TOT + EXTRA, :TOT].astype(F32)[1:2] for x in x_refs]
    kind = lax.broadcasted_iota(jnp.int32, (EXTRA, TOT), 0)
    out_ref[rows:, :TOT] = jnp.where(kind == 0, utts[0], utts[1]).astype(BF)
    out_ref[rows:, TOT:] = jnp.zeros((EXTRA, D - TOT), BF)


def encode(where, xs, gain_in, dw, gain_mid, shards):
    rows = 2 * TOT
    frame_rows = 2 * UTT * FR
    return pl.pallas_call(
        functools.partial(encode_kernel, len(shards)),
        out_shape=jax.ShapeDtypeStruct((rows + EXTRA, D), BF),
        in_specs=[SM] + [VM] * (5 + len(shards)),
        out_specs=VM,
        scratch_shapes=[
            pltpu.VMEM((rows, D), BF),
            pltpu.VMEM((rows, D), BF),
            pltpu.VMEM((frame_rows, D), F32),
            pltpu.VMEM((frame_rows, D), F32),
            pltpu.VMEM((TAPS, D), F32),
            pltpu.VMEM((frame_rows, D), BF),
        ],
        compiler_params=params(9),
        cost_estimate=cost(8_000_000_000, 8 << 20),
        name="encode",
    )(where, *xs, gain_in, dw, gain_mid, *shards)


def decode_kernel(n_mem, aliased, micro_ref, tgt_ref, *refs):
    mem_refs = refs[:n_mem]
    q_ref, hidden_ref, wk, wv, wo = refs[n_mem : n_mem + 5]
    rest = refs[n_mem + 5 + (1 if aliased else 0) :]
    out_hbm, keys, values, ctx, res, seg, out_sems = rest
    slots = UTT * TGT
    micros = 2 * n_mem
    for w, out in ((wk, keys), (wv, values)):
        for p, mem in enumerate(mem_refs):
            for j in range(D // 256):
                cols = slice(j * 256, (j + 1) * 256)
                out[p * 2 * TOT : (p + 1) * 2 * TOT, cols] = jnp.dot(
                    mem[: 2 * TOT, :], w[:, cols], preferred_element_type=F32
                ).astype(BF)
    width = GROUP * HEAD
    tall = GROUP * slots
    row = lax.broadcasted_iota(jnp.int32, (tall, width), 0)
    lane = lax.broadcasted_iota(jnp.int32, (tall, width), 1)
    own = (row // slots) == (lane // HEAD)
    own_bf = one_hot(own)
    utt_of_row = (lax.broadcasted_iota(jnp.int32, (tall, TOT), 0) // TGT) % UTT
    groups = HEADS // GROUP
    for i in range(micros):
        utts = mem_refs[i // 2][2 * TOT : 2 * TOT + EXTRA, :TOT].astype(F32)
        seg[i * 8 : i * 8 + 8, :] = jnp.broadcast_to(utts[i % 2 : i % 2 + 1], (8, TOT))

    def attend(i):
        line = seg[pl.ds(pl.multiple_of(i * 8, 8), 8), :]
        allowed = utt_of_row == line[0:1].astype(jnp.int32)
        at = pl.ds(pl.multiple_of(i * TOT, TOT), TOT)
        mine = pl.ds(pl.multiple_of(i * slots, slots), slots)
        from_rows = pl.ds(pl.multiple_of(micro_ref[i] * slots, slots), slots)
        cuts = [slice(j * width, (j + 1) * width) for j in range(groups)]
        scores = []
        for cols in cuts:
            q = q_ref[from_rows, cols]
            q = jnp.concatenate([q] * GROUP, axis=0) * own_bf
            scores.append(
                lax.dot_general(
                    q, keys[at, cols], (((1,), (1,)), ((), ())), preferred_element_type=F32
                )
            )
        probs = []
        for s in scores:
            s = jnp.where(allowed, s, -1e30)
            expo = jnp.exp(s - jnp.max(s, -1, keepdims=True))
            probs.append((expo * (1.0 / jnp.sum(expo, -1, keepdims=True))).astype(BF))
        for prob, cols in zip(probs, cuts):
            mixed = jnp.dot(prob, values[at, cols], preferred_element_type=F32)
            mixed = jnp.where(own, mixed, 0.0)
            total = mixed[:slots]
            for g in range(1, GROUP):
                total = total + mixed[g * slots : (g + 1) * slots]
            ctx[mine, cols] = total.astype(BF)

    @pl.loop(0, micros // 2)
    def _(p):
        attend(2 * p)
        attend(2 * p + 1)

    pos = lax.broadcasted_iota(jnp.int32, (slots, 256), 0)

    @pl.loop(0, D // 512)
    def _(h):
      for half in range(2):
        cols = pl.ds(pl.multiple_of(h * 512 + half * 256, 256), 256)
        proj = jnp.dot(ctx[...], wo[:, cols], preferred_element_type=F32)
        for i in range(micros):
            mine = slice(i * slots, (i + 1) * slots)
            from_rows = pl.ds(pl.multiple_of(micro_ref[i] * slots, slots), slots)
            base = micro_ref[i] * UTT
            limit = jnp.full((slots, 256), tgt_ref[base], jnp.int32)
            for u in range(1, UTT):
                limit = jnp.where(pos // TGT == u, tgt_ref[base + u], limit)
            both = hidden_ref[from_rows, cols].astype(F32) + proj[mine]
            res[mine, cols] = jnp.where(pos % TGT < limit, both, 0.0).astype(BF)

    outs = []
    for i in range(micros):
        at = pl.ds(pl.multiple_of(micro_ref[i] * slots, slots), slots)
        here = pl.ds(i * slots, slots)
        copy = pltpu.make_async_copy(res.at[here, :], out_hbm.at[at, :], out_sems.at[i])
        copy.start()
        outs.append(copy)
    for copy in outs:
        copy.wait()


def decode(micro, tgt, mems, q, hidden, wk, wv, wo, prev):
    rows = hidden.shape[0]
    micros = 2 * len(mems)
    total = micros * TOT
    slots = UTT * TGT
    aliased = prev is not None
    args = [micro, tgt, *mems, q, hidden, wk, wv, wo] + ([prev] if aliased else [])
    return pl.pallas_call(
        functools.partial(decode_kernel, len(mems), aliased),
        out_shape=jax.ShapeDtypeStruct((rows, D), BF),
        in_specs=[SM, SM] + [VM] * (len(mems) + 5) + [HBM] * aliased,
        out_specs=HBM,
        scratch_shapes=[
            pltpu.VMEM((total, D), BF),
            pltpu.VMEM((total, D), BF),
            pltpu.VMEM((micros * slots, D), BF),
            pltpu.VMEM((micros * slots, D), BF),
            pltpu.VMEM((micros * 8, TOT), F32),
            pltpu.SemaphoreType.DMA((micros,)),
        ],
        input_output_aliases={len(args) - 1: 0} if aliased else {},
        compiler_params=params(7),
        cost_estimate=cost(16 * total * D * D, 8 << 20),
        name="decode",
    )(*args)


def dp_perm(move):
    pairs = []
    for z in range(2):
        for x in range(4):
            for c in range(2):
                nz, nx, nc = move(z, x, c)
                pairs.append(((z * 4 + x) * 2 + c, (nz * 4 + nx % 4) * 2 + nc))
    return pairs


def section_perm(dy, dz):
    return [(y * 4 + z, (y + dy) % 4 * 4 + (z + dz) % 4) for y in range(4) for z in range(4)]


TO_PAIR = dp_perm(lambda z, x, c: (1 - z, x, c))
TO_RIGHT = dp_perm(lambda z, x, c: (z, x + 1, c))
TO_LEFT = dp_perm(lambda z, x, c: (z, x + 3, c))
TO_CORE = dp_perm(lambda z, x, c: (z, x, 1 - c))


def pass_kernel(value_ref, *refs):
    refs[-1][...] = value_ref[...]


def pass_after(value, *others):
    return pl.pallas_call(
        pass_kernel,
        out_shape=jax.ShapeDtypeStruct(value.shape, value.dtype),
        in_specs=[VM] + [HBM] * len(others),
        out_specs=VM,
        compiler_params=params(2),
        cost_estimate=cost(0, 600_000),
        name="pass_after",
    )(value, *others)


def shard_table():
    places = [(0, 0), (1, 0), (0, 3), (0, 1), (1, 3), (1, 1), (0, 2), (1, 2)]
    table = []
    for index in range(16):
        z, x, c = index // 8, index // 2 % 4, index % 2
        table.append(
            [
                ((z + a) % 2 * 4 + (x + b) % 4) * 2 + (c + s) % 2
                for s in (0, 1)
                for a, b in places
            ]
        )
    return table


REL = (0, -1, 1, 2)


def micro_table():
    return [
        [(y + dy) % 4 * 4 + (z + dz) % 4 for dy in REL for dz in REL]
        for y in range(4)
        for z in range(4)
    ]


def body(
    frames,
    frame_lens,
    tgt_lens,
    enc_gain_in,
    w_in,
    depthwise,
    enc_gain_mid,
    w_out,
    dec_gain,
    w_query,
    w_key,
    w_value,
    w_output,
    hidden,
):
    across = lambda v, perm: lax.ppermute(v, "dp", perm)
    along = lambda v, dy, dz: lax.ppermute(v, "section", section_perm(dy, dz))
    where = jnp.array(shard_table(), jnp.int32)[lax.axis_index("dp")]
    micros = jnp.array(micro_table(), jnp.int32)[lax.axis_index("section")].reshape(4, 4)

    own, packed = prepare(
        frame_lens.reshape(UTT), frames.reshape(UTT * FR, D), w_in, w_out
    )
    pair = across(own, TO_PAIR)
    own_r, own_l = across(own, TO_LEFT), across(own, TO_RIGHT)
    source = hidden.reshape(-1, D)
    query = project_query(source, dec_gain, w_query[0])
    pair_l, pair_r = across(pair, TO_RIGHT), across(pair, TO_LEFT)
    own_2, pair_2 = across(own_l, TO_RIGHT), across(pair_r, TO_LEFT)
    ready = pass_after(packed, pair, query)
    from_b = along(ready, 0, 1)
    shards = [own, pair, own_l, own_r, pair_l, pair_r, own_2, pair_2]
    turn = [pass_after(own, pair, query, from_b)] + shards[1:]
    shards += [across(v, TO_CORE) for v in turn]

    from_a, from_2 = along(ready, 0, -1), along(ready, 0, 2)

    def encode_pair(first, second):
        return encode(
            where,
            [first, second],
            enc_gain_in.reshape(1, D),
            depthwise,
            enc_gain_mid.reshape(1, D),
            shards,
        )

    mem_a = encode_pair(packed, from_b)
    mem_b = encode_pair(from_a, from_2)

    a_from_l, a_from_r = along(mem_a, 1, 0), along(mem_a, -1, 0)
    b_from_l, b_from_r = along(mem_b, 1, 0), along(mem_b, -1, 0)

    tgt = tgt_lens.reshape(-1)

    def attend(parts, mems, prev):
        micro = jnp.concatenate([micros[y, z : z + 2] for y, z in parts])
        return decode(micro, tgt, mems, query, source, w_key[0], w_value[0], w_output[0], prev)

    a_far, b_far = along(a_from_l, 1, 0), along(b_from_r, -1, 0)
    out = attend([(0, 0), (0, 2)], [mem_a, mem_b], None)
    out = attend([(1, 0), (2, 0)], [a_from_l, a_from_r], out)
    out = attend([(1, 2), (2, 2)], [b_from_l, b_from_r], out)
    out = attend([(3, 0), (3, 2)], [a_far, b_far], out)
    return out.reshape(hidden.shape)


def solution(mesh):
    return jax.shard_map(
        body,
        mesh=mesh,
        in_specs=(
            P("section", "dp", None, None),
            P("section", "dp", None),
            P(None, "dp"),
            P(),
            P("dp", None),
            P(),
            P(),
            P("dp", None),
            P("section", None),
            P("section", None, None),
            P("section", None, None),
            P("section", None, None),
            P("section", None, None),
            P("section", None, "dp", None, None),
        ),
        out_specs=P("section", None, "dp", None, None),
        check_vma=False,
    )
```

```python
import functools

import jax
import jax.numpy as jnp
from jax import lax
from jax.experimental import pallas as pl
from jax.experimental.pallas import tpu as pltpu
from jax.sharding import PartitionSpec as P

HEADS = 16
D = 1024
HEAD = 64
FR = 40
TGT = 8
UTT = 4
TOT = 128
TAPS = 31
HALF = 15
GROUP = 4
EXTRA = 16
BF = jnp.bfloat16
F32 = jnp.float32
HBM = pl.BlockSpec(memory_space=pltpu.HBM)
VM = pl.BlockSpec(memory_space=pltpu.VMEM)
SM = pl.BlockSpec(memory_space=pltpu.SMEM)


def norm_rows(values, gain):
    average = jnp.mean(values, -1, keepdims=True)
    centered = values - average
    spread = jnp.mean(centered * centered, -1, keepdims=True)
    return centered * lax.rsqrt(spread + 1e-05) * gain


def params(limit):
    return pltpu.CompilerParams(vmem_limit_bytes=limit << 20)


def cost(flops, moved):
    return pl.CostEstimate(flops=flops, bytes_accessed=moved, transcendentals=0)


def one_hot(flags):
    return jnp.where(flags, 1.0, 0.0).astype(BF)


def slot_place(slot, lens_ref):
    utt = jnp.zeros_like(slot)
    start = jnp.zeros_like(slot)
    end = jnp.int32(0)
    for u in range(UTT - 1):
        end = end + lens_ref[u]
        later = slot >= end
        utt = jnp.where(later, u + 1, utt)
        start = jnp.where(later, end, start)
    return utt, slot - start


def prepare_kernel(lens_ref, frames_hbm, w_in_hbm, w_out_hbm, own_ref, out_ref, frames_ref, sems):
    loads = [
        pltpu.make_async_copy(w_in_hbm, own_ref.at[:, pl.ds(0, 2 * D)], sems.at[0]),
        pltpu.make_async_copy(w_out_hbm, own_ref.at[:, pl.ds(2 * D, D)], sems.at[1]),
        pltpu.make_async_copy(frames_hbm, frames_ref, sems.at[2]),
    ]
    for load in loads:
        load.start()
    slot = lax.broadcasted_iota(jnp.int32, (TOT, UTT * FR), 0)
    lane = lax.broadcasted_iota(jnp.int32, (TOT, UTT * FR), 1)
    utt, frame = slot_place(slot, lens_ref)
    pick = one_hot(utt * FR + frame == lane)
    utt, frame = slot_place(lax.broadcasted_iota(jnp.int32, (EXTRA, TOT), 1), lens_ref)
    kind = lax.broadcasted_iota(jnp.int32, (EXTRA, TOT), 0)
    out_ref[TOT:, :TOT] = jnp.where(kind == 0, frame, utt).astype(F32).astype(BF)
    out_ref[TOT:, TOT:] = jnp.zeros((EXTRA, D - TOT), BF)
    loads[2].wait()
    for j in range(D // 256):
        cols = slice(j * 256, (j + 1) * 256)
        out_ref[:TOT, cols] = jnp.dot(
            pick, frames_ref[:, cols], preferred_element_type=F32
        ).astype(BF)
    loads[0].wait()
    loads[1].wait()


def prepare(lens, frames, w_in, w_out):
    depth = w_in.shape[0]
    return pl.pallas_call(
        prepare_kernel,
        out_shape=(
            jax.ShapeDtypeStruct((depth, 3 * D), BF),
            jax.ShapeDtypeStruct((TOT + EXTRA, D), BF),
        ),
        in_specs=[SM, HBM, HBM, HBM],
        out_specs=(VM, VM),
        scratch_shapes=[pltpu.VMEM((UTT * FR, D), BF), pltpu.SemaphoreType.DMA((3,))],
        compiler_params=params(60),
        cost_estimate=cost(50_000_000, 1_400_000),
        name="prepare",
    )(lens, frames, w_in, w_out)


def query_kernel(hidden_ref, gain_ref, w_ref, out_ref, normed):
    @pl.loop(0, hidden_ref.shape[0] // 64)
    def _(i):
        for r in range(0, 64, 16):
            rows = pl.ds(pl.multiple_of(i * 64 + r, 16), 16)
            normed[rows, :] = norm_rows(hidden_ref[rows, :].astype(F32), gain_ref[...]).astype(BF)

    for j in range(D // 256):
        cols = slice(j * 256, (j + 1) * 256)
        q = jnp.dot(normed[...], w_ref[:, cols], preferred_element_type=F32)
        out_ref[:, cols] = (q * (HEAD**-0.5)).astype(BF)


def project_query(hidden, gain, w):
    rows = hidden.shape[0]
    return pl.pallas_call(
        query_kernel,
        out_shape=jax.ShapeDtypeStruct((rows, D), BF),
        in_specs=[VM, VM, VM],
        out_specs=VM,
        scratch_shapes=[pltpu.VMEM((rows, D), BF)],
        compiler_params=params(8),
        cost_estimate=cost(2 * rows * D * D, 4 << 20),
        name="project_query",
    )(hidden, gain, w)


def order_columns(dst, src, where_ref):
    odd = jnp.broadcast_to(where_ref[0] % 2 == 1, (src.shape[0], 128))
    for i in range(D // 128):
        at = pl.multiple_of(where_ref[i] // 2 * 128, 128)
        block = src[:, pl.ds(at, 128)].astype(F32)
        block = jnp.where(odd, pltpu.roll(block, HEAD, 1), block)
        dst[:, i * 128 : (i + 1) * 128] = block.astype(BF)


def shard_rows(w_refs, k, cols):
    own, other = w_refs
    picks = [own[2 * k], other[2 * k], own[2 * k + 1], other[2 * k + 1]]
    return jnp.concatenate([ref[row : row + 64, cols] for ref, row in picks], axis=0)


def dot_shards(lhs, w_refs, cols):
    total = None
    for k in range(D // 256):
        term = jnp.dot(
            lhs[:, k * 256 : (k + 1) * 256],
            shard_rows(w_refs, k, cols),
            preferred_element_type=F32,
        )
        total = term if total is None else total + term
    return total


def encode_kernel(n_w, where_ref, *refs):
    x_refs = refs[:2]
    gain_in_ref, dw_ref, gain_mid_ref = refs[2:5]
    blocks = []
    for ref in refs[5 : 5 + n_w]:
        blocks += [(ref, row) for row in range(0, ref.shape[0], 64)]
    w_refs = blocks[: len(blocks) // 2], blocks[len(blocks) // 2 :]
    out_ref, plain, normed, spread, conv, taps, act = refs[5 + n_w :]
    step = 16
    for i, x in enumerate(x_refs):
        for r in range(0, TOT, step):
            plain[i * TOT + r : i * TOT + r + step, :] = norm_rows(
                x[r : r + step, :].astype(F32), gain_in_ref[...]
            ).astype(BF)
    order_columns(normed, plain, where_ref)
    taps[...] = dw_ref[...].astype(F32)
    rows = normed.shape[0]
    frame_rows = conv.shape[0]
    lanes = 2 * UTT
    target = []
    for i, x in enumerate(x_refs):
        places = x[TOT : TOT + EXTRA, :TOT].astype(F32)
        target.append(places[0:1] * lanes + places[1:2] + i * UTT)
    target = jnp.concatenate(target, axis=1)
    spot = lax.broadcasted_iota(jnp.int32, (frame_rows, rows), 0)
    expand = one_hot(target.astype(jnp.int32) == spot)
    column = jnp.broadcast_to(target, (8, rows)).T[:, 0:1].astype(jnp.int32)
    shrink = one_hot(column == lax.broadcasted_iota(jnp.int32, (rows, frame_rows), 1))
    for j in range(D // 256):
        value = dot_shards(normed, w_refs, slice(j * 256, (j + 1) * 256))
        gate = dot_shards(normed, w_refs, slice(D + j * 256, D + (j + 1) * 256))
        gated = (value * jax.nn.sigmoid(gate)).astype(BF)
        spread[:, j * 256 : (j + 1) * 256] = jnp.dot(expand, gated, preferred_element_type=F32)
    block = 8

    @pl.loop(0, D // 128)
    def _(c):
        cols = pl.ds(pl.multiple_of(c * 128, 128), 128)
        weights = [jnp.broadcast_to(taps[k : k + 1, cols], (lanes, 128)) for k in range(TAPS)]
        for first in range(0, FR, block):
            sums = [None] * block
            for f in range(max(0, first - HALF), min(FR, first + block + HALF)):
                here = spread[f * lanes : (f + 1) * lanes, cols]
                for b in range(block):
                    k = f - (first + b) + HALF
                    if 0 <= k < TAPS:
                        term = here * weights[k]
                        sums[b] = term if sums[b] is None else sums[b] + term
            for b in range(block):
                at = (first + b) * lanes
                conv[at : at + lanes, cols] = sums[b]

    for r in range(0, frame_rows, step):
        v = norm_rows(conv[r : r + step, :], gain_mid_ref[...])
        act[r : r + step, :] = (v * jax.nn.sigmoid(v)).astype(BF)
    for j in range(D // 256):
        cols = slice(j * 256, (j + 1) * 256)
        plain[:, cols] = jnp.dot(shrink, act[:, cols], preferred_element_type=F32).astype(BF)
    order_columns(normed, plain, where_ref)
    for j in range(D // 256):
        cols = slice(j * 256, (j + 1) * 256)
        low = dot_shards(normed, w_refs, slice(2 * D + j * 256, 2 * D + (j + 1) * 256))
        for i, x in enumerate(x_refs):
            at = slice(i * TOT, (i + 1) * TOT)
            out_ref[at, cols] = (x[:TOT, cols].astype(F32) + low[at]).astype(BF)
    utts = [x[TOT : TOT + EXTRA, :TOT].astype(F32)[1:2] for x in x_refs]
    kind = lax.broadcasted_iota(jnp.int32, (EXTRA, TOT), 0)
    out_ref[rows:, :TOT] = jnp.where(kind == 0, utts[0], utts[1]).astype(BF)
    out_ref[rows:, TOT:] = jnp.zeros((EXTRA, D - TOT), BF)


def encode(where, xs, gain_in, dw, gain_mid, shards):
    rows = 2 * TOT
    frame_rows = 2 * UTT * FR
    return pl.pallas_call(
        functools.partial(encode_kernel, len(shards)),
        out_shape=jax.ShapeDtypeStruct((rows + EXTRA, D), BF),
        in_specs=[SM] + [VM] * (5 + len(shards)),
        out_specs=VM,
        scratch_shapes=[
            pltpu.VMEM((rows, D), BF),
            pltpu.VMEM((rows, D), BF),
            pltpu.VMEM((frame_rows, D), F32),
            pltpu.VMEM((frame_rows, D), F32),
            pltpu.VMEM((TAPS, D), F32),
            pltpu.VMEM((frame_rows, D), BF),
        ],
        compiler_params=params(9),
        cost_estimate=cost(8_000_000_000, 8 << 20),
        name="encode",
    )(where, *xs, gain_in, dw, gain_mid, *shards)


def decode_kernel(n_mem, aliased, micro_ref, tgt_ref, *refs):
    mem_refs = refs[:n_mem]
    q_ref, hidden_ref, wk, wv, wo = refs[n_mem : n_mem + 5]
    rest = refs[n_mem + 5 + (1 if aliased else 0) :]
    out_hbm, keys, values, ctx, res, seg, out_sems = rest
    slots = UTT * TGT
    micros = 2 * n_mem
    for w, out in ((wk, keys), (wv, values)):
        for p, mem in enumerate(mem_refs):
            for j in range(D // 256):
                cols = slice(j * 256, (j + 1) * 256)
                out[p * 2 * TOT : (p + 1) * 2 * TOT, cols] = jnp.dot(
                    mem[: 2 * TOT, :], w[:, cols], preferred_element_type=F32
                ).astype(BF)
    width = GROUP * HEAD
    tall = GROUP * slots
    row = lax.broadcasted_iota(jnp.int32, (tall, width), 0)
    lane = lax.broadcasted_iota(jnp.int32, (tall, width), 1)
    own = (row // slots) == (lane // HEAD)
    own_bf = one_hot(own)
    utt_of_row = (lax.broadcasted_iota(jnp.int32, (tall, TOT), 0) // TGT) % UTT
    groups = HEADS // GROUP
    for i in range(micros):
        utts = mem_refs[i // 2][2 * TOT : 2 * TOT + EXTRA, :TOT].astype(F32)
        seg[i * 8 : i * 8 + 8, :] = jnp.broadcast_to(utts[i % 2 : i % 2 + 1], (8, TOT))

    def attend(i):
        line = seg[pl.ds(pl.multiple_of(i * 8, 8), 8), :]
        allowed = utt_of_row == line[0:1].astype(jnp.int32)
        at = pl.ds(pl.multiple_of(i * TOT, TOT), TOT)
        mine = pl.ds(pl.multiple_of(i * slots, slots), slots)
        from_rows = pl.ds(pl.multiple_of(micro_ref[i] * slots, slots), slots)
        cuts = [slice(j * width, (j + 1) * width) for j in range(groups)]
        scores = []
        for cols in cuts:
            q = q_ref[from_rows, cols]
            q = jnp.concatenate([q] * GROUP, axis=0) * own_bf
            scores.append(
                lax.dot_general(
                    q, keys[at, cols], (((1,), (1,)), ((), ())), preferred_element_type=F32
                )
            )
        probs = []
        for s in scores:
            s = jnp.where(allowed, s, -1e30)
            expo = jnp.exp(s - jnp.max(s, -1, keepdims=True))
            probs.append((expo * (1.0 / jnp.sum(expo, -1, keepdims=True))).astype(BF))
        for prob, cols in zip(probs, cuts):
            mixed = jnp.dot(prob, values[at, cols], preferred_element_type=F32)
            mixed = jnp.where(own, mixed, 0.0)
            total = mixed[:slots]
            for g in range(1, GROUP):
                total = total + mixed[g * slots : (g + 1) * slots]
            ctx[mine, cols] = total.astype(BF)

    @pl.loop(0, micros // 2)
    def _(p):
        attend(2 * p)
        attend(2 * p + 1)

    pos = lax.broadcasted_iota(jnp.int32, (slots, 256), 0)

    @pl.loop(0, D // 512)
    def _(h):
      for half in range(2):
        cols = pl.ds(pl.multiple_of(h * 512 + half * 256, 256), 256)
        proj = jnp.dot(ctx[...], wo[:, cols], preferred_element_type=F32)
        for i in range(micros):
            mine = slice(i * slots, (i + 1) * slots)
            from_rows = pl.ds(pl.multiple_of(micro_ref[i] * slots, slots), slots)
            base = micro_ref[i] * UTT
            limit = jnp.full((slots, 256), tgt_ref[base], jnp.int32)
            for u in range(1, UTT):
                limit = jnp.where(pos // TGT == u, tgt_ref[base + u], limit)
            both = hidden_ref[from_rows, cols].astype(F32) + proj[mine]
            res[mine, cols] = jnp.where(pos % TGT < limit, both, 0.0).astype(BF)

    outs = []
    for i in range(micros):
        at = pl.ds(pl.multiple_of(micro_ref[i] * slots, slots), slots)
        here = pl.ds(i * slots, slots)
        copy = pltpu.make_async_copy(res.at[here, :], out_hbm.at[at, :], out_sems.at[i])
        copy.start()
        outs.append(copy)
    for copy in outs:
        copy.wait()


def decode(micro, tgt, mems, q, hidden, wk, wv, wo, prev):
    rows = hidden.shape[0]
    micros = 2 * len(mems)
    total = micros * TOT
    slots = UTT * TGT
    aliased = prev is not None
    args = [micro, tgt, *mems, q, hidden, wk, wv, wo] + ([prev] if aliased else [])
    return pl.pallas_call(
        functools.partial(decode_kernel, len(mems), aliased),
        out_shape=jax.ShapeDtypeStruct((rows, D), BF),
        in_specs=[SM, SM] + [VM] * (len(mems) + 5) + [HBM] * aliased,
        out_specs=HBM,
        scratch_shapes=[
            pltpu.VMEM((total, D), BF),
            pltpu.VMEM((total, D), BF),
            pltpu.VMEM((micros * slots, D), BF),
            pltpu.VMEM((micros * slots, D), BF),
            pltpu.VMEM((micros * 8, TOT), F32),
            pltpu.SemaphoreType.DMA((micros,)),
        ],
        input_output_aliases={len(args) - 1: 0} if aliased else {},
        compiler_params=params(7),
        cost_estimate=cost(16 * total * D * D, 8 << 20),
        name="decode",
    )(*args)


def dp_perm(move):
    pairs = []
    for z in range(2):
        for x in range(4):
            for c in range(2):
                nz, nx, nc = move(z, x, c)
                pairs.append(((z * 4 + x) * 2 + c, (nz * 4 + nx % 4) * 2 + nc))
    return pairs


def section_perm(dy, dz):
    return [(y * 4 + z, (y + dy) % 4 * 4 + (z + dz) % 4) for y in range(4) for z in range(4)]


TO_PAIR = dp_perm(lambda z, x, c: (1 - z, x, c))
TO_RIGHT = dp_perm(lambda z, x, c: (z, x + 1, c))
TO_LEFT = dp_perm(lambda z, x, c: (z, x + 3, c))
TO_CORE = dp_perm(lambda z, x, c: (z, x, 1 - c))


def pass_kernel(value_ref, *refs):
    refs[-1][...] = value_ref[...]


def pass_after(value, *others):
    return pl.pallas_call(
        pass_kernel,
        out_shape=jax.ShapeDtypeStruct(value.shape, value.dtype),
        in_specs=[VM] + [HBM] * len(others),
        out_specs=VM,
        compiler_params=params(2),
        cost_estimate=cost(0, 600_000),
        name="pass_after",
    )(value, *others)


def shard_table():
    places = [(0, 0), (1, 0), (0, 3), (0, 1), (1, 3), (1, 1), (0, 2), (1, 2)]
    table = []
    for index in range(16):
        z, x, c = index // 8, index // 2 % 4, index % 2
        table.append(
            [
                ((z + a) % 2 * 4 + (x + b) % 4) * 2 + (c + s) % 2
                for s in (0, 1)
                for a, b in places
            ]
        )
    return table


REL = (0, -1, 1, 2)


def micro_table():
    return [
        [(y + dy) % 4 * 4 + (z + dz) % 4 for dy in REL for dz in REL]
        for y in range(4)
        for z in range(4)
    ]


def body(
    frames,
    frame_lens,
    tgt_lens,
    enc_gain_in,
    w_in,
    depthwise,
    enc_gain_mid,
    w_out,
    dec_gain,
    w_query,
    w_key,
    w_value,
    w_output,
    hidden,
):
    across = lambda v, perm: lax.ppermute(v, "dp", perm)
    along = lambda v, dy, dz: lax.ppermute(v, "section", section_perm(dy, dz))
    where = jnp.array(shard_table(), jnp.int32)[lax.axis_index("dp")]
    micros = jnp.array(micro_table(), jnp.int32)[lax.axis_index("section")].reshape(4, 4)

    own, packed = prepare(
        frame_lens.reshape(UTT), frames.reshape(UTT * FR, D), w_in, w_out
    )
    pair = across(own, TO_PAIR)
    own_r, own_l = across(own, TO_LEFT), across(own, TO_RIGHT)
    source = hidden.reshape(-1, D)
    query = project_query(source, dec_gain, w_query[0])
    pair_l, pair_r = across(pair, TO_RIGHT), across(pair, TO_LEFT)
    own_2, pair_2 = across(own_l, TO_RIGHT), across(pair_r, TO_LEFT)
    ready = pass_after(packed, pair)
    from_b, from_a = along(ready, 0, 1), along(ready, 0, -1)
    shards = [own, pair, own_l, own_r, pair_l, pair_r, own_2, pair_2]
    turn = [pass_after(own, query, from_b, from_a)] + shards[1:]
    shards += [across(v, TO_CORE) for v in turn]
    from_2 = along(pass_after(packed, from_a), 0, 2)

    def encode_pair(first, second):
        return encode(
            where,
            [first, second],
            enc_gain_in.reshape(1, D),
            depthwise,
            enc_gain_mid.reshape(1, D),
            shards,
        )

    mem_a = encode_pair(packed, from_b)
    mem_b = encode_pair(from_a, from_2)

    a_from_l, a_from_r = along(mem_a, 1, 0), along(mem_a, -1, 0)
    b_from_l, b_from_r = along(mem_b, 1, 0), along(mem_b, -1, 0)

    tgt = tgt_lens.reshape(-1)

    def attend(parts, mems, prev):
        micro = jnp.concatenate([micros[y, z : z + 2] for y, z in parts])
        return decode(micro, tgt, mems, query, source, w_key[0], w_value[0], w_output[0], prev)

    a_far, b_far = along(a_from_l, 1, 0), along(b_from_r, -1, 0)
    out = attend([(0, 0), (0, 2)], [mem_a, mem_b], None)
    out = attend([(1, 0), (2, 0)], [a_from_l, a_from_r], out)
    out = attend([(1, 2), (2, 2)], [b_from_l, b_from_r], out)
    out = attend([(3, 0), (3, 2)], [a_far, b_far], out)
    return out.reshape(hidden.shape)


def solution(mesh):
    return jax.shard_map(
        body,
        mesh=mesh,
        in_specs=(
            P("section", "dp", None, None),
            P("section", "dp", None),
            P(None, "dp"),
            P(),
            P("dp", None),
            P(),
            P(),
            P("dp", None),
            P("section", None),
            P("section", None, None),
            P("section", None, None),
            P("section", None, None),
            P("section", None, None),
            P("section", None, "dp", None, None),
        ),
        out_specs=P("section", None, "dp", None, None),
        check_vma=False,
    )
```

```python
import functools

import jax
import jax.numpy as jnp
from jax import lax
from jax.experimental import pallas as pl
from jax.experimental.pallas import tpu as pltpu
from jax.sharding import PartitionSpec as P

HEADS = 16
D = 1024
HEAD = 64
FR = 40
TGT = 8
UTT = 4
TOT = 128
TAPS = 31
HALF = 15
GROUP = 4
EXTRA = 16
BF = jnp.bfloat16
F32 = jnp.float32
HBM = pl.BlockSpec(memory_space=pltpu.HBM)
VM = pl.BlockSpec(memory_space=pltpu.VMEM)
SM = pl.BlockSpec(memory_space=pltpu.SMEM)


def norm_rows(values, gain):
    average = jnp.mean(values, -1, keepdims=True)
    centered = values - average
    spread = jnp.mean(centered * centered, -1, keepdims=True)
    return centered * lax.rsqrt(spread + 1e-05) * gain


def params(limit):
    return pltpu.CompilerParams(vmem_limit_bytes=limit << 20)


def cost(flops, moved):
    return pl.CostEstimate(flops=flops, bytes_accessed=moved, transcendentals=0)


def one_hot(flags):
    return jnp.where(flags, 1.0, 0.0).astype(BF)


def slot_place(slot, lens_ref):
    utt = jnp.zeros_like(slot)
    start = jnp.zeros_like(slot)
    end = jnp.int32(0)
    for u in range(UTT - 1):
        end = end + lens_ref[u]
        later = slot >= end
        utt = jnp.where(later, u + 1, utt)
        start = jnp.where(later, end, start)
    return utt, slot - start


def join_kernel(w_in_hbm, w_out_hbm, own_ref, sems):
    loads = [
        pltpu.make_async_copy(w_in_hbm, own_ref.at[:, pl.ds(0, 2 * D)], sems.at[0]),
        pltpu.make_async_copy(w_out_hbm, own_ref.at[:, pl.ds(2 * D, D)], sems.at[1]),
    ]
    for load in loads:
        load.start()
    for load in loads:
        load.wait()


def join_shards(w_in, w_out):
    return pl.pallas_call(
        join_kernel,
        out_shape=jax.ShapeDtypeStruct((w_in.shape[0], 3 * D), BF),
        in_specs=[HBM, HBM],
        out_specs=VM,
        scratch_shapes=[pltpu.SemaphoreType.DMA((2,))],
        compiler_params=params(60),
        cost_estimate=cost(0, 800_000),
        name="join_shards",
    )(w_in, w_out)


def pack_kernel(lens_ref, frames_ref, own_hbm, out_ref):
    slot = lax.broadcasted_iota(jnp.int32, (TOT, UTT * FR), 0)
    lane = lax.broadcasted_iota(jnp.int32, (TOT, UTT * FR), 1)
    utt, frame = slot_place(slot, lens_ref)
    pick = one_hot(utt * FR + frame == lane)
    utt, frame = slot_place(lax.broadcasted_iota(jnp.int32, (EXTRA, TOT), 1), lens_ref)
    kind = lax.broadcasted_iota(jnp.int32, (EXTRA, TOT), 0)
    out_ref[TOT:, :TOT] = jnp.where(kind == 0, frame, utt).astype(F32).astype(BF)
    out_ref[TOT:, TOT:] = jnp.zeros((EXTRA, D - TOT), BF)
    for j in range(D // 256):
        cols = slice(j * 256, (j + 1) * 256)
        out_ref[:TOT, cols] = jnp.dot(
            pick, frames_ref[:, cols], preferred_element_type=F32
        ).astype(BF)


def pack_frames(lens, frames, after):
    return pl.pallas_call(
        pack_kernel,
        out_shape=jax.ShapeDtypeStruct((TOT + EXTRA, D), BF),
        in_specs=[SM, VM, HBM],
        out_specs=VM,
        compiler_params=params(4),
        cost_estimate=cost(50_000_000, 600_000),
        name="pack_frames",
    )(lens, frames, after)


def query_kernel(hidden_ref, gain_ref, w_ref, after_hbm, out_ref, normed):
    @pl.loop(0, hidden_ref.shape[0] // 64)
    def _(i):
        for r in range(0, 64, 16):
            rows = pl.ds(pl.multiple_of(i * 64 + r, 16), 16)
            normed[rows, :] = norm_rows(hidden_ref[rows, :].astype(F32), gain_ref[...]).astype(BF)

    for j in range(D // 256):
        cols = slice(j * 256, (j + 1) * 256)
        q = jnp.dot(normed[...], w_ref[:, cols], preferred_element_type=F32)
        out_ref[:, cols] = (q * (HEAD**-0.5)).astype(BF)


def project_query(hidden, gain, w, after):
    rows = hidden.shape[0]
    return pl.pallas_call(
        query_kernel,
        out_shape=jax.ShapeDtypeStruct((rows, D), BF),
        in_specs=[VM, VM, VM, HBM],
        out_specs=VM,
        scratch_shapes=[pltpu.VMEM((rows, D), BF)],
        compiler_params=params(8),
        cost_estimate=cost(2 * rows * D * D, 4 << 20),
        name="project_query",
    )(hidden, gain, w, after)


def order_columns(dst, src, where_ref):
    odd = jnp.broadcast_to(where_ref[0] % 2 == 1, (src.shape[0], 128))
    for i in range(D // 128):
        at = pl.multiple_of(where_ref[i] // 2 * 128, 128)
        block = src[:, pl.ds(at, 128)].astype(F32)
        block = jnp.where(odd, pltpu.roll(block, HEAD, 1), block)
        dst[:, i * 128 : (i + 1) * 128] = block.astype(BF)


def shard_rows(w_refs, k, cols):
    own, other = w_refs
    picks = [own[2 * k], other[2 * k], own[2 * k + 1], other[2 * k + 1]]
    return jnp.concatenate([ref[row : row + 64, cols] for ref, row in picks], axis=0)


def dot_shards(lhs, w_refs, cols):
    total = None
    for k in range(D // 256):
        term = jnp.dot(
            lhs[:, k * 256 : (k + 1) * 256],
            shard_rows(w_refs, k, cols),
            preferred_element_type=F32,
        )
        total = term if total is None else total + term
    return total


def encode_kernel(n_w, where_ref, *refs):
    x_refs = refs[:2]
    gain_in_ref, dw_ref, gain_mid_ref = refs[2:5]
    blocks = []
    for ref in refs[5 : 5 + n_w]:
        blocks += [(ref, row) for row in range(0, ref.shape[0], 64)]
    w_refs = blocks[: len(blocks) // 2], blocks[len(blocks) // 2 :]
    out_ref, plain, normed, spread, conv, taps, act = refs[5 + n_w :]
    step = 16
    for i, x in enumerate(x_refs):
        for r in range(0, TOT, step):
            plain[i * TOT + r : i * TOT + r + step, :] = norm_rows(
                x[r : r + step, :].astype(F32), gain_in_ref[...]
            ).astype(BF)
    order_columns(normed, plain, where_ref)
    taps[...] = dw_ref[...].astype(F32)
    rows = normed.shape[0]
    frame_rows = conv.shape[0]
    lanes = 2 * UTT
    target = []
    for i, x in enumerate(x_refs):
        places = x[TOT : TOT + EXTRA, :TOT].astype(F32)
        target.append(places[0:1] * lanes + places[1:2] + i * UTT)
    target = jnp.concatenate(target, axis=1)
    spot = lax.broadcasted_iota(jnp.int32, (frame_rows, rows), 0)
    expand = one_hot(target.astype(jnp.int32) == spot)
    column = jnp.broadcast_to(target, (8, rows)).T[:, 0:1].astype(jnp.int32)
    shrink = one_hot(column == lax.broadcasted_iota(jnp.int32, (rows, frame_rows), 1))
    for j in range(D // 256):
        value = dot_shards(normed, w_refs, slice(j * 256, (j + 1) * 256))
        gate = dot_shards(normed, w_refs, slice(D + j * 256, D + (j + 1) * 256))
        gated = (value * jax.nn.sigmoid(gate)).astype(BF)
        spread[:, j * 256 : (j + 1) * 256] = jnp.dot(expand, gated, preferred_element_type=F32)
    block = 8

    @pl.loop(0, D // 128)
    def _(c):
        cols = pl.ds(pl.multiple_of(c * 128, 128), 128)
        weights = [jnp.broadcast_to(taps[k : k + 1, cols], (lanes, 128)) for k in range(TAPS)]
        for first in range(0, FR, block):
            sums = [None] * block
            for f in range(max(0, first - HALF), min(FR, first + block + HALF)):
                here = spread[f * lanes : (f + 1) * lanes, cols]
                for b in range(block):
                    k = f - (first + b) + HALF
                    if 0 <= k < TAPS:
                        term = here * weights[k]
                        sums[b] = term if sums[b] is None else sums[b] + term
            for b in range(block):
                at = (first + b) * lanes
                conv[at : at + lanes, cols] = sums[b]

    for r in range(0, frame_rows, step):
        v = norm_rows(conv[r : r + step, :], gain_mid_ref[...])
        act[r : r + step, :] = (v * jax.nn.sigmoid(v)).astype(BF)
    for j in range(D // 256):
        cols = slice(j * 256, (j + 1) * 256)
        plain[:, cols] = jnp.dot(shrink, act[:, cols], preferred_element_type=F32).astype(BF)
    order_columns(normed, plain, where_ref)
    for j in range(D // 256):
        cols = slice(j * 256, (j + 1) * 256)
        low = dot_shards(normed, w_refs, slice(2 * D + j * 256, 2 * D + (j + 1) * 256))
        for i, x in enumerate(x_refs):
            at = slice(i * TOT, (i + 1) * TOT)
            out_ref[at, cols] = (x[:TOT, cols].astype(F32) + low[at]).astype(BF)
    utts = [x[TOT : TOT + EXTRA, :TOT].astype(F32)[1:2] for x in x_refs]
    kind = lax.broadcasted_iota(jnp.int32, (EXTRA, TOT), 0)
    out_ref[rows:, :TOT] = jnp.where(kind == 0, utts[0], utts[1]).astype(BF)
    out_ref[rows:, TOT:] = jnp.zeros((EXTRA, D - TOT), BF)


def encode(where, xs, gain_in, dw, gain_mid, shards):
    rows = 2 * TOT
    frame_rows = 2 * UTT * FR
    return pl.pallas_call(
        functools.partial(encode_kernel, len(shards)),
        out_shape=jax.ShapeDtypeStruct((rows + EXTRA, D), BF),
        in_specs=[SM] + [VM] * (5 + len(shards)),
        out_specs=VM,
        scratch_shapes=[
            pltpu.VMEM((rows, D), BF),
            pltpu.VMEM((rows, D), BF),
            pltpu.VMEM((frame_rows, D), F32),
            pltpu.VMEM((frame_rows, D), F32),
            pltpu.VMEM((TAPS, D), F32),
            pltpu.VMEM((frame_rows, D), BF),
        ],
        compiler_params=params(9),
        cost_estimate=cost(8_000_000_000, 8 << 20),
        name="encode",
    )(where, *xs, gain_in, dw, gain_mid, *shards)


def decode_kernel(n_mem, aliased, micro_ref, tgt_ref, *refs):
    mem_refs = refs[:n_mem]
    q_ref, hidden_ref, wk, wv, wo = refs[n_mem : n_mem + 5]
    rest = refs[n_mem + 5 + (1 if aliased else 0) :]
    out_hbm, keys, values, ctx, res, seg, out_sems = rest
    slots = UTT * TGT
    micros = 2 * n_mem
    for w, out in ((wk, keys), (wv, values)):
        for p, mem in enumerate(mem_refs):
            for j in range(D // 256):
                cols = slice(j * 256, (j + 1) * 256)
                out[p * 2 * TOT : (p + 1) * 2 * TOT, cols] = jnp.dot(
                    mem[: 2 * TOT, :], w[:, cols], preferred_element_type=F32
                ).astype(BF)
    width = GROUP * HEAD
    tall = GROUP * slots
    row = lax.broadcasted_iota(jnp.int32, (tall, width), 0)
    lane = lax.broadcasted_iota(jnp.int32, (tall, width), 1)
    own = (row // slots) == (lane // HEAD)
    own_bf = one_hot(own)
    utt_of_row = (lax.broadcasted_iota(jnp.int32, (tall, TOT), 0) // TGT) % UTT
    groups = HEADS // GROUP
    for i in range(micros):
        utts = mem_refs[i // 2][2 * TOT : 2 * TOT + EXTRA, :TOT].astype(F32)
        seg[i * 8 : i * 8 + 8, :] = jnp.broadcast_to(utts[i % 2 : i % 2 + 1], (8, TOT))

    def attend(i):
        line = seg[pl.ds(pl.multiple_of(i * 8, 8), 8), :]
        allowed = utt_of_row == line[0:1].astype(jnp.int32)
        at = pl.ds(pl.multiple_of(i * TOT, TOT), TOT)
        mine = pl.ds(pl.multiple_of(i * slots, slots), slots)
        from_rows = pl.ds(pl.multiple_of(micro_ref[i] * slots, slots), slots)
        cuts = [slice(j * width, (j + 1) * width) for j in range(groups)]
        scores = []
        for cols in cuts:
            q = q_ref[from_rows, cols]
            q = jnp.concatenate([q] * GROUP, axis=0) * own_bf
            scores.append(
                lax.dot_general(
                    q, keys[at, cols], (((1,), (1,)), ((), ())), preferred_element_type=F32
                )
            )
        probs = []
        for s in scores:
            s = jnp.where(allowed, s, -1e30)
            expo = jnp.exp(s - jnp.max(s, -1, keepdims=True))
            probs.append((expo * (1.0 / jnp.sum(expo, -1, keepdims=True))).astype(BF))
        for prob, cols in zip(probs, cuts):
            mixed = jnp.dot(prob, values[at, cols], preferred_element_type=F32)
            mixed = jnp.where(own, mixed, 0.0)
            total = mixed[:slots]
            for g in range(1, GROUP):
                total = total + mixed[g * slots : (g + 1) * slots]
            ctx[mine, cols] = total.astype(BF)

    @pl.loop(0, micros // 2)
    def _(p):
        attend(2 * p)
        attend(2 * p + 1)

    pos = lax.broadcasted_iota(jnp.int32, (slots, 256), 0)

    @pl.loop(0, D // 512)
    def _(h):
      for half in range(2):
        cols = pl.ds(pl.multiple_of(h * 512 + half * 256, 256), 256)
        proj = jnp.dot(ctx[...], wo[:, cols], preferred_element_type=F32)
        for i in range(micros):
            mine = slice(i * slots, (i + 1) * slots)
            from_rows = pl.ds(pl.multiple_of(micro_ref[i] * slots, slots), slots)
            base = micro_ref[i] * UTT
            limit = jnp.full((slots, 256), tgt_ref[base], jnp.int32)
            for u in range(1, UTT):
                limit = jnp.where(pos // TGT == u, tgt_ref[base + u], limit)
            both = hidden_ref[from_rows, cols].astype(F32) + proj[mine]
            res[mine, cols] = jnp.where(pos % TGT < limit, both, 0.0).astype(BF)

    outs = []
    for i in range(micros):
        at = pl.ds(pl.multiple_of(micro_ref[i] * slots, slots), slots)
        here = pl.ds(i * slots, slots)
        copy = pltpu.make_async_copy(res.at[here, :], out_hbm.at[at, :], out_sems.at[i])
        copy.start()
        outs.append(copy)
    for copy in outs:
        copy.wait()


def decode(micro, tgt, mems, q, hidden, wk, wv, wo, prev):
    rows = hidden.shape[0]
    micros = 2 * len(mems)
    total = micros * TOT
    slots = UTT * TGT
    aliased = prev is not None
    args = [micro, tgt, *mems, q, hidden, wk, wv, wo] + ([prev] if aliased else [])
    return pl.pallas_call(
        functools.partial(decode_kernel, len(mems), aliased),
        out_shape=jax.ShapeDtypeStruct((rows, D), BF),
        in_specs=[SM, SM] + [VM] * (len(mems) + 5) + [HBM] * aliased,
        out_specs=HBM,
        scratch_shapes=[
            pltpu.VMEM((total, D), BF),
            pltpu.VMEM((total, D), BF),
            pltpu.VMEM((micros * slots, D), BF),
            pltpu.VMEM((micros * slots, D), BF),
            pltpu.VMEM((micros * 8, TOT), F32),
            pltpu.SemaphoreType.DMA((micros,)),
        ],
        input_output_aliases={len(args) - 1: 0} if aliased else {},
        compiler_params=params(7),
        cost_estimate=cost(16 * total * D * D, 8 << 20),
        name="decode",
    )(*args)


def dp_perm(move):
    pairs = []
    for z in range(2):
        for x in range(4):
            for c in range(2):
                nz, nx, nc = move(z, x, c)
                pairs.append(((z * 4 + x) * 2 + c, (nz * 4 + nx % 4) * 2 + nc))
    return pairs


def section_perm(dy, dz):
    return [(y * 4 + z, (y + dy) % 4 * 4 + (z + dz) % 4) for y in range(4) for z in range(4)]


TO_PAIR = dp_perm(lambda z, x, c: (1 - z, x, c))
TO_RIGHT = dp_perm(lambda z, x, c: (z, x + 1, c))
TO_LEFT = dp_perm(lambda z, x, c: (z, x + 3, c))
TO_CORE = dp_perm(lambda z, x, c: (z, x, 1 - c))


def pass_kernel(value_ref, *refs):
    refs[-1][...] = value_ref[...]


def pass_after(value, *others):
    return pl.pallas_call(
        pass_kernel,
        out_shape=jax.ShapeDtypeStruct(value.shape, value.dtype),
        in_specs=[VM] + [HBM] * len(others),
        out_specs=VM,
        compiler_params=params(2),
        cost_estimate=cost(0, 600_000),
        name="pass_after",
    )(value, *others)


def shard_table():
    places = [(0, 0), (1, 0), (0, 3), (0, 1), (1, 3), (1, 1), (0, 2), (1, 2)]
    table = []
    for index in range(16):
        z, x, c = index // 8, index // 2 % 4, index % 2
        table.append(
            [
                ((z + a) % 2 * 4 + (x + b) % 4) * 2 + (c + s) % 2
                for s in (0, 1)
                for a, b in places
            ]
        )
    return table


REL = (0, -1, 1, 2)


def micro_table():
    return [
        [(y + dy) % 4 * 4 + (z + dz) % 4 for dy in REL for dz in REL]
        for y in range(4)
        for z in range(4)
    ]


def body(
    frames,
    frame_lens,
    tgt_lens,
    enc_gain_in,
    w_in,
    depthwise,
    enc_gain_mid,
    w_out,
    dec_gain,
    w_query,
    w_key,
    w_value,
    w_output,
    hidden,
):
    across = lambda v, perm: lax.ppermute(v, "dp", perm)
    along = lambda v, dy, dz: lax.ppermute(v, "section", section_perm(dy, dz))
    where = jnp.array(shard_table(), jnp.int32)[lax.axis_index("dp")]
    micros = jnp.array(micro_table(), jnp.int32)[lax.axis_index("section")].reshape(4, 4)

    own = join_shards(w_in, w_out)
    pair = across(own, TO_PAIR)
    own_l, own_r = across(own, TO_RIGHT), across(own, TO_LEFT)
    pair_l, pair_r = across(pair, TO_RIGHT), across(pair, TO_LEFT)
    own_2, pair_2 = across(own_l, TO_RIGHT), across(pair_r, TO_LEFT)
    shards = [own, pair, own_l, own_r, pair_l, pair_r, own_2, pair_2]

    packed = pack_frames(frame_lens.reshape(UTT), frames.reshape(UTT * FR, D), pair)
    from_b, from_a = along(packed, 0, 1), along(packed, 0, -1)
    source = hidden.reshape(-1, D)
    turn = list(shards)
    turn[1] = pass_after(turn[1], from_b, from_a)
    from_2 = along(pass_after(packed, from_a), 0, 2)
    shards += [across(v, TO_CORE) for v in turn]

    def encode_pair(first, second):
        return encode(
            where,
            [first, second],
            enc_gain_in.reshape(1, D),
            depthwise,
            enc_gain_mid.reshape(1, D),
            shards,
        )

    mem_a = encode_pair(packed, from_b)
    query = project_query(source, dec_gain, w_query[0], mem_a)
    mem_b = encode_pair(from_a, from_2)

    a_from_l, a_from_r = along(mem_a, 1, 0), along(mem_a, -1, 0)
    b_from_l, b_from_r = along(mem_b, 1, 0), along(mem_b, -1, 0)

    tgt = tgt_lens.reshape(-1)

    def attend(parts, mems, prev):
        micro = jnp.concatenate([micros[y, z : z + 2] for y, z in parts])
        return decode(micro, tgt, mems, query, source, w_key[0], w_value[0], w_output[0], prev)

    a_far, b_far = along(a_from_l, 1, 0), along(b_from_r, -1, 0)
    out = attend([(0, 0), (0, 2)], [mem_a, mem_b], None)
    out = attend([(1, 0), (2, 0)], [a_from_l, a_from_r], out)
    out = attend([(1, 2), (2, 2)], [b_from_l, b_from_r], out)
    out = attend([(3, 0), (3, 2)], [a_far, b_far], out)
    return out.reshape(hidden.shape)


def solution(mesh):
    return jax.shard_map(
        body,
        mesh=mesh,
        in_specs=(
            P("section", "dp", None, None),
            P("section", "dp", None),
            P(None, "dp"),
            P(),
            P("dp", None),
            P(),
            P(),
            P("dp", None),
            P("section", None),
            P("section", None, None),
            P("section", None, None),
            P("section", None, None),
            P("section", None, None),
            P("section", None, "dp", None, None),
        ),
        out_specs=P("section", None, "dp", None, None),
        check_vma=False,
    )
```

```python
import functools

import jax
import jax.numpy as jnp
from jax import lax
from jax.experimental import pallas as pl
from jax.experimental.pallas import tpu as pltpu
from jax.sharding import PartitionSpec as P

HEADS = 16
D = 1024
HEAD = 64
FR = 40
TGT = 8
UTT = 4
TOT = 128
TAPS = 31
HALF = 15
GROUP = 4
EXTRA = 16
BF = jnp.bfloat16
F32 = jnp.float32
HBM = pl.BlockSpec(memory_space=pltpu.HBM)
VM = pl.BlockSpec(memory_space=pltpu.VMEM)
SM = pl.BlockSpec(memory_space=pltpu.SMEM)


def norm_rows(values, gain):
    average = jnp.mean(values, -1, keepdims=True)
    centered = values - average
    spread = jnp.mean(centered * centered, -1, keepdims=True)
    return centered * lax.rsqrt(spread + 1e-05) * gain


def params(limit):
    return pltpu.CompilerParams(vmem_limit_bytes=limit << 20)


def cost(flops, moved):
    return pl.CostEstimate(flops=flops, bytes_accessed=moved, transcendentals=0)


def one_hot(flags):
    return jnp.where(flags, 1.0, 0.0).astype(BF)


def slot_place(slot, lens_ref):
    utt = jnp.zeros_like(slot)
    start = jnp.zeros_like(slot)
    end = jnp.int32(0)
    for u in range(UTT - 1):
        end = end + lens_ref[u]
        later = slot >= end
        utt = jnp.where(later, u + 1, utt)
        start = jnp.where(later, end, start)
    return utt, slot - start


def join_kernel(w_in_hbm, w_out_hbm, own_ref, sems):
    loads = [
        pltpu.make_async_copy(w_in_hbm, own_ref.at[:, pl.ds(0, 2 * D)], sems.at[0]),
        pltpu.make_async_copy(w_out_hbm, own_ref.at[:, pl.ds(2 * D, D)], sems.at[1]),
    ]
    for load in loads:
        load.start()
    for load in loads:
        load.wait()


def join_shards(w_in, w_out):
    return pl.pallas_call(
        join_kernel,
        out_shape=jax.ShapeDtypeStruct((w_in.shape[0], 3 * D), BF),
        in_specs=[HBM, HBM],
        out_specs=VM,
        scratch_shapes=[pltpu.SemaphoreType.DMA((2,))],
        compiler_params=params(60),
        cost_estimate=cost(0, 800_000),
        name="join_shards",
    )(w_in, w_out)


def pack_kernel(lens_ref, frames_ref, own_hbm, out_ref):
    slot = lax.broadcasted_iota(jnp.int32, (TOT, UTT * FR), 0)
    lane = lax.broadcasted_iota(jnp.int32, (TOT, UTT * FR), 1)
    utt, frame = slot_place(slot, lens_ref)
    pick = one_hot(utt * FR + frame == lane)
    utt, frame = slot_place(lax.broadcasted_iota(jnp.int32, (EXTRA, TOT), 1), lens_ref)
    kind = lax.broadcasted_iota(jnp.int32, (EXTRA, TOT), 0)
    out_ref[TOT:, :TOT] = jnp.where(kind == 0, frame, utt).astype(F32).astype(BF)
    out_ref[TOT:, TOT:] = jnp.zeros((EXTRA, D - TOT), BF)
    for j in range(D // 256):
        cols = slice(j * 256, (j + 1) * 256)
        out_ref[:TOT, cols] = jnp.dot(
            pick, frames_ref[:, cols], preferred_element_type=F32
        ).astype(BF)


def pack_frames(lens, frames, after):
    return pl.pallas_call(
        pack_kernel,
        out_shape=jax.ShapeDtypeStruct((TOT + EXTRA, D), BF),
        in_specs=[SM, VM, HBM],
        out_specs=VM,
        compiler_params=params(4),
        cost_estimate=cost(50_000_000, 600_000),
        name="pack_frames",
    )(lens, frames, after)


def query_kernel(hidden_ref, gain_ref, w_ref, after_hbm, out_ref, normed):
    @pl.loop(0, hidden_ref.shape[0] // 32)
    def _(i):
        for r in range(0, 32, 16):
            rows = pl.ds(pl.multiple_of(i * 32 + r, 16), 16)
            normed[rows, :] = norm_rows(hidden_ref[rows, :].astype(F32), gain_ref[...]).astype(BF)

    for j in range(D // 256):
        cols = slice(j * 256, (j + 1) * 256)
        q = jnp.dot(normed[...], w_ref[:, cols], preferred_element_type=F32)
        out_ref[:, cols] = (q * (HEAD**-0.5)).astype(BF)


def project_query(hidden, gain, w, after):
    rows = hidden.shape[0]
    return pl.pallas_call(
        query_kernel,
        out_shape=jax.ShapeDtypeStruct((rows, D), BF),
        in_specs=[VM, VM, VM, HBM],
        out_specs=VM,
        scratch_shapes=[pltpu.VMEM((rows, D), BF)],
        compiler_params=params(8),
        cost_estimate=cost(2 * rows * D * D, 4 << 20),
        name="project_query",
    )(hidden, gain, w, after)


def order_columns(dst, src, where_ref):
    odd = jnp.broadcast_to(where_ref[0] % 2 == 1, (src.shape[0], 128))
    for i in range(D // 128):
        at = pl.multiple_of(where_ref[i] // 2 * 128, 128)
        block = src[:, pl.ds(at, 128)].astype(F32)
        block = jnp.where(odd, pltpu.roll(block, HEAD, 1), block)
        dst[:, i * 128 : (i + 1) * 128] = block.astype(BF)


def shard_rows(w_refs, k, cols):
    own, other = w_refs
    picks = [own[2 * k], other[2 * k], own[2 * k + 1], other[2 * k + 1]]
    return jnp.concatenate([ref[row : row + 64, cols] for ref, row in picks], axis=0)


def dot_shards(lhs, w_refs, cols):
    total = None
    for k in range(D // 256):
        term = jnp.dot(
            lhs[:, k * 256 : (k + 1) * 256],
            shard_rows(w_refs, k, cols),
            preferred_element_type=F32,
        )
        total = term if total is None else total + term
    return total


def encode_kernel(n_w, where_ref, *refs):
    x_refs = refs[:2]
    gain_in_ref, dw_ref, gain_mid_ref = refs[2:5]
    blocks = []
    for ref in refs[5 : 5 + n_w]:
        blocks += [(ref, row) for row in range(0, ref.shape[0], 64)]
    w_refs = blocks[: len(blocks) // 2], blocks[len(blocks) // 2 :]
    out_ref, plain, normed, spread, conv, taps, act = refs[5 + n_w :]
    step = 16
    for i, x in enumerate(x_refs):
        for r in range(0, TOT, step):
            plain[i * TOT + r : i * TOT + r + step, :] = norm_rows(
                x[r : r + step, :].astype(F32), gain_in_ref[...]
            ).astype(BF)
    order_columns(normed, plain, where_ref)
    taps[...] = dw_ref[...].astype(F32)
    rows = normed.shape[0]
    frame_rows = conv.shape[0]
    lanes = 2 * UTT
    target = []
    for i, x in enumerate(x_refs):
        places = x[TOT : TOT + EXTRA, :TOT].astype(F32)
        target.append(places[0:1] * lanes + places[1:2] + i * UTT)
    target = jnp.concatenate(target, axis=1)
    spot = lax.broadcasted_iota(jnp.int32, (frame_rows, rows), 0)
    expand = one_hot(target.astype(jnp.int32) == spot)
    column = jnp.broadcast_to(target, (8, rows)).T[:, 0:1].astype(jnp.int32)
    shrink = one_hot(column == lax.broadcasted_iota(jnp.int32, (rows, frame_rows), 1))
    for j in range(D // 256):
        value = dot_shards(normed, w_refs, slice(j * 256, (j + 1) * 256))
        gate = dot_shards(normed, w_refs, slice(D + j * 256, D + (j + 1) * 256))
        gated = (value * jax.nn.sigmoid(gate)).astype(BF)
        spread[:, j * 256 : (j + 1) * 256] = jnp.dot(expand, gated, preferred_element_type=F32)
    block = 8

    @pl.loop(0, D // 128)
    def _(c):
        cols = pl.ds(pl.multiple_of(c * 128, 128), 128)
        weights = [jnp.broadcast_to(taps[k : k + 1, cols], (lanes, 128)) for k in range(TAPS)]
        for first in range(0, FR, block):
            sums = [None] * block
            for f in range(max(0, first - HALF), min(FR, first + block + HALF)):
                here = spread[f * lanes : (f + 1) * lanes, cols]
                for b in range(block):
                    k = f - (first + b) + HALF
                    if 0 <= k < TAPS:
                        term = here * weights[k]
                        sums[b] = term if sums[b] is None else sums[b] + term
            for b in range(block):
                at = (first + b) * lanes
                conv[at : at + lanes, cols] = sums[b]

    for r in range(0, frame_rows, step):
        v = norm_rows(conv[r : r + step, :], gain_mid_ref[...])
        act[r : r + step, :] = (v * jax.nn.sigmoid(v)).astype(BF)
    for j in range(D // 256):
        cols = slice(j * 256, (j + 1) * 256)
        plain[:, cols] = jnp.dot(shrink, act[:, cols], preferred_element_type=F32).astype(BF)
    order_columns(normed, plain, where_ref)
    for j in range(D // 256):
        cols = slice(j * 256, (j + 1) * 256)
        low = dot_shards(normed, w_refs, slice(2 * D + j * 256, 2 * D + (j + 1) * 256))
        for i, x in enumerate(x_refs):
            at = slice(i * TOT, (i + 1) * TOT)
            out_ref[at, cols] = (x[:TOT, cols].astype(F32) + low[at]).astype(BF)
    utts = [x[TOT : TOT + EXTRA, :TOT].astype(F32)[1:2] for x in x_refs]
    kind = lax.broadcasted_iota(jnp.int32, (EXTRA, TOT), 0)
    out_ref[rows:, :TOT] = jnp.where(kind == 0, utts[0], utts[1]).astype(BF)
    out_ref[rows:, TOT:] = jnp.zeros((EXTRA, D - TOT), BF)


def encode(where, xs, gain_in, dw, gain_mid, shards):
    rows = 2 * TOT
    frame_rows = 2 * UTT * FR
    return pl.pallas_call(
        functools.partial(encode_kernel, len(shards)),
        out_shape=jax.ShapeDtypeStruct((rows + EXTRA, D), BF),
        in_specs=[SM] + [VM] * (5 + len(shards)),
        out_specs=VM,
        scratch_shapes=[
            pltpu.VMEM((rows, D), BF),
            pltpu.VMEM((rows, D), BF),
            pltpu.VMEM((frame_rows, D), F32),
            pltpu.VMEM((frame_rows, D), F32),
            pltpu.VMEM((TAPS, D), F32),
            pltpu.VMEM((frame_rows, D), BF),
        ],
        compiler_params=params(9),
        cost_estimate=cost(8_000_000_000, 8 << 20),
        name="encode",
    )(where, *xs, gain_in, dw, gain_mid, *shards)


def decode_kernel(n_mem, aliased, micro_ref, tgt_ref, *refs):
    mem_refs = refs[:n_mem]
    q_ref, hidden_ref, wk, wv, wo = refs[n_mem : n_mem + 5]
    rest = refs[n_mem + 5 + (1 if aliased else 0) :]
    out_hbm, keys, values, ctx, res, seg, out_sems = rest
    slots = UTT * TGT
    micros = 2 * n_mem
    for w, out in ((wk, keys), (wv, values)):
        for p, mem in enumerate(mem_refs):
            for j in range(D // 256):
                cols = slice(j * 256, (j + 1) * 256)
                out[p * 2 * TOT : (p + 1) * 2 * TOT, cols] = jnp.dot(
                    mem[: 2 * TOT, :], w[:, cols], preferred_element_type=F32
                ).astype(BF)
    width = GROUP * HEAD
    tall = GROUP * slots
    row = lax.broadcasted_iota(jnp.int32, (tall, width), 0)
    lane = lax.broadcasted_iota(jnp.int32, (tall, width), 1)
    own = (row // slots) == (lane // HEAD)
    own_bf = one_hot(own)
    utt_of_row = (lax.broadcasted_iota(jnp.int32, (tall, TOT), 0) // TGT) % UTT
    groups = HEADS // GROUP
    for i in range(micros):
        utts = mem_refs[i // 2][2 * TOT : 2 * TOT + EXTRA, :TOT].astype(F32)
        seg[i * 8 : i * 8 + 8, :] = jnp.broadcast_to(utts[i % 2 : i % 2 + 1], (8, TOT))

    def attend(i):
        line = seg[pl.ds(pl.multiple_of(i * 8, 8), 8), :]
        allowed = utt_of_row == line[0:1].astype(jnp.int32)
        at = pl.ds(pl.multiple_of(i * TOT, TOT), TOT)
        mine = pl.ds(pl.multiple_of(i * slots, slots), slots)
        from_rows = pl.ds(pl.multiple_of(micro_ref[i] * slots, slots), slots)
        cuts = [slice(j * width, (j + 1) * width) for j in range(groups)]
        scores = []
        for cols in cuts:
            q = q_ref[from_rows, cols]
            q = jnp.concatenate([q] * GROUP, axis=0) * own_bf
            scores.append(
                lax.dot_general(
                    q, keys[at, cols], (((1,), (1,)), ((), ())), preferred_element_type=F32
                )
            )
        probs = []
        for s in scores:
            s = jnp.where(allowed, s, -1e30)
            expo = jnp.exp(s - jnp.max(s, -1, keepdims=True))
            probs.append((expo * (1.0 / jnp.sum(expo, -1, keepdims=True))).astype(BF))
        for prob, cols in zip(probs, cuts):
            mixed = jnp.dot(prob, values[at, cols], preferred_element_type=F32)
            mixed = jnp.where(own, mixed, 0.0)
            total = mixed[:slots]
            for g in range(1, GROUP):
                total = total + mixed[g * slots : (g + 1) * slots]
            ctx[mine, cols] = total.astype(BF)

    @pl.loop(0, micros // 2)
    def _(p):
        attend(2 * p)
        attend(2 * p + 1)

    pos = lax.broadcasted_iota(jnp.int32, (slots, 256), 0)

    @pl.loop(0, D // 512)
    def _(h):
      for half in range(2):
        cols = pl.ds(pl.multiple_of(h * 512 + half * 256, 256), 256)
        proj = jnp.dot(ctx[...], wo[:, cols], preferred_element_type=F32)
        for i in range(micros):
            mine = slice(i * slots, (i + 1) * slots)
            from_rows = pl.ds(pl.multiple_of(micro_ref[i] * slots, slots), slots)
            base = micro_ref[i] * UTT
            limit = jnp.full((slots, 256), tgt_ref[base], jnp.int32)
            for u in range(1, UTT):
                limit = jnp.where(pos // TGT == u, tgt_ref[base + u], limit)
            both = hidden_ref[from_rows, cols].astype(F32) + proj[mine]
            res[mine, cols] = jnp.where(pos % TGT < limit, both, 0.0).astype(BF)

    outs = []
    for i in range(micros):
        at = pl.ds(pl.multiple_of(micro_ref[i] * slots, slots), slots)
        here = pl.ds(i * slots, slots)
        copy = pltpu.make_async_copy(res.at[here, :], out_hbm.at[at, :], out_sems.at[i])
        copy.start()
        outs.append(copy)
    for copy in outs:
        copy.wait()


def decode(micro, tgt, mems, q, hidden, wk, wv, wo, prev):
    rows = hidden.shape[0]
    micros = 2 * len(mems)
    total = micros * TOT
    slots = UTT * TGT
    aliased = prev is not None
    args = [micro, tgt, *mems, q, hidden, wk, wv, wo] + ([prev] if aliased else [])
    return pl.pallas_call(
        functools.partial(decode_kernel, len(mems), aliased),
        out_shape=jax.ShapeDtypeStruct((rows, D), BF),
        in_specs=[SM, SM] + [VM] * (len(mems) + 5) + [HBM] * aliased,
        out_specs=HBM,
        scratch_shapes=[
            pltpu.VMEM((total, D), BF),
            pltpu.VMEM((total, D), BF),
            pltpu.VMEM((micros * slots, D), BF),
            pltpu.VMEM((micros * slots, D), BF),
            pltpu.VMEM((micros * 8, TOT), F32),
            pltpu.SemaphoreType.DMA((micros,)),
        ],
        input_output_aliases={len(args) - 1: 0} if aliased else {},
        compiler_params=params(7),
        cost_estimate=cost(16 * total * D * D, 8 << 20),
        name="decode",
    )(*args)


def dp_perm(move):
    pairs = []
    for z in range(2):
        for x in range(4):
            for c in range(2):
                nz, nx, nc = move(z, x, c)
                pairs.append(((z * 4 + x) * 2 + c, (nz * 4 + nx % 4) * 2 + nc))
    return pairs


def section_perm(dy, dz):
    return [(y * 4 + z, (y + dy) % 4 * 4 + (z + dz) % 4) for y in range(4) for z in range(4)]


TO_PAIR = dp_perm(lambda z, x, c: (1 - z, x, c))
TO_RIGHT = dp_perm(lambda z, x, c: (z, x + 1, c))
TO_LEFT = dp_perm(lambda z, x, c: (z, x + 3, c))
TO_CORE = dp_perm(lambda z, x, c: (z, x, 1 - c))


def pass_kernel(value_ref, *refs):
    refs[-1][...] = value_ref[...]


def pass_after(value, *others):
    return pl.pallas_call(
        pass_kernel,
        out_shape=jax.ShapeDtypeStruct(value.shape, value.dtype),
        in_specs=[VM] + [HBM] * len(others),
        out_specs=VM,
        compiler_params=params(2),
        cost_estimate=cost(0, 600_000),
        name="pass_after",
    )(value, *others)


def shard_table():
    places = [(0, 0), (1, 0), (0, 3), (0, 1), (1, 3), (1, 1), (0, 2), (1, 2)]
    table = []
    for index in range(16):
        z, x, c = index // 8, index // 2 % 4, index % 2
        table.append(
            [
                ((z + a) % 2 * 4 + (x + b) % 4) * 2 + (c + s) % 2
                for s in (0, 1)
                for a, b in places
            ]
        )
    return table


REL = (0, -1, 1, 2)


def micro_table():
    return [
        [(y + dy) % 4 * 4 + (z + dz) % 4 for dy in REL for dz in REL]
        for y in range(4)
        for z in range(4)
    ]


def body(
    frames,
    frame_lens,
    tgt_lens,
    enc_gain_in,
    w_in,
    depthwise,
    enc_gain_mid,
    w_out,
    dec_gain,
    w_query,
    w_key,
    w_value,
    w_output,
    hidden,
):
    across = lambda v, perm: lax.ppermute(v, "dp", perm)
    along = lambda v, dy, dz: lax.ppermute(v, "section", section_perm(dy, dz))
    where = jnp.array(shard_table(), jnp.int32)[lax.axis_index("dp")]
    micros = jnp.array(micro_table(), jnp.int32)[lax.axis_index("section")].reshape(4, 4)

    own = join_shards(w_in, w_out)
    pair = across(own, TO_PAIR)
    own_l, own_r = across(own, TO_RIGHT), across(own, TO_LEFT)
    pair_l, pair_r = across(pair, TO_RIGHT), across(pair, TO_LEFT)
    own_2, pair_2 = across(own_l, TO_RIGHT), across(pair_r, TO_LEFT)
    shards = [own, pair, own_l, own_r, pair_l, pair_r, own_2, pair_2]

    packed = pack_frames(frame_lens.reshape(UTT), frames.reshape(UTT * FR, D), pair)
    from_b, from_a = along(packed, 0, 1), along(packed, 0, -1)
    source = hidden.reshape(-1, D)
    turn = list(shards)
    turn[1] = pass_after(turn[1], from_b, from_a)
    from_2 = along(from_b, 0, 1)
    shards += [across(v, TO_CORE) for v in turn]

    def encode_pair(first, second):
        return encode(
            where,
            [first, second],
            enc_gain_in.reshape(1, D),
            depthwise,
            enc_gain_mid.reshape(1, D),
            shards,
        )

    mem_a = encode_pair(packed, from_b)
    query = project_query(source, dec_gain, w_query[0], mem_a)
    mem_b = encode_pair(from_a, from_2)

    a_from_l, a_from_r = along(mem_a, 1, 0), along(mem_a, -1, 0)
    b_from_l, b_from_r = along(mem_b, 1, 0), along(mem_b, -1, 0)

    tgt = tgt_lens.reshape(-1)

    def attend(parts, mems, prev):
        micro = jnp.concatenate([micros[y, z : z + 2] for y, z in parts])
        return decode(micro, tgt, mems, query, source, w_key[0], w_value[0], w_output[0], prev)

    a_far, b_far = along(a_from_l, 1, 0), along(b_from_r, -1, 0)
    out = attend([(0, 0), (0, 2)], [mem_a, mem_b], None)
    out = attend([(1, 0), (2, 0)], [a_from_l, a_from_r], out)
    out = attend([(1, 2), (2, 2)], [b_from_l, b_from_r], out)
    out = attend([(3, 0), (3, 2)], [a_far, b_far], out)
    return out.reshape(hidden.shape)


def solution(mesh):
    return jax.shard_map(
        body,
        mesh=mesh,
        in_specs=(
            P("section", "dp", None, None),
            P("section", "dp", None),
            P(None, "dp"),
            P(),
            P("dp", None),
            P(),
            P(),
            P("dp", None),
            P("section", None),
            P("section", None, None),
            P("section", None, None),
            P("section", None, None),
            P("section", None, None),
            P("section", None, "dp", None, None),
        ),
        out_specs=P("section", None, "dp", None, None),
        check_vma=False,
    )
```

```python
import functools

import jax
import jax.numpy as jnp
from jax import lax
from jax.experimental import pallas as pl
from jax.experimental.pallas import tpu as pltpu
from jax.sharding import PartitionSpec as P

HEADS = 16
D = 1024
HEAD = 64
FR = 40
TGT = 8
UTT = 4
TOT = 128
TAPS = 31
HALF = 15
GROUP = 4
EXTRA = 16
BF = jnp.bfloat16
F32 = jnp.float32
HBM = pl.BlockSpec(memory_space=pltpu.HBM)
VM = pl.BlockSpec(memory_space=pltpu.VMEM)
SM = pl.BlockSpec(memory_space=pltpu.SMEM)


def norm_rows(values, gain):
    average = jnp.mean(values, -1, keepdims=True)
    centered = values - average
    spread = jnp.mean(centered * centered, -1, keepdims=True)
    return centered * lax.rsqrt(spread + 1e-05) * gain


def params(limit):
    return pltpu.CompilerParams(vmem_limit_bytes=limit << 20)


def cost(flops, moved):
    return pl.CostEstimate(flops=flops, bytes_accessed=moved, transcendentals=0)


def one_hot(flags):
    return jnp.where(flags, 1.0, 0.0).astype(BF)


def slot_place(slot, lens_ref):
    utt = jnp.zeros_like(slot)
    start = jnp.zeros_like(slot)
    end = jnp.int32(0)
    for u in range(UTT - 1):
        end = end + lens_ref[u]
        later = slot >= end
        utt = jnp.where(later, u + 1, utt)
        start = jnp.where(later, end, start)
    return utt, slot - start


def join_kernel(w_in_hbm, w_out_hbm, own_ref, sems):
    loads = [
        pltpu.make_async_copy(w_in_hbm, own_ref.at[:, pl.ds(0, 2 * D)], sems.at[0]),
        pltpu.make_async_copy(w_out_hbm, own_ref.at[:, pl.ds(2 * D, D)], sems.at[1]),
    ]
    for load in loads:
        load.start()
    for load in loads:
        load.wait()


def join_shards(w_in, w_out):
    return pl.pallas_call(
        join_kernel,
        out_shape=jax.ShapeDtypeStruct((w_in.shape[0], 3 * D), BF),
        in_specs=[HBM, HBM],
        out_specs=VM,
        scratch_shapes=[pltpu.SemaphoreType.DMA((2,))],
        compiler_params=params(60),
        cost_estimate=cost(0, 800_000),
        name="join_shards",
    )(w_in, w_out)


def pack_kernel(lens_ref, frames_ref, own_hbm, out_ref):
    slot = lax.broadcasted_iota(jnp.int32, (TOT, UTT * FR), 0)
    lane = lax.broadcasted_iota(jnp.int32, (TOT, UTT * FR), 1)
    utt, frame = slot_place(slot, lens_ref)
    pick = one_hot(utt * FR + frame == lane)
    utt, frame = slot_place(lax.broadcasted_iota(jnp.int32, (EXTRA, TOT), 1), lens_ref)
    kind = lax.broadcasted_iota(jnp.int32, (EXTRA, TOT), 0)
    out_ref[TOT:, :TOT] = jnp.where(kind == 0, frame, utt).astype(F32).astype(BF)
    out_ref[TOT:, TOT:] = jnp.zeros((EXTRA, D - TOT), BF)
    for j in range(D // 256):
        cols = slice(j * 256, (j + 1) * 256)
        out_ref[:TOT, cols] = jnp.dot(
            pick, frames_ref[:, cols], preferred_element_type=F32
        ).astype(BF)


def pack_frames(lens, frames, after):
    return pl.pallas_call(
        pack_kernel,
        out_shape=jax.ShapeDtypeStruct((TOT + EXTRA, D), BF),
        in_specs=[SM, VM, HBM],
        out_specs=VM,
        compiler_params=params(4),
        cost_estimate=cost(50_000_000, 600_000),
        name="pack_frames",
    )(lens, frames, after)


def query_kernel(hidden_ref, gain_ref, w_ref, after_hbm, out_ref, normed):
    @pl.loop(0, hidden_ref.shape[0] // 32)
    def _(i):
        for r in range(0, 32, 16):
            rows = pl.ds(pl.multiple_of(i * 32 + r, 16), 16)
            normed[rows, :] = norm_rows(hidden_ref[rows, :].astype(F32), gain_ref[...]).astype(BF)

    for j in range(D // 256):
        cols = slice(j * 256, (j + 1) * 256)
        q = jnp.dot(normed[...], w_ref[:, cols], preferred_element_type=F32)
        out_ref[:, cols] = (q * (HEAD**-0.5)).astype(BF)


def project_query(hidden, gain, w, after):
    rows = hidden.shape[0]
    return pl.pallas_call(
        query_kernel,
        out_shape=jax.ShapeDtypeStruct((rows, D), BF),
        in_specs=[VM, VM, VM, HBM],
        out_specs=VM,
        scratch_shapes=[pltpu.VMEM((rows, D), BF)],
        compiler_params=params(8),
        cost_estimate=cost(2 * rows * D * D, 4 << 20),
        name="project_query",
    )(hidden, gain, w, after)


def order_columns(dst, src, where_ref):
    odd = jnp.broadcast_to(where_ref[0] % 2 == 1, (src.shape[0], 128))
    for i in range(D // 128):
        at = pl.multiple_of(where_ref[i] // 2 * 128, 128)
        block = src[:, pl.ds(at, 128)].astype(F32)
        block = jnp.where(odd, pltpu.roll(block, HEAD, 1), block)
        dst[:, i * 128 : (i + 1) * 128] = block.astype(BF)


def shard_rows(w_refs, k, cols):
    own, other = w_refs
    picks = [own[2 * k], other[2 * k], own[2 * k + 1], other[2 * k + 1]]
    return jnp.concatenate([ref[row : row + 64, cols] for ref, row in picks], axis=0)


def dot_shards(lhs, w_refs, cols):
    total = None
    for k in range(D // 256):
        term = jnp.dot(
            lhs[:, k * 256 : (k + 1) * 256],
            shard_rows(w_refs, k, cols),
            preferred_element_type=F32,
        )
        total = term if total is None else total + term
    return total


LATE = (6, 7, 10, 11)


def encode_kernel(n_w, where_ref, *refs):
    x_refs = refs[:2]
    gain_in_ref, dw_ref, gain_mid_ref = refs[2:5]
    blocks = [(ref, 0) for ref in refs[5 : 5 + n_w]]
    out_ref, plain, normed, spread, conv, taps, act, late, sems = refs[5 + n_w :]
    depth = late.shape[0] // len(LATE)
    copies = []
    for i, shard in enumerate(LATE):
        rows = pl.ds(i * depth, depth)
        copies.append(pltpu.make_async_copy(blocks[shard][0], late.at[rows, :], sems.at[i]))
        copies[-1].start()
        blocks[shard] = (late, i * depth)
    w_refs = blocks[: n_w // 2], blocks[n_w // 2 :]
    step = 16
    for i, x in enumerate(x_refs):

        @pl.loop(0, 2)
        def _(h):
            for r in range(0, TOT // 2, step):
                at = pl.multiple_of(h * (TOT // 2) + r, step)
                plain[pl.ds(i * TOT + at, step), :] = norm_rows(
                    x[pl.ds(at, step), :].astype(F32), gain_in_ref[...]
                ).astype(BF)

    order_columns(normed, plain, where_ref)
    taps[...] = dw_ref[...].astype(F32)
    rows = normed.shape[0]
    frame_rows = conv.shape[0]
    lanes = 2 * UTT
    target = []
    for i, x in enumerate(x_refs):
        places = x[TOT : TOT + EXTRA, :TOT].astype(F32)
        target.append(places[0:1] * lanes + places[1:2] + i * UTT)
    target = jnp.concatenate(target, axis=1)
    spot = lax.broadcasted_iota(jnp.int32, (frame_rows, rows), 0)
    expand = one_hot(target.astype(jnp.int32) == spot)
    column = jnp.broadcast_to(target, (8, rows)).T[:, 0:1].astype(jnp.int32)
    shrink = one_hot(column == lax.broadcasted_iota(jnp.int32, (rows, frame_rows), 1))
    for copy in copies:
        copy.wait()
    for j in range(D // 256):
        value = dot_shards(normed, w_refs, slice(j * 256, (j + 1) * 256))
        gate = dot_shards(normed, w_refs, slice(D + j * 256, D + (j + 1) * 256))
        gated = (value * jax.nn.sigmoid(gate)).astype(BF)
        spread[:, j * 256 : (j + 1) * 256] = jnp.dot(expand, gated, preferred_element_type=F32)
    block = 8

    @pl.loop(0, D // 128)
    def _(c):
        cols = pl.ds(pl.multiple_of(c * 128, 128), 128)
        weights = [jnp.broadcast_to(taps[k : k + 1, cols], (lanes, 128)) for k in range(TAPS)]
        for first in range(0, FR, block):
            sums = [None] * block
            for f in range(max(0, first - HALF), min(FR, first + block + HALF)):
                here = spread[f * lanes : (f + 1) * lanes, cols]
                for b in range(block):
                    k = f - (first + b) + HALF
                    if 0 <= k < TAPS:
                        term = here * weights[k]
                        sums[b] = term if sums[b] is None else sums[b] + term
            for b in range(block):
                at = (first + b) * lanes
                conv[at : at + lanes, cols] = sums[b]

    for r in range(0, frame_rows, step):
        v = norm_rows(conv[r : r + step, :], gain_mid_ref[...])
        act[r : r + step, :] = (v * jax.nn.sigmoid(v)).astype(BF)
    for j in range(D // 256):
        cols = slice(j * 256, (j + 1) * 256)
        plain[:, cols] = jnp.dot(shrink, act[:, cols], preferred_element_type=F32).astype(BF)
    order_columns(normed, plain, where_ref)
    for j in range(D // 256):
        cols = slice(j * 256, (j + 1) * 256)
        low = dot_shards(normed, w_refs, slice(2 * D + j * 256, 2 * D + (j + 1) * 256))
        for i, x in enumerate(x_refs):
            at = slice(i * TOT, (i + 1) * TOT)
            out_ref[at, cols] = (x[:TOT, cols].astype(F32) + low[at]).astype(BF)
    utts = [x[TOT : TOT + EXTRA, :TOT].astype(F32)[1:2] for x in x_refs]
    kind = lax.broadcasted_iota(jnp.int32, (EXTRA, TOT), 0)
    out_ref[rows:, :TOT] = jnp.where(kind == 0, utts[0], utts[1]).astype(BF)
    out_ref[rows:, TOT:] = jnp.zeros((EXTRA, D - TOT), BF)


def encode(where, xs, gain_in, dw, gain_mid, shards):
    rows = 2 * TOT
    frame_rows = 2 * UTT * FR
    return pl.pallas_call(
        functools.partial(encode_kernel, len(shards)),
        out_shape=jax.ShapeDtypeStruct((rows + EXTRA, D), BF),
        in_specs=[SM] + [VM] * 5 + [HBM if i in LATE else VM for i in range(len(shards))],
        out_specs=VM,
        scratch_shapes=[
            pltpu.VMEM((rows, D), BF),
            pltpu.VMEM((rows, D), BF),
            pltpu.VMEM((frame_rows, D), F32),
            pltpu.VMEM((frame_rows, D), F32),
            pltpu.VMEM((TAPS, D), F32),
            pltpu.VMEM((frame_rows, D), BF),
            pltpu.VMEM((len(LATE) * D // 16, 3 * D), BF),
            pltpu.SemaphoreType.DMA((len(LATE),)),
        ],
        compiler_params=params(9),
        cost_estimate=cost(8_000_000_000, 8 << 20),
        name="encode",
    )(where, *xs, gain_in, dw, gain_mid, *shards)


def decode_kernel(n_mem, aliased, micro_ref, tgt_ref, *refs):
    mem_refs = refs[:n_mem]
    q_ref, hidden_ref, wk, wv, wo = refs[n_mem : n_mem + 5]
    rest = refs[n_mem + 5 + (1 if aliased else 0) :]
    out_hbm, keys, values, ctx, res, seg, out_sems = rest
    slots = UTT * TGT
    micros = 2 * n_mem
    for w, out in ((wk, keys), (wv, values)):
        for p, mem in enumerate(mem_refs):
            for j in range(D // 256):
                cols = slice(j * 256, (j + 1) * 256)
                out[p * 2 * TOT : (p + 1) * 2 * TOT, cols] = jnp.dot(
                    mem[: 2 * TOT, :], w[:, cols], preferred_element_type=F32
                ).astype(BF)
    width = GROUP * HEAD
    tall = GROUP * slots
    row = lax.broadcasted_iota(jnp.int32, (tall, width), 0)
    lane = lax.broadcasted_iota(jnp.int32, (tall, width), 1)
    own = (row // slots) == (lane // HEAD)
    own_bf = one_hot(own)
    utt_of_row = (lax.broadcasted_iota(jnp.int32, (tall, TOT), 0) // TGT) % UTT
    groups = HEADS // GROUP
    for i in range(micros):
        utts = mem_refs[i // 2][2 * TOT : 2 * TOT + EXTRA, :TOT].astype(F32)
        seg[i * 8 : i * 8 + 8, :] = jnp.broadcast_to(utts[i % 2 : i % 2 + 1], (8, TOT))

    def attend(i):
        line = seg[pl.ds(pl.multiple_of(i * 8, 8), 8), :]
        allowed = utt_of_row == line[0:1].astype(jnp.int32)
        at = pl.ds(pl.multiple_of(i * TOT, TOT), TOT)
        mine = pl.ds(pl.multiple_of(i * slots, slots), slots)
        from_rows = pl.ds(pl.multiple_of(micro_ref[i] * slots, slots), slots)
        cuts = [slice(j * width, (j + 1) * width) for j in range(groups)]
        scores = []
        for cols in cuts:
            q = q_ref[from_rows, cols]
            q = jnp.concatenate([q] * GROUP, axis=0) * own_bf
            scores.append(
                lax.dot_general(
                    q, keys[at, cols], (((1,), (1,)), ((), ())), preferred_element_type=F32
                )
            )
        probs = []
        for s in scores:
            s = jnp.where(allowed, s, -1e30)
            expo = jnp.exp(s - jnp.max(s, -1, keepdims=True))
            probs.append((expo * (1.0 / jnp.sum(expo, -1, keepdims=True))).astype(BF))
        for prob, cols in zip(probs, cuts):
            mixed = jnp.dot(prob, values[at, cols], preferred_element_type=F32)
            mixed = jnp.where(own, mixed, 0.0)
            total = mixed[:slots]
            for g in range(1, GROUP):
                total = total + mixed[g * slots : (g + 1) * slots]
            ctx[mine, cols] = total.astype(BF)

    @pl.loop(0, micros // 2)
    def _(p):
        attend(2 * p)
        attend(2 * p + 1)

    pos = lax.broadcasted_iota(jnp.int32, (slots, 256), 0)

    @pl.loop(0, D // 512)
    def _(h):
      for half in range(2):
        cols = pl.ds(pl.multiple_of(h * 512 + half * 256, 256), 256)
        proj = jnp.dot(ctx[...], wo[:, cols], preferred_element_type=F32)
        for i in range(micros):
            mine = slice(i * slots, (i + 1) * slots)
            from_rows = pl.ds(pl.multiple_of(micro_ref[i] * slots, slots), slots)
            base = micro_ref[i] * UTT
            limit = jnp.full((slots, 256), tgt_ref[base], jnp.int32)
            for u in range(1, UTT):
                limit = jnp.where(pos // TGT == u, tgt_ref[base + u], limit)
            both = hidden_ref[from_rows, cols].astype(F32) + proj[mine]
            res[mine, cols] = jnp.where(pos % TGT < limit, both, 0.0).astype(BF)

    outs = []
    for i in range(micros):
        at = pl.ds(pl.multiple_of(micro_ref[i] * slots, slots), slots)
        here = pl.ds(i * slots, slots)
        copy = pltpu.make_async_copy(res.at[here, :], out_hbm.at[at, :], out_sems.at[i])
        copy.start()
        outs.append(copy)
    for copy in outs:
        copy.wait()


def decode(micro, tgt, mems, q, hidden, wk, wv, wo, prev):
    rows = hidden.shape[0]
    micros = 2 * len(mems)
    total = micros * TOT
    slots = UTT * TGT
    aliased = prev is not None
    args = [micro, tgt, *mems, q, hidden, wk, wv, wo] + ([prev] if aliased else [])
    return pl.pallas_call(
        functools.partial(decode_kernel, len(mems), aliased),
        out_shape=jax.ShapeDtypeStruct((rows, D), BF),
        in_specs=[SM, SM] + [VM] * (len(mems) + 5) + [HBM] * aliased,
        out_specs=HBM,
        scratch_shapes=[
            pltpu.VMEM((total, D), BF),
            pltpu.VMEM((total, D), BF),
            pltpu.VMEM((micros * slots, D), BF),
            pltpu.VMEM((micros * slots, D), BF),
            pltpu.VMEM((micros * 8, TOT), F32),
            pltpu.SemaphoreType.DMA((micros,)),
        ],
        input_output_aliases={len(args) - 1: 0} if aliased else {},
        compiler_params=params(7),
        cost_estimate=cost(16 * total * D * D, 8 << 20),
        name="decode",
    )(*args)


def dp_perm(move):
    pairs = []
    for z in range(2):
        for x in range(4):
            for c in range(2):
                nz, nx, nc = move(z, x, c)
                pairs.append(((z * 4 + x) * 2 + c, (nz * 4 + nx % 4) * 2 + nc))
    return pairs


def section_perm(dy, dz):
    return [(y * 4 + z, (y + dy) % 4 * 4 + (z + dz) % 4) for y in range(4) for z in range(4)]


TO_PAIR = dp_perm(lambda z, x, c: (1 - z, x, c))
TO_RIGHT = dp_perm(lambda z, x, c: (z, x + 1, c))
TO_LEFT = dp_perm(lambda z, x, c: (z, x + 3, c))
TO_CORE = dp_perm(lambda z, x, c: (z, x, 1 - c))


def pass_kernel(value_ref, *refs):
    refs[-1][...] = value_ref[...]


def pass_after(value, *others):
    return pl.pallas_call(
        pass_kernel,
        out_shape=jax.ShapeDtypeStruct(value.shape, value.dtype),
        in_specs=[VM] + [HBM] * len(others),
        out_specs=VM,
        compiler_params=params(2),
        cost_estimate=cost(0, 600_000),
        name="pass_after",
    )(value, *others)


def shard_table():
    places = [(0, 0), (1, 0), (0, 3), (0, 1), (1, 3), (1, 1), (0, 2), (1, 2)]
    table = []
    for index in range(16):
        z, x, c = index // 8, index // 2 % 4, index % 2
        table.append(
            [
                ((z + a) % 2 * 4 + (x + b) % 4) * 2 + (c + s) % 2
                for s in (0, 1)
                for a, b in places
            ]
        )
    return table


REL = (0, -1, 1, 2)


def micro_table():
    return [
        [(y + dy) % 4 * 4 + (z + dz) % 4 for dy in REL for dz in REL]
        for y in range(4)
        for z in range(4)
    ]


def body(
    frames,
    frame_lens,
    tgt_lens,
    enc_gain_in,
    w_in,
    depthwise,
    enc_gain_mid,
    w_out,
    dec_gain,
    w_query,
    w_key,
    w_value,
    w_output,
    hidden,
):
    across = lambda v, perm: lax.ppermute(v, "dp", perm)
    along = lambda v, dy, dz: lax.ppermute(v, "section", section_perm(dy, dz))
    where = jnp.array(shard_table(), jnp.int32)[lax.axis_index("dp")]
    micros = jnp.array(micro_table(), jnp.int32)[lax.axis_index("section")].reshape(4, 4)

    own = join_shards(w_in, w_out)
    pair = across(own, TO_PAIR)
    own_l, own_r = across(own, TO_RIGHT), across(own, TO_LEFT)
    pair_l, pair_r = across(pair, TO_RIGHT), across(pair, TO_LEFT)
    own_2, pair_2 = across(own_l, TO_RIGHT), across(pair_r, TO_LEFT)
    shards = [own, pair, own_l, own_r, pair_l, pair_r, own_2, pair_2]

    packed = pack_frames(frame_lens.reshape(UTT), frames.reshape(UTT * FR, D), pair)
    from_b, from_a = along(packed, 0, 1), along(packed, 0, -1)
    source = hidden.reshape(-1, D)
    turn = list(shards)
    turn[1] = pass_after(turn[1], from_b, from_a)
    from_2 = along(from_b, 0, 1)
    shards += [across(v, TO_CORE) for v in turn]

    def encode_pair(first, second):
        return encode(
            where,
            [first, second],
            enc_gain_in.reshape(1, D),
            depthwise,
            enc_gain_mid.reshape(1, D),
            shards,
        )

    mem_a = encode_pair(packed, from_b)
    query = project_query(source, dec_gain, w_query[0], mem_a)
    mem_b = encode_pair(from_a, from_2)

    a_from_l, a_from_r = along(mem_a, 1, 0), along(mem_a, -1, 0)
    b_from_l, b_from_r = along(mem_b, 1, 0), along(mem_b, -1, 0)

    tgt = tgt_lens.reshape(-1)

    def attend(parts, mems, prev):
        micro = jnp.concatenate([micros[y, z : z + 2] for y, z in parts])
        return decode(micro, tgt, mems, query, source, w_key[0], w_value[0], w_output[0], prev)

    a_far, b_far = along(a_from_l, 1, 0), along(b_from_r, -1, 0)
    out = attend([(0, 0), (0, 2)], [mem_a, mem_b], None)
    out = attend([(1, 0), (2, 0)], [a_from_l, a_from_r], out)
    out = attend([(1, 2), (2, 2)], [b_from_l, b_from_r], out)
    out = attend([(3, 0), (3, 2)], [a_far, b_far], out)
    return out.reshape(hidden.shape)


def solution(mesh):
    return jax.shard_map(
        body,
        mesh=mesh,
        in_specs=(
            P("section", "dp", None, None),
            P("section", "dp", None),
            P(None, "dp"),
            P(),
            P("dp", None),
            P(),
            P(),
            P("dp", None),
            P("section", None),
            P("section", None, None),
            P("section", None, None),
            P("section", None, None),
            P("section", None, None),
            P("section", None, "dp", None, None),
        ),
        out_specs=P("section", None, "dp", None, None),
        check_vma=False,
    )
```

```python
import functools

import jax
import jax.numpy as jnp
from jax import lax
from jax.experimental import pallas as pl
from jax.experimental.pallas import tpu as pltpu
from jax.sharding import PartitionSpec as P

HEADS = 16
D = 1024
HEAD = 64
FR = 40
TGT = 8
UTT = 4
TOT = 128
TAPS = 31
HALF = 15
GROUP = 4
EXTRA = 16
BF = jnp.bfloat16
F32 = jnp.float32
HBM = pl.BlockSpec(memory_space=pltpu.HBM)
VM = pl.BlockSpec(memory_space=pltpu.VMEM)
SM = pl.BlockSpec(memory_space=pltpu.SMEM)


def norm_rows(values, gain):
    average = jnp.mean(values, -1, keepdims=True)
    centered = values - average
    spread = jnp.mean(centered * centered, -1, keepdims=True)
    return centered * lax.rsqrt(spread + 1e-05) * gain


def params(limit):
    return pltpu.CompilerParams(vmem_limit_bytes=limit << 20)


def cost(flops, moved):
    return pl.CostEstimate(flops=flops, bytes_accessed=moved, transcendentals=0)


def one_hot(flags):
    return jnp.where(flags, 1.0, 0.0).astype(BF)


def slot_place(slot, lens_ref):
    utt = jnp.zeros_like(slot)
    start = jnp.zeros_like(slot)
    end = jnp.int32(0)
    for u in range(UTT - 1):
        end = end + lens_ref[u]
        later = slot >= end
        utt = jnp.where(later, u + 1, utt)
        start = jnp.where(later, end, start)
    return utt, slot - start


def join_kernel(w_in_hbm, w_out_hbm, own_ref, sems):
    loads = [
        pltpu.make_async_copy(w_in_hbm, own_ref.at[:, pl.ds(0, 2 * D)], sems.at[0]),
        pltpu.make_async_copy(w_out_hbm, own_ref.at[:, pl.ds(2 * D, D)], sems.at[1]),
    ]
    for load in loads:
        load.start()
    for load in loads:
        load.wait()


def join_shards(w_in, w_out):
    return pl.pallas_call(
        join_kernel,
        out_shape=jax.ShapeDtypeStruct((w_in.shape[0], 3 * D), BF),
        in_specs=[HBM, HBM],
        out_specs=VM,
        scratch_shapes=[pltpu.SemaphoreType.DMA((2,))],
        compiler_params=params(60),
        cost_estimate=cost(0, 800_000),
        name="join_shards",
    )(w_in, w_out)


def pack_kernel(lens_ref, frames_ref, own_hbm, out_ref):
    slot = lax.broadcasted_iota(jnp.int32, (TOT, UTT * FR), 0)
    lane = lax.broadcasted_iota(jnp.int32, (TOT, UTT * FR), 1)
    utt, frame = slot_place(slot, lens_ref)
    pick = one_hot(utt * FR + frame == lane)
    utt, frame = slot_place(lax.broadcasted_iota(jnp.int32, (EXTRA, TOT), 1), lens_ref)
    kind = lax.broadcasted_iota(jnp.int32, (EXTRA, TOT), 0)
    out_ref[TOT:, :TOT] = jnp.where(kind == 0, frame, utt).astype(F32).astype(BF)
    out_ref[TOT:, TOT:] = jnp.zeros((EXTRA, D - TOT), BF)
    for j in range(D // 256):
        cols = slice(j * 256, (j + 1) * 256)
        out_ref[:TOT, cols] = jnp.dot(
            pick, frames_ref[:, cols], preferred_element_type=F32
        ).astype(BF)


def pack_frames(lens, frames, after):
    return pl.pallas_call(
        pack_kernel,
        out_shape=jax.ShapeDtypeStruct((TOT + EXTRA, D), BF),
        in_specs=[SM, VM, HBM],
        out_specs=VM,
        compiler_params=params(4),
        cost_estimate=cost(50_000_000, 600_000),
        name="pack_frames",
    )(lens, frames, after)


def query_kernel(hidden_ref, gain_ref, w_ref, after_hbm, out_ref, normed):
    @pl.loop(0, hidden_ref.shape[0] // 32)
    def _(i):
        for r in range(0, 32, 16):
            rows = pl.ds(pl.multiple_of(i * 32 + r, 16), 16)
            normed[rows, :] = norm_rows(hidden_ref[rows, :].astype(F32), gain_ref[...]).astype(BF)

    for j in range(D // 256):
        cols = slice(j * 256, (j + 1) * 256)
        q = jnp.dot(normed[...], w_ref[:, cols], preferred_element_type=F32)
        out_ref[:, cols] = (q * (HEAD**-0.5)).astype(BF)


def project_query(hidden, gain, w, after):
    rows = hidden.shape[0]
    return pl.pallas_call(
        query_kernel,
        out_shape=jax.ShapeDtypeStruct((rows, D), BF),
        in_specs=[VM, VM, VM, HBM],
        out_specs=VM,
        scratch_shapes=[pltpu.VMEM((rows, D), BF)],
        compiler_params=params(8),
        cost_estimate=cost(2 * rows * D * D, 4 << 20),
        name="project_query",
    )(hidden, gain, w, after)


def order_columns(dst, src, where_ref):
    odd = jnp.broadcast_to(where_ref[0] % 2 == 1, (src.shape[0], 128))
    for i in range(D // 128):
        at = pl.multiple_of(where_ref[i] // 2 * 128, 128)
        block = src[:, pl.ds(at, 128)].astype(F32)
        block = jnp.where(odd, pltpu.roll(block, HEAD, 1), block)
        dst[:, i * 128 : (i + 1) * 128] = block.astype(BF)


def shard_rows(w_refs, k, cols):
    own, other = w_refs
    picks = [own[2 * k], other[2 * k], own[2 * k + 1], other[2 * k + 1]]
    return jnp.concatenate([ref[row : row + 64, cols] for ref, row in picks], axis=0)


def dot_shards(lhs, w_refs, cols):
    total = None
    for k in range(D // 256):
        term = jnp.dot(
            lhs[:, k * 256 : (k + 1) * 256],
            shard_rows(w_refs, k, cols),
            preferred_element_type=F32,
        )
        total = term if total is None else total + term
    return total


LATE = (6, 7, 10, 11)


def encode_kernel(n_w, where_ref, *refs):
    x_refs = refs[:2]
    gain_in_ref, dw_ref, gain_mid_ref = refs[2:5]
    blocks = [(ref, 0) for ref in refs[5 : 5 + n_w]]
    out_ref, plain, normed, spread, conv, taps, act, late, sems = refs[5 + n_w :]
    depth = late.shape[0] // len(LATE)
    copies = []
    for i, shard in enumerate(LATE):
        rows = pl.ds(i * depth, depth)
        copies.append(pltpu.make_async_copy(blocks[shard][0], late.at[rows, :], sems.at[i]))
        copies[-1].start()
        blocks[shard] = (late, i * depth)
    w_refs = blocks[: n_w // 2], blocks[n_w // 2 :]
    step = 16
    for i, x in enumerate(x_refs):
        for r in range(0, TOT, step):
            plain[i * TOT + r : i * TOT + r + step, :] = norm_rows(
                x[r : r + step, :].astype(F32), gain_in_ref[...]
            ).astype(BF)
    order_columns(normed, plain, where_ref)
    taps[...] = dw_ref[...].astype(F32)
    rows = normed.shape[0]
    frame_rows = conv.shape[0]
    lanes = 2 * UTT
    target = []
    for i, x in enumerate(x_refs):
        places = x[TOT : TOT + EXTRA, :TOT].astype(F32)
        target.append(places[0:1] * lanes + places[1:2] + i * UTT)
    target = jnp.concatenate(target, axis=1)
    spot = lax.broadcasted_iota(jnp.int32, (frame_rows, rows), 0)
    expand = one_hot(target.astype(jnp.int32) == spot)
    column = jnp.broadcast_to(target, (8, rows)).T[:, 0:1].astype(jnp.int32)
    shrink = one_hot(column == lax.broadcasted_iota(jnp.int32, (rows, frame_rows), 1))
    for copy in copies:
        copy.wait()
    for j in range(D // 256):
        value = dot_shards(normed, w_refs, slice(j * 256, (j + 1) * 256))
        gate = dot_shards(normed, w_refs, slice(D + j * 256, D + (j + 1) * 256))
        gated = (value * jax.nn.sigmoid(gate)).astype(BF)
        spread[:, j * 256 : (j + 1) * 256] = jnp.dot(expand, gated, preferred_element_type=F32)
    block = 8

    @pl.loop(0, D // 128)
    def _(c):
        cols = pl.ds(pl.multiple_of(c * 128, 128), 128)
        weights = [jnp.broadcast_to(taps[k : k + 1, cols], (lanes, 128)) for k in range(TAPS)]
        for first in range(0, FR, block):
            sums = [None] * block
            for f in range(max(0, first - HALF), min(FR, first + block + HALF)):
                here = spread[f * lanes : (f + 1) * lanes, cols]
                for b in range(block):
                    k = f - (first + b) + HALF
                    if 0 <= k < TAPS:
                        term = here * weights[k]
                        sums[b] = term if sums[b] is None else sums[b] + term
            for b in range(block):
                at = (first + b) * lanes
                conv[at : at + lanes, cols] = sums[b]

    for r in range(0, frame_rows, step):
        v = norm_rows(conv[r : r + step, :], gain_mid_ref[...])
        act[r : r + step, :] = (v * jax.nn.sigmoid(v)).astype(BF)
    for j in range(D // 256):
        cols = slice(j * 256, (j + 1) * 256)
        plain[:, cols] = jnp.dot(shrink, act[:, cols], preferred_element_type=F32).astype(BF)
    order_columns(normed, plain, where_ref)
    for j in range(D // 256):
        cols = slice(j * 256, (j + 1) * 256)
        low = dot_shards(normed, w_refs, slice(2 * D + j * 256, 2 * D + (j + 1) * 256))
        for i, x in enumerate(x_refs):
            at = slice(i * TOT, (i + 1) * TOT)
            out_ref[at, cols] = (x[:TOT, cols].astype(F32) + low[at]).astype(BF)
    utts = [x[TOT : TOT + EXTRA, :TOT].astype(F32)[1:2] for x in x_refs]
    kind = lax.broadcasted_iota(jnp.int32, (EXTRA, TOT), 0)
    out_ref[rows:, :TOT] = jnp.where(kind == 0, utts[0], utts[1]).astype(BF)
    out_ref[rows:, TOT:] = jnp.zeros((EXTRA, D - TOT), BF)


def encode(where, xs, gain_in, dw, gain_mid, shards):
    rows = 2 * TOT
    frame_rows = 2 * UTT * FR
    return pl.pallas_call(
        functools.partial(encode_kernel, len(shards)),
        out_shape=jax.ShapeDtypeStruct((rows + EXTRA, D), BF),
        in_specs=[SM] + [VM] * 5 + [HBM if i in LATE else VM for i in range(len(shards))],
        out_specs=VM,
        scratch_shapes=[
            pltpu.VMEM((rows, D), BF),
            pltpu.VMEM((rows, D), BF),
            pltpu.VMEM((frame_rows, D), F32),
            pltpu.VMEM((frame_rows, D), F32),
            pltpu.VMEM((TAPS, D), F32),
            pltpu.VMEM((frame_rows, D), BF),
            pltpu.VMEM((len(LATE) * D // 16, 3 * D), BF),
            pltpu.SemaphoreType.DMA((len(LATE),)),
        ],
        compiler_params=params(9),
        cost_estimate=cost(8_000_000_000, 8 << 20),
        name="encode",
    )(where, *xs, gain_in, dw, gain_mid, *shards)


def decode_kernel(n_mem, aliased, micro_ref, tgt_ref, *refs):
    mem_refs = refs[:n_mem]
    q_ref, hidden_ref, wk, wv, wo = refs[n_mem : n_mem + 5]
    rest = refs[n_mem + 5 + (1 if aliased else 0) :]
    out_hbm, keys, values, ctx, res, seg, out_sems = rest
    slots = UTT * TGT
    micros = 2 * n_mem
    for w, out in ((wk, keys), (wv, values)):
        for p, mem in enumerate(mem_refs):
            for j in range(D // 256):
                cols = slice(j * 256, (j + 1) * 256)
                out[p * 2 * TOT : (p + 1) * 2 * TOT, cols] = jnp.dot(
                    mem[: 2 * TOT, :], w[:, cols], preferred_element_type=F32
                ).astype(BF)
    width = GROUP * HEAD
    tall = GROUP * slots
    row = lax.broadcasted_iota(jnp.int32, (tall, width), 0)
    lane = lax.broadcasted_iota(jnp.int32, (tall, width), 1)
    own = (row // slots) == (lane // HEAD)
    own_bf = one_hot(own)
    utt_of_row = (lax.broadcasted_iota(jnp.int32, (tall, TOT), 0) // TGT) % UTT
    groups = HEADS // GROUP
    for i in range(micros):
        utts = mem_refs[i // 2][2 * TOT : 2 * TOT + EXTRA, :TOT].astype(F32)
        seg[i * 8 : i * 8 + 8, :] = jnp.broadcast_to(utts[i % 2 : i % 2 + 1], (8, TOT))

    def attend(i):
        line = seg[pl.ds(pl.multiple_of(i * 8, 8), 8), :]
        allowed = utt_of_row == line[0:1].astype(jnp.int32)
        at = pl.ds(pl.multiple_of(i * TOT, TOT), TOT)
        mine = pl.ds(pl.multiple_of(i * slots, slots), slots)
        from_rows = pl.ds(pl.multiple_of(micro_ref[i] * slots, slots), slots)
        cuts = [slice(j * width, (j + 1) * width) for j in range(groups)]
        scores = []
        for cols in cuts:
            q = q_ref[from_rows, cols]
            q = jnp.concatenate([q] * GROUP, axis=0) * own_bf
            scores.append(
                lax.dot_general(
                    q, keys[at, cols], (((1,), (1,)), ((), ())), preferred_element_type=F32
                )
            )
        probs = []
        for s in scores:
            s = jnp.where(allowed, s, -1e30)
            expo = jnp.exp(s - jnp.max(s, -1, keepdims=True))
            probs.append((expo * (1.0 / jnp.sum(expo, -1, keepdims=True))).astype(BF))
        for prob, cols in zip(probs, cuts):
            mixed = jnp.dot(prob, values[at, cols], preferred_element_type=F32)
            mixed = jnp.where(own, mixed, 0.0)
            total = mixed[:slots]
            for g in range(1, GROUP):
                total = total + mixed[g * slots : (g + 1) * slots]
            ctx[mine, cols] = total.astype(BF)

    @pl.loop(0, micros // 2)
    def _(p):
        attend(2 * p)
        attend(2 * p + 1)

    pos = lax.broadcasted_iota(jnp.int32, (slots, 256), 0)

    @pl.loop(0, D // 256)
    def _(j):
        cols = pl.ds(pl.multiple_of(j * 256, 256), 256)
        proj = jnp.dot(ctx[...], wo[:, cols], preferred_element_type=F32)
        for i in range(micros):
            mine = slice(i * slots, (i + 1) * slots)
            from_rows = pl.ds(pl.multiple_of(micro_ref[i] * slots, slots), slots)
            base = micro_ref[i] * UTT
            limit = jnp.full((slots, 256), tgt_ref[base], jnp.int32)
            for u in range(1, UTT):
                limit = jnp.where(pos // TGT == u, tgt_ref[base + u], limit)
            both = hidden_ref[from_rows, cols].astype(F32) + proj[mine]
            res[mine, cols] = jnp.where(pos % TGT < limit, both, 0.0).astype(BF)

    outs = []
    for i in range(micros):
        at = pl.ds(pl.multiple_of(micro_ref[i] * slots, slots), slots)
        here = pl.ds(i * slots, slots)
        copy = pltpu.make_async_copy(res.at[here, :], out_hbm.at[at, :], out_sems.at[i])
        copy.start()
        outs.append(copy)
    for copy in outs:
        copy.wait()


def decode(micro, tgt, mems, q, hidden, wk, wv, wo, prev):
    rows = hidden.shape[0]
    micros = 2 * len(mems)
    total = micros * TOT
    slots = UTT * TGT
    aliased = prev is not None
    args = [micro, tgt, *mems, q, hidden, wk, wv, wo] + ([prev] if aliased else [])
    return pl.pallas_call(
        functools.partial(decode_kernel, len(mems), aliased),
        out_shape=jax.ShapeDtypeStruct((rows, D), BF),
        in_specs=[SM, SM] + [VM] * (len(mems) + 5) + [HBM] * aliased,
        out_specs=HBM,
        scratch_shapes=[
            pltpu.VMEM((total, D), BF),
            pltpu.VMEM((total, D), BF),
            pltpu.VMEM((micros * slots, D), BF),
            pltpu.VMEM((micros * slots, D), BF),
            pltpu.VMEM((micros * 8, TOT), F32),
            pltpu.SemaphoreType.DMA((micros,)),
        ],
        input_output_aliases={len(args) - 1: 0} if aliased else {},
        compiler_params=params(7),
        cost_estimate=cost(16 * total * D * D, 8 << 20),
        name="decode",
    )(*args)


def dp_perm(move):
    pairs = []
    for z in range(2):
        for x in range(4):
            for c in range(2):
                nz, nx, nc = move(z, x, c)
                pairs.append(((z * 4 + x) * 2 + c, (nz * 4 + nx % 4) * 2 + nc))
    return pairs


def section_perm(dy, dz):
    return [(y * 4 + z, (y + dy) % 4 * 4 + (z + dz) % 4) for y in range(4) for z in range(4)]


TO_PAIR = dp_perm(lambda z, x, c: (1 - z, x, c))
TO_RIGHT = dp_perm(lambda z, x, c: (z, x + 1, c))
TO_LEFT = dp_perm(lambda z, x, c: (z, x + 3, c))
TO_CORE = dp_perm(lambda z, x, c: (z, x, 1 - c))


def pass_kernel(value_ref, *refs):
    refs[-1][...] = value_ref[...]


def pass_after(value, *others):
    return pl.pallas_call(
        pass_kernel,
        out_shape=jax.ShapeDtypeStruct(value.shape, value.dtype),
        in_specs=[VM] + [HBM] * len(others),
        out_specs=VM,
        compiler_params=params(2),
        cost_estimate=cost(0, 600_000),
        name="pass_after",
    )(value, *others)


def shard_table():
    places = [(0, 0), (1, 0), (0, 3), (0, 1), (1, 3), (1, 1), (0, 2), (1, 2)]
    table = []
    for index in range(16):
        z, x, c = index // 8, index // 2 % 4, index % 2
        table.append(
            [
                ((z + a) % 2 * 4 + (x + b) % 4) * 2 + (c + s) % 2
                for s in (0, 1)
                for a, b in places
            ]
        )
    return table


REL = (0, -1, 1, 2)


def micro_table():
    return [
        [(y + dy) % 4 * 4 + (z + dz) % 4 for dy in REL for dz in REL]
        for y in range(4)
        for z in range(4)
    ]


def body(
    frames,
    frame_lens,
    tgt_lens,
    enc_gain_in,
    w_in,
    depthwise,
    enc_gain_mid,
    w_out,
    dec_gain,
    w_query,
    w_key,
    w_value,
    w_output,
    hidden,
):
    across = lambda v, perm: lax.ppermute(v, "dp", perm)
    along = lambda v, dy, dz: lax.ppermute(v, "section", section_perm(dy, dz))
    where = jnp.array(shard_table(), jnp.int32)[lax.axis_index("dp")]
    micros = jnp.array(micro_table(), jnp.int32)[lax.axis_index("section")].reshape(4, 4)

    own = join_shards(w_in, w_out)
    pair = across(own, TO_PAIR)
    own_l, own_r = across(own, TO_RIGHT), across(own, TO_LEFT)
    pair_l, pair_r = across(pair, TO_RIGHT), across(pair, TO_LEFT)
    own_2, pair_2 = across(own_l, TO_RIGHT), across(pair_r, TO_LEFT)
    shards = [own, pair, own_l, own_r, pair_l, pair_r, own_2, pair_2]

    packed = pack_frames(frame_lens.reshape(UTT), frames.reshape(UTT * FR, D), pair)
    from_b, from_a = along(packed, 0, 1), along(packed, 0, -1)
    source = hidden.reshape(-1, D)
    turn = list(shards)
    turn[1] = pass_after(turn[1], from_b, from_a)
    from_2 = along(from_b, 0, 1)
    shards += [across(v, TO_CORE) for v in turn]

    def encode_pair(first, second):
        return encode(
            where,
            [first, second],
            enc_gain_in.reshape(1, D),
            depthwise,
            enc_gain_mid.reshape(1, D),
            shards,
        )

    mem_a = encode_pair(packed, from_b)
    query = project_query(source, dec_gain, w_query[0], mem_a)
    mem_b = encode_pair(from_a, from_2)

    a_from_l, a_from_r = along(mem_a, 1, 0), along(mem_a, -1, 0)
    b_from_l, b_from_r = along(mem_b, 1, 0), along(mem_b, -1, 0)

    tgt = tgt_lens.reshape(-1)

    def attend(parts, mems, prev):
        micro = jnp.concatenate([micros[y, z : z + 2] for y, z in parts])
        return decode(micro, tgt, mems, query, source, w_key[0], w_value[0], w_output[0], prev)

    a_far, b_far = along(a_from_l, 1, 0), along(b_from_r, -1, 0)
    out = attend([(0, 0), (0, 2)], [mem_a, mem_b], None)
    out = attend([(1, 0), (2, 0)], [a_from_l, a_from_r], out)
    out = attend([(1, 2), (2, 2)], [b_from_l, b_from_r], out)
    out = attend([(3, 0), (3, 2)], [a_far, b_far], out)
    return out.reshape(hidden.shape)


def solution(mesh):
    return jax.shard_map(
        body,
        mesh=mesh,
        in_specs=(
            P("section", "dp", None, None),
            P("section", "dp", None),
            P(None, "dp"),
            P(),
            P("dp", None),
            P(),
            P(),
            P("dp", None),
            P("section", None),
            P("section", None, None),
            P("section", None, None),
            P("section", None, None),
            P("section", None, None),
            P("section", None, "dp", None, None),
        ),
        out_specs=P("section", None, "dp", None, None),
        check_vma=False,
    )
```

```python
import functools

import jax
import jax.numpy as jnp
from jax import lax
from jax.experimental import pallas as pl
from jax.experimental.pallas import tpu as pltpu
from jax.sharding import PartitionSpec as P

HEADS = 16
D = 1024
HEAD = 64
FR = 40
TGT = 8
UTT = 4
TOT = 128
TAPS = 31
HALF = 15
GROUP = 4
EXTRA = 16
BF = jnp.bfloat16
F32 = jnp.float32
HBM = pl.BlockSpec(memory_space=pltpu.HBM)
VM = pl.BlockSpec(memory_space=pltpu.VMEM)
SM = pl.BlockSpec(memory_space=pltpu.SMEM)


def norm_rows(values, gain):
    average = jnp.mean(values, -1, keepdims=True)
    centered = values - average
    spread = jnp.mean(centered * centered, -1, keepdims=True)
    return centered * lax.rsqrt(spread + 1e-05) * gain


def params(limit):
    return pltpu.CompilerParams(vmem_limit_bytes=limit << 20)


def cost(flops, moved):
    return pl.CostEstimate(flops=flops, bytes_accessed=moved, transcendentals=0)


def one_hot(flags):
    return jnp.where(flags, 1.0, 0.0).astype(BF)


def slot_place(slot, lens_ref):
    utt = jnp.zeros_like(slot)
    start = jnp.zeros_like(slot)
    end = jnp.int32(0)
    for u in range(UTT - 1):
        end = end + lens_ref[u]
        later = slot >= end
        utt = jnp.where(later, u + 1, utt)
        start = jnp.where(later, end, start)
    return utt, slot - start


def join_kernel(w_in_hbm, w_out_hbm, own_ref, sems):
    loads = [
        pltpu.make_async_copy(w_in_hbm, own_ref.at[:, pl.ds(0, 2 * D)], sems.at[0]),
        pltpu.make_async_copy(w_out_hbm, own_ref.at[:, pl.ds(2 * D, D)], sems.at[1]),
    ]
    for load in loads:
        load.start()
    for load in loads:
        load.wait()


def join_shards(w_in, w_out):
    return pl.pallas_call(
        join_kernel,
        out_shape=jax.ShapeDtypeStruct((w_in.shape[0], 3 * D), BF),
        in_specs=[HBM, HBM],
        out_specs=VM,
        scratch_shapes=[pltpu.SemaphoreType.DMA((2,))],
        compiler_params=params(60),
        cost_estimate=cost(0, 800_000),
        name="join_shards",
    )(w_in, w_out)


def pack_kernel(lens_ref, frames_ref, own_hbm, out_ref):
    slot = lax.broadcasted_iota(jnp.int32, (TOT, UTT * FR), 0)
    lane = lax.broadcasted_iota(jnp.int32, (TOT, UTT * FR), 1)
    utt, frame = slot_place(slot, lens_ref)
    pick = one_hot(utt * FR + frame == lane)
    utt, frame = slot_place(lax.broadcasted_iota(jnp.int32, (EXTRA, TOT), 1), lens_ref)
    kind = lax.broadcasted_iota(jnp.int32, (EXTRA, TOT), 0)
    out_ref[TOT:, :TOT] = jnp.where(kind == 0, frame, utt).astype(F32).astype(BF)
    out_ref[TOT:, TOT:] = jnp.zeros((EXTRA, D - TOT), BF)
    for j in range(D // 256):
        cols = slice(j * 256, (j + 1) * 256)
        out_ref[:TOT, cols] = jnp.dot(
            pick, frames_ref[:, cols], preferred_element_type=F32
        ).astype(BF)


def pack_frames(lens, frames, after):
    return pl.pallas_call(
        pack_kernel,
        out_shape=jax.ShapeDtypeStruct((TOT + EXTRA, D), BF),
        in_specs=[SM, VM, HBM],
        out_specs=VM,
        compiler_params=params(4),
        cost_estimate=cost(50_000_000, 600_000),
        name="pack_frames",
    )(lens, frames, after)


def query_kernel(hidden_ref, gain_ref, w_ref, after_hbm, out_ref, normed):
    @pl.loop(0, hidden_ref.shape[0] // 32)
    def _(i):
        for r in range(0, 32, 16):
            rows = pl.ds(pl.multiple_of(i * 32 + r, 16), 16)
            normed[rows, :] = norm_rows(hidden_ref[rows, :].astype(F32), gain_ref[...]).astype(BF)

    for j in range(D // 256):
        cols = slice(j * 256, (j + 1) * 256)
        q = jnp.dot(normed[...], w_ref[:, cols], preferred_element_type=F32)
        out_ref[:, cols] = (q * (HEAD**-0.5)).astype(BF)


def project_query(hidden, gain, w, after):
    rows = hidden.shape[0]
    return pl.pallas_call(
        query_kernel,
        out_shape=jax.ShapeDtypeStruct((rows, D), BF),
        in_specs=[VM, VM, VM, HBM],
        out_specs=VM,
        scratch_shapes=[pltpu.VMEM((rows, D), BF)],
        compiler_params=params(8),
        cost_estimate=cost(2 * rows * D * D, 4 << 20),
        name="project_query",
    )(hidden, gain, w, after)


def order_columns(dst, src, where_ref):
    odd = jnp.broadcast_to(where_ref[0] % 2 == 1, (src.shape[0], 128))
    for i in range(D // 128):
        at = pl.multiple_of(where_ref[i] // 2 * 128, 128)
        block = src[:, pl.ds(at, 128)].astype(F32)
        block = jnp.where(odd, pltpu.roll(block, HEAD, 1), block)
        dst[:, i * 128 : (i + 1) * 128] = block.astype(BF)


def shard_rows(w_refs, k, cols):
    own, other = w_refs
    picks = [own[2 * k], other[2 * k], own[2 * k + 1], other[2 * k + 1]]
    return jnp.concatenate([ref[row : row + 64, cols] for ref, row in picks], axis=0)


def dot_shards(lhs, w_refs, cols):
    total = None
    for k in range(D // 256):
        term = jnp.dot(
            lhs[:, k * 256 : (k + 1) * 256],
            shard_rows(w_refs, k, cols),
            preferred_element_type=F32,
        )
        total = term if total is None else total + term
    return total


def encode_kernel(n_w, where_ref, *refs):
    x_refs = refs[:2]
    gain_in_ref, dw_ref, gain_mid_ref = refs[2:5]
    blocks = []
    for ref in refs[5 : 5 + n_w]:
        blocks += [(ref, row) for row in range(0, ref.shape[0], 64)]
    w_refs = blocks[: len(blocks) // 2], blocks[len(blocks) // 2 :]
    out_ref, plain, normed, spread, conv, taps, act = refs[5 + n_w :]
    step = 16
    for i, x in enumerate(x_refs):
        for r in range(0, TOT, step):
            plain[i * TOT + r : i * TOT + r + step, :] = norm_rows(
                x[r : r + step, :].astype(F32), gain_in_ref[...]
            ).astype(BF)
    order_columns(normed, plain, where_ref)
    taps[...] = dw_ref[...].astype(F32)
    rows = normed.shape[0]
    frame_rows = conv.shape[0]
    lanes = 2 * UTT
    target = []
    for i, x in enumerate(x_refs):
        places = x[TOT : TOT + EXTRA, :TOT].astype(F32)
        target.append(places[0:1] * lanes + places[1:2] + i * UTT)
    target = jnp.concatenate(target, axis=1)
    spot = lax.broadcasted_iota(jnp.int32, (frame_rows, rows), 0)
    expand = one_hot(target.astype(jnp.int32) == spot)
    column = jnp.broadcast_to(target, (8, rows)).T[:, 0:1].astype(jnp.int32)
    shrink = one_hot(column == lax.broadcasted_iota(jnp.int32, (rows, frame_rows), 1))
    for j in range(D // 256):
        value = dot_shards(normed, w_refs, slice(j * 256, (j + 1) * 256))
        gate = dot_shards(normed, w_refs, slice(D + j * 256, D + (j + 1) * 256))
        gated = (value * jax.nn.sigmoid(gate)).astype(BF)
        spread[:, j * 256 : (j + 1) * 256] = jnp.dot(expand, gated, preferred_element_type=F32)
    block = 8

    @pl.loop(0, D // 128)
    def _(c):
        cols = pl.ds(pl.multiple_of(c * 128, 128), 128)
        weights = [jnp.broadcast_to(taps[k : k + 1, cols], (lanes, 128)) for k in range(TAPS)]
        for first in range(0, FR, block):
            sums = [None] * block
            for f in range(max(0, first - HALF), min(FR, first + block + HALF)):
                here = spread[f * lanes : (f + 1) * lanes, cols]
                for b in range(block):
                    k = f - (first + b) + HALF
                    if 0 <= k < TAPS:
                        term = here * weights[k]
                        sums[b] = term if sums[b] is None else sums[b] + term
            for b in range(block):
                at = (first + b) * lanes
                conv[at : at + lanes, cols] = sums[b]

    for r in range(0, frame_rows, step):
        v = norm_rows(conv[r : r + step, :], gain_mid_ref[...])
        act[r : r + step, :] = (v * jax.nn.sigmoid(v)).astype(BF)
    for j in range(D // 256):
        cols = slice(j * 256, (j + 1) * 256)
        plain[:, cols] = jnp.dot(shrink, act[:, cols], preferred_element_type=F32).astype(BF)
    order_columns(normed, plain, where_ref)
    for j in range(D // 256):
        cols = slice(j * 256, (j + 1) * 256)
        low = dot_shards(normed, w_refs, slice(2 * D + j * 256, 2 * D + (j + 1) * 256))
        for i, x in enumerate(x_refs):
            at = slice(i * TOT, (i + 1) * TOT)
            out_ref[at, cols] = (x[:TOT, cols].astype(F32) + low[at]).astype(BF)
    utts = [x[TOT : TOT + EXTRA, :TOT].astype(F32)[1:2] for x in x_refs]
    kind = lax.broadcasted_iota(jnp.int32, (EXTRA, TOT), 0)
    out_ref[rows:, :TOT] = jnp.where(kind == 0, utts[0], utts[1]).astype(BF)
    out_ref[rows:, TOT:] = jnp.zeros((EXTRA, D - TOT), BF)


def encode(where, xs, gain_in, dw, gain_mid, shards):
    rows = 2 * TOT
    frame_rows = 2 * UTT * FR
    return pl.pallas_call(
        functools.partial(encode_kernel, len(shards)),
        out_shape=jax.ShapeDtypeStruct((rows + EXTRA, D), BF),
        in_specs=[SM] + [VM] * (5 + len(shards)),
        out_specs=VM,
        scratch_shapes=[
            pltpu.VMEM((rows, D), BF),
            pltpu.VMEM((rows, D), BF),
            pltpu.VMEM((frame_rows, D), F32),
            pltpu.VMEM((frame_rows, D), F32),
            pltpu.VMEM((TAPS, D), F32),
            pltpu.VMEM((frame_rows, D), BF),
        ],
        compiler_params=params(9),
        cost_estimate=cost(8_000_000_000, 8 << 20),
        name="encode",
    )(where, *xs, gain_in, dw, gain_mid, *shards)


def decode_kernel(n_mem, aliased, micro_ref, tgt_ref, *refs):
    mem_refs = refs[:n_mem]
    q_ref, hidden_ref, wk, wv, wo = refs[n_mem : n_mem + 5]
    rest = refs[n_mem + 5 + (1 if aliased else 0) :]
    out_hbm, keys, values, ctx, res, seg, out_sems = rest
    slots = UTT * TGT
    micros = 2 * n_mem
    for w, out in ((wk, keys), (wv, values)):
        for p, mem in enumerate(mem_refs):
            for j in range(D // 256):
                cols = slice(j * 256, (j + 1) * 256)
                out[p * 2 * TOT : (p + 1) * 2 * TOT, cols] = jnp.dot(
                    mem[: 2 * TOT, :], w[:, cols], preferred_element_type=F32
                ).astype(BF)
    width = GROUP * HEAD
    tall = GROUP * slots
    row = lax.broadcasted_iota(jnp.int32, (tall, width), 0)
    lane = lax.broadcasted_iota(jnp.int32, (tall, width), 1)
    own = (row // slots) == (lane // HEAD)
    own_bf = one_hot(own)
    utt_of_row = (lax.broadcasted_iota(jnp.int32, (tall, TOT), 0) // TGT) % UTT
    groups = HEADS // GROUP
    for i in range(micros):
        utts = mem_refs[i // 2][2 * TOT : 2 * TOT + EXTRA, :TOT].astype(F32)
        seg[i * 8 : i * 8 + 8, :] = jnp.broadcast_to(utts[i % 2 : i % 2 + 1], (8, TOT))

    def attend(i):
        line = seg[pl.ds(pl.multiple_of(i * 8, 8), 8), :]
        allowed = utt_of_row == line[0:1].astype(jnp.int32)
        at = pl.ds(pl.multiple_of(i * TOT, TOT), TOT)
        mine = pl.ds(pl.multiple_of(i * slots, slots), slots)
        from_rows = pl.ds(pl.multiple_of(micro_ref[i] * slots, slots), slots)
        cuts = [slice(j * width, (j + 1) * width) for j in range(groups)]
        scores = []
        for cols in cuts:
            q = q_ref[from_rows, cols]
            q = jnp.concatenate([q] * GROUP, axis=0) * own_bf
            scores.append(
                lax.dot_general(
                    q, keys[at, cols], (((1,), (1,)), ((), ())), preferred_element_type=F32
                )
            )
        probs = []
        for s in scores:
            s = jnp.where(allowed, s, -1e30)
            expo = jnp.exp(s - jnp.max(s, -1, keepdims=True))
            probs.append((expo * (1.0 / jnp.sum(expo, -1, keepdims=True))).astype(BF))
        for prob, cols in zip(probs, cuts):
            mixed = jnp.dot(prob, values[at, cols], preferred_element_type=F32)
            mixed = jnp.where(own, mixed, 0.0)
            total = mixed[:slots]
            for g in range(1, GROUP):
                total = total + mixed[g * slots : (g + 1) * slots]
            ctx[mine, cols] = total.astype(BF)

    @pl.loop(0, micros // 2)
    def _(p):
        attend(2 * p)
        attend(2 * p + 1)

    pos = lax.broadcasted_iota(jnp.int32, (slots, 256), 0)

    @pl.loop(0, D // 512)
    def _(h):
      for half in range(2):
        cols = pl.ds(pl.multiple_of(h * 512 + half * 256, 256), 256)
        proj = jnp.dot(ctx[...], wo[:, cols], preferred_element_type=F32)
        for i in range(micros):
            mine = slice(i * slots, (i + 1) * slots)
            from_rows = pl.ds(pl.multiple_of(micro_ref[i] * slots, slots), slots)
            base = micro_ref[i] * UTT
            limit = jnp.full((slots, 256), tgt_ref[base], jnp.int32)
            for u in range(1, UTT):
                limit = jnp.where(pos // TGT == u, tgt_ref[base + u], limit)
            both = hidden_ref[from_rows, cols].astype(F32) + proj[mine]
            res[mine, cols] = jnp.where(pos % TGT < limit, both, 0.0).astype(BF)

    outs = []
    for i in range(micros):
        at = pl.ds(pl.multiple_of(micro_ref[i] * slots, slots), slots)
        here = pl.ds(i * slots, slots)
        copy = pltpu.make_async_copy(res.at[here, :], out_hbm.at[at, :], out_sems.at[i])
        copy.start()
        outs.append(copy)
    for copy in outs:
        copy.wait()


def decode(micro, tgt, mems, q, hidden, wk, wv, wo, prev):
    rows = hidden.shape[0]
    micros = 2 * len(mems)
    total = micros * TOT
    slots = UTT * TGT
    aliased = prev is not None
    args = [micro, tgt, *mems, q, hidden, wk, wv, wo] + ([prev] if aliased else [])
    return pl.pallas_call(
        functools.partial(decode_kernel, len(mems), aliased),
        out_shape=jax.ShapeDtypeStruct((rows, D), BF),
        in_specs=[SM, SM] + [VM] * (len(mems) + 5) + [HBM] * aliased,
        out_specs=HBM,
        scratch_shapes=[
            pltpu.VMEM((total, D), BF),
            pltpu.VMEM((total, D), BF),
            pltpu.VMEM((micros * slots, D), BF),
            pltpu.VMEM((micros * slots, D), BF),
            pltpu.VMEM((micros * 8, TOT), F32),
            pltpu.SemaphoreType.DMA((micros,)),
        ],
        input_output_aliases={len(args) - 1: 0} if aliased else {},
        compiler_params=params(7),
        cost_estimate=cost(16 * total * D * D, 8 << 20),
        name="decode",
    )(*args)


def dp_perm(move):
    pairs = []
    for z in range(2):
        for x in range(4):
            for c in range(2):
                nz, nx, nc = move(z, x, c)
                pairs.append(((z * 4 + x) * 2 + c, (nz * 4 + nx % 4) * 2 + nc))
    return pairs


def section_perm(dy, dz):
    return [(y * 4 + z, (y + dy) % 4 * 4 + (z + dz) % 4) for y in range(4) for z in range(4)]


TO_PAIR = dp_perm(lambda z, x, c: (1 - z, x, c))
TO_RIGHT = dp_perm(lambda z, x, c: (z, x + 1, c))
TO_LEFT = dp_perm(lambda z, x, c: (z, x + 3, c))
TO_CORE = dp_perm(lambda z, x, c: (z, x, 1 - c))


def pass_kernel(value_ref, *refs):
    refs[-1][...] = value_ref[...]


def pass_after(value, *others):
    return pl.pallas_call(
        pass_kernel,
        out_shape=jax.ShapeDtypeStruct(value.shape, value.dtype),
        in_specs=[VM] + [HBM] * len(others),
        out_specs=VM,
        compiler_params=params(2),
        cost_estimate=cost(0, 600_000),
        name="pass_after",
    )(value, *others)


def shard_table():
    places = [(0, 0), (1, 0), (0, 3), (0, 1), (1, 3), (1, 1), (0, 2), (1, 2)]
    table = []
    for index in range(16):
        z, x, c = index // 8, index // 2 % 4, index % 2
        table.append(
            [
                ((z + a) % 2 * 4 + (x + b) % 4) * 2 + (c + s) % 2
                for s in (0, 1)
                for a, b in places
            ]
        )
    return table


REL = (0, -1, 1, 2)


def micro_table():
    return [
        [(y + dy) % 4 * 4 + (z + dz) % 4 for dy in REL for dz in REL]
        for y in range(4)
        for z in range(4)
    ]


def body(
    frames,
    frame_lens,
    tgt_lens,
    enc_gain_in,
    w_in,
    depthwise,
    enc_gain_mid,
    w_out,
    dec_gain,
    w_query,
    w_key,
    w_value,
    w_output,
    hidden,
):
    across = lambda v, perm: lax.ppermute(v, "dp", perm)
    along = lambda v, dy, dz: lax.ppermute(v, "section", section_perm(dy, dz))
    where = jnp.array(shard_table(), jnp.int32)[lax.axis_index("dp")]
    micros = jnp.array(micro_table(), jnp.int32)[lax.axis_index("section")].reshape(4, 4)

    own = join_shards(w_in, w_out)
    pair = across(own, TO_PAIR)
    own_l, own_r = across(own, TO_RIGHT), across(own, TO_LEFT)
    pair_l, pair_r = across(pair, TO_RIGHT), across(pair, TO_LEFT)
    own_2, pair_2 = across(own_l, TO_RIGHT), across(pair_r, TO_LEFT)
    shards = [own, pair, own_l, own_r, pair_l, pair_r, own_2, pair_2]

    packed = pack_frames(frame_lens.reshape(UTT), frames.reshape(UTT * FR, D), pair)
    from_b, from_a = along(packed, 0, 1), along(packed, 0, -1)
    source = hidden.reshape(-1, D)
    turn = list(shards)
    turn[1] = pass_after(turn[1], from_b)
    from_2 = along(from_b, 0, 1)
    shards += [across(v, TO_CORE) for v in turn]

    def encode_pair(first, second):
        return encode(
            where,
            [first, second],
            enc_gain_in.reshape(1, D),
            depthwise,
            enc_gain_mid.reshape(1, D),
            shards,
        )

    mem_a = encode_pair(packed, from_b)
    query = project_query(source, dec_gain, w_query[0], mem_a)
    mem_b = encode_pair(from_a, from_2)

    a_from_l, a_from_r = along(mem_a, 1, 0), along(mem_a, -1, 0)
    b_from_l, b_from_r = along(mem_b, 1, 0), along(mem_b, -1, 0)

    tgt = tgt_lens.reshape(-1)

    def attend(parts, mems, prev):
        micro = jnp.concatenate([micros[y, z : z + 2] for y, z in parts])
        return decode(micro, tgt, mems, query, source, w_key[0], w_value[0], w_output[0], prev)

    a_far, b_far = along(a_from_l, 1, 0), along(b_from_r, -1, 0)
    out = attend([(0, 0), (0, 2)], [mem_a, mem_b], None)
    out = attend([(1, 0), (2, 0)], [a_from_l, a_from_r], out)
    out = attend([(1, 2), (2, 2)], [b_from_l, b_from_r], out)
    out = attend([(3, 0), (3, 2)], [a_far, b_far], out)
    return out.reshape(hidden.shape)


def solution(mesh):
    return jax.shard_map(
        body,
        mesh=mesh,
        in_specs=(
            P("section", "dp", None, None),
            P("section", "dp", None),
            P(None, "dp"),
            P(),
            P("dp", None),
            P(),
            P(),
            P("dp", None),
            P("section", None),
            P("section", None, None),
            P("section", None, None),
            P("section", None, None),
            P("section", None, None),
            P("section", None, "dp", None, None),
        ),
        out_specs=P("section", None, "dp", None, None),
        check_vma=False,
    )
```
